32 devices in a mesh: ctx: 8 (over z, x), fsdp: 4 (over y, core).
Axes of the slice: x: 2, y: 2, z: 4, core: 2. Of those that a mesh axis runs over, the one named last changes fastest.
Arguments:
- tokens: bfloat16 [4, 1024, 1536], P('fsdp', 'ctx'), may hold values from -6 to 6
- segments: int32 [4, 1024], P('fsdp'), may hold values from 0 to 3, never falling along the last dimension, each value on 1 to 512 neighbouring positions
- gain_attn: bfloat16 [1536], replicated, may hold values from 0.5 to 1.5
- w_query: bfloat16 [1536, 1536], P('fsdp'), may hold values from -0.15625 to 0.15625
- w_key: bfloat16 [1536, 1536], P('fsdp'), may hold values from -0.15625 to 0.15625
- w_value: bfloat16 [1536, 1536], P('fsdp'), may hold values from -0.15625 to 0.15625
- w_forget: bfloat16 [1536, 24], P('fsdp'), may hold values from -0.15625 to 0.15625
- forget_bias: float32 [24], replicated, may hold values from 2 to 8
- w_outgate: bfloat16 [1536, 1536], P('fsdp'), may hold values from -0.15625 to 0.15625
- w_out: bfloat16 [1536, 1536], P('fsdp'), may hold values from -0.625 to 0.625
- gain_ffn: bfloat16 [1536], replicated, may hold values from 0.5 to 1.5
- w_gate: bfloat16 [1536, 4096], P('fsdp'), may hold values from -0.15625 to 0.15625
- w_up: bfloat16 [1536, 4096], P('fsdp'), may hold values from -0.15625 to 0.15625
- w_down: bfloat16 [4096, 1536], P('fsdp'), may hold values from -0.09375 to 0.09375
- cotangent: bfloat16 [4, 1024, 1536], P('fsdp', 'ctx'), may hold values from -6 to 6
Outputs:
- output: bfloat16 [4, 1024, 1536], P('fsdp', 'ctx')
- grad_tokens: float32 [4, 1024, 1536], P('fsdp', 'ctx')
- grad_gain_attn: float32 [1536], replicated
- grad_query: float32 [1536, 1536], P('fsdp')
- grad_key: float32 [1536, 1536], P('fsdp')
- grad_value: float32 [1536, 1536], P('fsdp')
- grad_forget: float32 [1536, 24], P('fsdp')
- grad_bias: float32 [24], replicated
- grad_outgate: float32 [1536, 1536], P('fsdp')
- grad_out: float32 [1536, 1536], P('fsdp')
- grad_gain_ffn: float32 [1536], replicated
- grad_gate: float32 [1536, 4096], P('fsdp')
- grad_up: float32 [1536, 4096], P('fsdp')
- grad_down: float32 [4096, 1536], P('fsdp')
The draws below stay inside these ranges and needn't reach their ends.
Inputs may be any that keep to these rules, and one draw needn't show every extreme that they name: `segments`: along each sequence the document numbers never fall; every document has 1 to 512 tokens and one has exactly 512.
All inputs are finite; a program needn't handle non-finite values.
Results may differ from the reference program's by a relative error of at most 0.014.
Values may be sent and summed in bfloat16 or wider, within the bound.
A program may use at most 448 MiB of HBM per device.

```python
import math
import jax
import jax.numpy as jnp
import numpy as np
from jax import lax

D = 1536
H = 24
FF = 4096
LENGTH = 1024
SEQS = 4
DOC_MAX = 512
DOCS = 4


def levels(rng, extent, split, smallest, largest):
    level, own = 1.0, jax.random.fold_in(rng, 6)
    for position, shards_of in split:
        heights = jnp.exp(jax.random.uniform(jax.random.fold_in(own, position), (shards_of,), jnp.float32, smallest / len(split), largest / len(split)))
        level = level * jnp.repeat(heights, extent[position] // shards_of).reshape([-1 if axis == position else 1 for axis in range(len(extent))])
    return level


def split_up(number_of, total, reach, lean):
    portions = [(1 << 20) // math.isqrt(grade ** lean) + 1 for grade in range(2, number_of + 1)]
    rest, holding = total - reach - (number_of - 1), [1] * (number_of - 1)
    while rest > 0:
        movable = [i for i in range(number_of - 1) if holding[i] < reach]
        pool, left = sum([portions[i] for i in movable]), rest
        for i in movable:
            addition = min(reach - holding[i], max(1, left * portions[i] // pool), rest)
            holding[i] = holding[i] + addition
            rest = rest - addition
    return np.array([reach] + holding)


def ragged(stream_key, amount, total, bound, skew):
    if amount == 2:
        one = jax.random.randint(stream_key, (), max(1, total - bound), min(bound, total - 1) + 1)
        return jnp.stack([one, total - one])
    tallies = jnp.asarray(split_up(amount, total, bound, skew), jnp.int32)
    couples = (amount - 1) // 2
    donor, taker = tallies[1:1 + 2 * couples:2], tallies[2:2 + 2 * couples:2]
    room = jnp.minimum(donor - 1, bound - taker)
    passed = jax.random.randint(jax.random.fold_in(stream_key, 1), (couples,), 0, 1 << 20) % (room + 1)
    tallies = tallies.at[1:1 + 2 * couples:2].set(donor - passed).at[2:2 + 2 * couples:2].set(taker + passed)
    return tallies[jax.random.permutation(jax.random.fold_in(stream_key, 2), amount)]


def scatter_about(key, shape, width, limit, split=(), kind=jnp.bfloat16):
    entries = jax.random.normal(key, shape, jnp.float32) * width
    if len(split) > 0:
        entries = levels(key, shape, split, -0.22, 0.18) * entries
    return jnp.clip(entries, min=-limit, max=limit).astype(kind)


def setup_inputs(seed: int = 0) -> dict:
    streams_of = jax.random.split(jax.random.key(seed), 16)
    return {
        "tokens": scatter_about(streams_of[0], (SEQS, LENGTH, D), 1.0, 6.0, ((0, 4), (1, 8))),
        "segments": jax.vmap(lambda own: jnp.searchsorted(jnp.cumsum(ragged(own, DOCS, LENGTH, DOC_MAX, 2)), jnp.arange(LENGTH), side="right"))(jax.random.split(streams_of[1], SEQS)).reshape((SEQS, LENGTH)).astype(jnp.int32),
        "gain_attn": jnp.clip(1.0 + 0.1 * jax.random.normal(streams_of[2], (D,), jnp.float32), 0.5, 1.5).astype(jnp.bfloat16),
        "w_query": scatter_about(streams_of[3], (D, D), D ** -0.5, 0.15625, ((0, 4),)),
        "w_key": scatter_about(streams_of[4], (D, D), D ** -0.5, 0.15625, ((0, 4),)),
        "w_value": scatter_about(streams_of[5], (D, D), D ** -0.5, 0.15625, ((0, 4),)),
        "w_forget": scatter_about(streams_of[6], (D, H), D ** -0.5, 0.15625, ((0, 4),)),
        "forget_bias": jnp.clip(jax.random.uniform(streams_of[7], (H,), jnp.float32, 2.0, 8.0), 2.0, 8.0),
        "w_outgate": scatter_about(streams_of[8], (D, D), D ** -0.5, 0.15625, ((0, 4),)),
        "w_out": scatter_about(streams_of[9], (D, D), (D // 16) ** -0.5, 0.625, ((0, 4),)),
        "gain_ffn": jnp.clip(1.0 + 0.1 * jax.random.normal(streams_of[10], (D,), jnp.float32), 0.5, 1.5).astype(jnp.bfloat16),
        "w_gate": scatter_about(streams_of[11], (D, FF), D ** -0.5, 0.15625, ((0, 4),)),
        "w_up": scatter_about(streams_of[12], (D, FF), D ** -0.5, 0.15625, ((0, 4),)),
        "w_down": scatter_about(streams_of[13], (FF, D), FF ** -0.5, 0.09375, ((0, 4),)),
        "cotangent": scatter_about(streams_of[14], (SEQS, LENGTH, D), 1.0, 6.0, ((0, 4), (1, 8))),
    }


@jax.custom_vjp
def low(v):
    return lax.optimization_barrier(v.astype(jnp.bfloat16)).astype(jnp.float32)

@jax.custom_vjp
def low_back(v):
    return v

def low_keep(v):
    return (low(v), None)

def low_pass(kept, grad):
    return (grad,)

def back_keep(v):
    return (v, None)

def back_low(kept, grad):
    return (low(grad),)
low.defvjp(low_keep, low_pass)
low_back.defvjp(back_keep, back_low)
EPSILON = 1e-06
NEGATIVE = -1e+30

def product(left, right):
    return jnp.dot(left, right, precision=lax.Precision.HIGHEST, preferred_element_type=jnp.float32)

def normalize(values, gain):
    return values * lax.rsqrt(lax.optimization_barrier(jnp.mean(values * values, axis=-1, keepdims=True)) + EPSILON) * gain

def attention(queries, keys_all, values, decay, seg_ids, n_heads):
    length = queries.shape[0]
    head_dim = queries.shape[1] // n_heads
    query_heads = queries.reshape(length, n_heads, head_dim)
    key_heads = keys_all.reshape(length, n_heads, head_dim)
    value_heads = values.reshape(length, n_heads, head_dim)
    block_rows = 512 if length % 512 == 0 else length
    positions = jnp.arange(length, dtype=jnp.int32)

    def one_block(block_index):
        first_row = block_index * block_rows
        query_block = lax.dynamic_slice_in_dim(query_heads, first_row, block_rows, 0)
        decay_block = lax.dynamic_slice_in_dim(decay, first_row, block_rows, 0)
        seg_block = lax.dynamic_slice_in_dim(seg_ids, first_row, block_rows, 0)
        pos_block = first_row + jnp.arange(block_rows, dtype=jnp.int32)
        scores = jnp.einsum('bhd,nhd->hbn', query_block, key_heads, precision=lax.Precision.HIGHEST) * head_dim ** (-0.5)
        scores = scores + decay_block.T[:, :, None] - decay.T[:, None, :]
        scores = low_back(scores)
        allowed = (positions[None, :] <= pos_block[:, None]) & (seg_ids[None, :] == seg_block[:, None])
        scores = jnp.where(allowed[None], scores, NEGATIVE)
        weights = jax.nn.softmax(scores, axis=-1)
        return jnp.einsum('hbn,nhd->bhd', low(weights), value_heads, precision=lax.Precision.HIGHEST)
    blocks = lax.map(jax.checkpoint(one_block), jnp.arange(length // block_rows, dtype=jnp.int32))
    return blocks.reshape(length, n_heads * head_dim)

def layer(tokens, params, seg_ids):
    gain_attn, w_query, w_key, w_value, w_forget, forget_bias, w_outgate, w_out, gain_ffn, w_gate, w_up, w_down = params
    n_heads = forget_bias.shape[0]
    normed = low(normalize(tokens, gain_attn))
    queries = low_back(low(product(normed, w_query)))
    keys_all = low_back(low(product(normed, w_key)))
    values = low_back(low(product(normed, w_value)))
    logits = low_back(product(normed, w_forget) + forget_bias)
    decay = jnp.cumsum(jax.nn.log_sigmoid(logits), axis=0)
    attended = low_back(attention(queries, keys_all, values, decay, seg_ids, n_heads))
    gate_logits = low_back(product(normed, w_outgate))
    gated_out = low(attended * jax.nn.sigmoid(gate_logits))
    middle = tokens + low_back(product(gated_out, w_out))
    normed_two = low(normalize(middle, gain_ffn))
    gate_part = low_back(product(normed_two, w_gate))
    up_part = low_back(product(normed_two, w_up))
    hidden = low(jax.nn.silu(gate_part) * up_part)
    return middle + low_back(product(hidden, w_down))

def reference(tokens, segments, gain_attn, w_query, w_key, w_value, w_forget, forget_bias, w_outgate, w_out, gain_ffn, w_gate, w_up, w_down, cotangent):
    params = (gain_attn.astype(jnp.float32), w_query.astype(jnp.float32), w_key.astype(jnp.float32), w_value.astype(jnp.float32), w_forget.astype(jnp.float32), forget_bias.astype(jnp.float32), w_outgate.astype(jnp.float32), w_out.astype(jnp.float32), gain_ffn.astype(jnp.float32), w_gate.astype(jnp.float32), w_up.astype(jnp.float32), w_down.astype(jnp.float32))

    def one_sequence(totals, inputs):
        seq_tokens, seq_ids, seq_cot = inputs

        def forward(tok_in, weights):
            return layer(tok_in, weights, seq_ids)
        result, pullback = jax.vjp(forward, seq_tokens, params)
        grad_in, grad_params = pullback(seq_cot)
        totals = jax.tree.map(jnp.add, totals, grad_params)
        return (totals, (result.astype(jnp.bfloat16), grad_in))
    zero_sums = jax.tree.map(jnp.zeros_like, params)
    totals, (outputs, grad_tokens) = lax.scan(one_sequence, zero_sums, (tokens.astype(jnp.float32), segments, cotangent.astype(jnp.float32)))
    return (outputs, grad_tokens, totals[0], totals[1], totals[2], totals[3], totals[4], totals[5], totals[6], totals[7], totals[8], totals[9], totals[10], totals[11])
```

```python
import jax
import jax.numpy as jnp
from jax import lax
from jax.experimental import pallas as pl
from jax.experimental.pallas import tpu as pltpu
from jax.sharding import PartitionSpec as P

EPSILON = 1e-06
NEGATIVE = -1e30
BF16, F32 = jnp.bfloat16, jnp.float32


def matmul(left, right):
    return jnp.dot(left, right, preferred_element_type=F32)


def matmul_rows(left, right):
    return lax.dot_general(left, right, (((1,), (1,)), ((), ())), preferred_element_type=F32)


def weight_grad(left, right):
    return lax.dot_general(left, right, (((0,), (0,)), ((), ())), preferred_element_type=F32)


def rms_stats(values):
    rstat = lax.rsqrt(jnp.mean(values * values, axis=-1, keepdims=True) + EPSILON)
    return (values * rstat, rstat)


def norm_back(grad_in, normed, rstat, gain):
    grad_normed = grad_in * gain
    grad_gain = jnp.sum(grad_in * normed, axis=0)
    grad_values = rstat * (
        grad_normed - normed * jnp.mean(grad_normed * normed, axis=-1, keepdims=True)
    )
    return (grad_values, grad_gain)


MESH = pl.DeviceIdType.MESH
RING_PIECES = 4


def ring_place(ctx, count):
    odd = ctx % 2
    return ctx // 2 + odd * (count - 1 - 2 * (ctx // 2))


def ring_index(place, count):
    back = place // (count // 2)
    return 2 * place + back * (2 * (count - 1 - place) + 1 - 2 * place)


class Ring:
    def __init__(self, count):
        self.count, self.half = count, count // 2
        self.ctx, self.fsdp = lax.axis_index("ctx"), lax.axis_index("fsdp")
        self.place = ring_place(self.ctx, count)

    def at(self, offset):
        return ring_index((self.place + offset + self.count) % self.count, self.count)

    def device(self, offset):
        return (self.at(offset), self.fsdp)


def greet(devices):
    barrier = pltpu.get_barrier_semaphore()
    for device in devices:
        pl.semaphore_signal(barrier, inc=1, device_id=device, device_id_type=MESH)
    pl.semaphore_wait(barrier, len(devices))


def remote(src, dst, send, recv, device):
    return pltpu.make_async_remote_copy(
        src_ref=src, dst_ref=dst, send_sem=send, recv_sem=recv, device_id=device, device_id_type=MESH
    )


def carried(step, half, pieces, way):
    if step < half - 1:
        return range(pieces)
    return range(pieces // 2) if way == 0 else range(pieces // 2, pieces)


def ring_gather(ring, own, full, local_sem, send_sem, recv_sem, pieces=RING_PIECES):
    rows = own.shape[0] // pieces

    def part(k):
        return pl.ds(k * rows, rows)

    keep = pltpu.make_async_copy(own, full.at[ring.ctx], local_sem)
    keep.start()
    copies = {}
    for step in range(ring.half):
        for k in range(pieces):
            for way, sign in ((0, 1), (1, -1)):
                if k not in carried(step, ring.half, pieces, way):
                    continue
                if step > 0:
                    copies[step - 1, k, way].wait_recv()
                block = ring.at(-sign * step)
                src = own.at[part(k)] if step == 0 else full.at[block, part(k)]
                copy = remote(
                    src,
                    full.at[block, part(k)],
                    send_sem.at[step, k, way],
                    recv_sem.at[step, k, way],
                    ring.device(sign),
                )
                copy.start()
                copies[step, k, way] = copy
        yield
    for (step, k, way), copy in copies.items():
        if step == ring.half - 1 or k not in carried(step + 1, ring.half, pieces, way):
            copy.wait_recv()
    for copy in copies.values():
        copy.wait_send()
    keep.wait()


def ring_sum(ring, parts, held, total, send_sem, recv_sem, pieces=RING_PIECES):
    rows = parts.shape[1] // pieces

    def part(k):
        return pl.ds(k * rows, rows)

    copies = {}
    for step in range(ring.half):
        for k in range(pieces):
            for way, sign in ((0, 1), (1, -1)):
                if k not in carried(ring.half - 1 - step, ring.half, pieces, way):
                    continue
                block = ring.at(sign * (ring.half - step))
                src = parts.at[block, part(k)]
                if (step - 1, k, way) in copies:
                    copies[step - 1, k, way].wait_recv()
                    slot = held.at[way, step - 1, part(k)]
                    slot[...] = (slot[...].astype(F32) + src[...].astype(F32)).astype(BF16)
                    src = slot
                copy = remote(
                    src,
                    held.at[way, step, part(k)],
                    send_sem.at[step, k, way],
                    recv_sem.at[step, k, way],
                    ring.device(sign),
                )
                copy.start()
                copies[step, k, way] = copy
    last = ring.half - 1
    for k in range(pieces):
        for way in range(2):
            copies[last, k, way].wait_recv()
        total[part(k)] = (
            parts[ring.ctx, part(k)].astype(F32)
            + held[0, last, part(k)].astype(F32)
            + held[1, last, part(k)].astype(F32)
        )
    for copy in copies.values():
        copy.wait_send()


def ring_sems(count, pieces=RING_PIECES):
    shape = (count // 2, pieces, 2)
    return [pltpu.SemaphoreType.DMA(shape), pltpu.SemaphoreType.DMA(shape)]


def gather_rows(value, ident):
    count = lax.axis_size("ctx")

    def kernel(own, full, local_sem, send_sem, recv_sem):
        ring = Ring(count)
        greet([ring.device(1), ring.device(-1)])
        for _ in ring_gather(ring, own, full, local_sem, send_sem, recv_sem):
            pass

    full = pl.pallas_call(
        kernel,
        out_shape=jax.ShapeDtypeStruct((count,) + value.shape, value.dtype),
        in_specs=[pl.BlockSpec(memory_space=pl.ANY)],
        out_specs=pl.BlockSpec(memory_space=pl.ANY),
        scratch_shapes=[pltpu.SemaphoreType.DMA] + ring_sems(count),
        compiler_params=pltpu.CompilerParams(collective_id=ident, has_side_effects=True),
        cost_estimate=pl.CostEstimate(flops=0, bytes_accessed=100_000_000, transcendentals=0),
        name="gather_rows",
    )(value)
    return full.reshape(-1, value.shape[1])


def sum_rows(partial, ident):
    count = lax.axis_size("ctx")
    rows, width = partial.shape[0] // count, partial.shape[1]

    def kernel(parts, total, held, send_sem, recv_sem):
        ring = Ring(count)
        greet([ring.device(1), ring.device(-1)])
        ring_sum(ring, parts, held, total, send_sem, recv_sem)

    return pl.pallas_call(
        kernel,
        out_shape=jax.ShapeDtypeStruct((rows, width), F32),
        in_specs=[pl.BlockSpec(memory_space=pltpu.VMEM)],
        out_specs=pl.BlockSpec(memory_space=pltpu.VMEM),
        scratch_shapes=[pltpu.VMEM((2, count // 2, rows, width), BF16)] + ring_sems(count),
        compiler_params=pltpu.CompilerParams(
            collective_id=ident, has_side_effects=True, vmem_limit_bytes=32 * 2**20
        ),
        cost_estimate=pl.CostEstimate(flops=0, bytes_accessed=100_000_000, transcendentals=0),
        name="sum_rows",
    )(partial.astype(BF16).reshape(count, rows, width))


def gather_start(value, weight):
    count, shards = lax.axis_size("ctx"), lax.axis_size("fsdp")

    def kernel(own, shard, full, whole, local_sem, send_sem, recv_sem, far_send, far_recv):
        ring = Ring(count)
        me = ring.fsdp
        pair = me + 1 - 2 * (me % 2)
        others = [(me + 2 * hop) % shards for hop in range(1, shards // 2)]
        greet(
            [ring.device(1), ring.device(-1), (ring.ctx, pair)]
            + [(ring.ctx, other) for other in others]
        )
        keep = pltpu.make_async_copy(shard, whole.at[me], local_sem.at[1])
        keep.start()
        copies = [
            remote(shard, whole.at[me], far_send.at[i], far_recv.at[i], (ring.ctx, to))
            for i, to in enumerate([pair] + others)
        ]
        for copy in copies:
            copy.start()
        walk = ring_gather(ring, own, full, local_sem.at[0], send_sem, recv_sem)
        next(walk)
        passed = []
        for i in range(1, len(copies)):
            copies[i].wait_recv()
            origin = (me - 2 * i + shards) % shards
            at = shards // 2 - 1 + i
            copy = remote(whole.at[origin], whole.at[origin], far_send.at[at], far_recv.at[at], (ring.ctx, pair))
            copy.start()
            passed.append(copy)
        for _ in walk:
            pass
        copies[0].wait_recv()
        for copy in passed:
            copy.wait_recv()
        for copy in copies + passed:
            copy.wait_send()
        keep.wait()

    full, whole = pl.pallas_call(
        kernel,
        out_shape=(
            jax.ShapeDtypeStruct((count,) + value.shape, value.dtype),
            jax.ShapeDtypeStruct((shards,) + weight.shape, weight.dtype),
        ),
        in_specs=[pl.BlockSpec(memory_space=pl.ANY)] * 2,
        out_specs=(pl.BlockSpec(memory_space=pl.ANY),) * 2,
        scratch_shapes=[pltpu.SemaphoreType.DMA((2,))]
        + ring_sems(count)
        + [pltpu.SemaphoreType.DMA((shards - 1,)), pltpu.SemaphoreType.DMA((shards - 1,))],
        compiler_params=pltpu.CompilerParams(collective_id=0, has_side_effects=True),
        cost_estimate=pl.CostEstimate(flops=0, bytes_accessed=100_000_000, transcendentals=0),
        name="gather_start",
    )(value, weight)
    return full.reshape(-1, value.shape[1]), whole.reshape(-1, weight.shape[1])


def rows_to_columns(value):
    return lax.all_to_all(value, "ctx", split_axis=1, concat_axis=0, tiled=True)


def columns_to_rows(value):
    return lax.all_to_all(value, "ctx", split_axis=0, concat_axis=1, tiled=True)


def sum_grad(partial):
    return lax.psum_scatter(partial.astype(BF16), "fsdp", scatter_dimension=0, tiled=True)


def attention_scores(queries, keys, decay, allowed, scaling):
    scores = jnp.einsum("ihd,jhd->hij", queries, keys, preferred_element_type=F32) * scaling
    scores = scores + decay.T[:, :, None] - decay.T[:, None, :]
    return jnp.where(allowed[None], scores, NEGATIVE)


def shards(
    tokens,
    segments,
    gain_attn,
    w_query,
    w_key,
    w_value,
    w_forget,
    forget_bias,
    w_outgate,
    w_out,
    gain_ffn,
    w_gate,
    w_up,
    w_down,
    cotangent,
):
    n_ctx, me = lax.axis_size("ctx"), lax.axis_index("ctx")
    n_fsdp = lax.axis_size("fsdp")
    tok_rows, width = tokens.shape[1:]
    seq_rows = tok_rows * n_ctx
    n_heads = forget_bias.shape[0]
    head_dim = width // n_heads
    scaling = head_dim ** (-0.5)
    own_heads = -(-n_heads // n_ctx)
    own_width = own_heads * head_dim
    padded = own_width * n_ctx
    ffn_rows = w_down.shape[0]
    ffn_piece = ffn_rows // n_ctx
    ffn_width = ffn_piece * n_fsdp
    shard_rows = w_query.shape[0]

    def widen(value, size):
        return jnp.pad(value, ((0, 0), (0, size - value.shape[1])))

    def own_columns(weight, size):
        return lax.dynamic_slice_in_dim(widen(weight, size * n_ctx), me * size, size, 1)

    def own_ffn(weight):
        pieces = weight.reshape(weight.shape[0], n_fsdp, n_ctx, ffn_piece)
        return lax.dynamic_slice_in_dim(pieces, me, 1, 2).reshape(weight.shape[0], ffn_width)

    def gather_weight(weight):
        return lax.all_gather(weight, "fsdp", axis=0, tiled=True)

    mixed_shard = jnp.concatenate(
        [own_columns(w, own_width) for w in (w_query, w_key, w_value, w_outgate)]
        + [own_columns(w_forget, own_heads)],
        axis=1,
    )
    full_out = gather_weight(w_out)
    ffn_in = gather_weight(jnp.concatenate([own_ffn(w_gate), own_ffn(w_up)], axis=1))
    ffn_out = gather_weight(lax.dynamic_slice_in_dim(w_down, me * ffn_piece, ffn_piece, 0))
    bias_own = lax.dynamic_slice_in_dim(
        jnp.pad(forget_bias, (0, own_heads * n_ctx - n_heads)), me * own_heads, own_heads, 0
    )

    seg = segments[0]
    places = jnp.arange(seq_rows, dtype=jnp.int32)
    allowed = (places[None, :] <= places[:, None]) & (seg[None, :] == seg[:, None])

    inputs = tokens[0].astype(F32)
    gain_one = gain_attn.astype(F32)
    normed_one, rstat_one = rms_stats(inputs)
    normed, mixed_in = gather_start((normed_one * gain_one).astype(BF16), mixed_shard)
    grad_out_low = lax.all_gather(cotangent[0], "ctx", axis=0, tiled=True)

    mixed = matmul(normed, mixed_in)
    split = [own_width * i for i in range(5)]
    queries, keys, values = [
        mixed[:, split[i] : split[i + 1]].astype(BF16).reshape(seq_rows, own_heads, head_dim)
        for i in range(3)
    ]
    gate_value = jax.nn.sigmoid(mixed[:, split[3] : split[4]])
    forget_logits = mixed[:, split[4] :] + bias_own
    decay = jnp.cumsum(jax.nn.log_sigmoid(forget_logits), axis=0)

    scores = attention_scores(queries, keys, decay, allowed, scaling)
    row_max = jnp.max(scores, axis=-1, keepdims=True)
    raised = jnp.exp(scores - row_max)
    row_total = jnp.sum(raised, axis=-1, keepdims=True)
    probabilities = raised / row_total
    attended = jnp.einsum(
        "hij,jhd->ihd", probabilities.astype(BF16), values, preferred_element_type=F32
    ).reshape(seq_rows, own_width)
    gated = columns_to_rows((attended * gate_value).astype(BF16))[:, :width]

    middle = inputs + matmul(gated, full_out)
    gain_two = gain_ffn.astype(F32)
    normed_two_f, rstat_two = rms_stats(middle)
    normed_two = gather_rows((normed_two_f * gain_two).astype(BF16), 1)
    gated_all = lax.all_gather(gated, "ctx", axis=0, tiled=True)

    ffn_mid = matmul(normed_two, ffn_in)
    gate_part, up_part = ffn_mid[:, :ffn_width], ffn_mid[:, ffn_width:]
    sig_gate = jax.nn.sigmoid(gate_part)
    silu_gate = gate_part * sig_gate
    hidden = (silu_gate * up_part).astype(BF16)
    output = middle + lax.psum_scatter(
        matmul(hidden, ffn_out).astype(BF16), "ctx", scatter_dimension=0, tiled=True
    ).astype(F32)

    grad_hidden = matmul_rows(grad_out_low, ffn_out)
    grad_gate_low = (
        grad_hidden * up_part * (sig_gate * (1.0 + gate_part * (1.0 - sig_gate)))
    ).astype(BF16)
    grad_up_low = (grad_hidden * silu_gate).astype(BF16)
    grad_mid_low = jnp.concatenate([grad_gate_low, grad_up_low], axis=1)
    grad_normed_two = sum_rows(matmul_rows(grad_mid_low, ffn_in), 2)
    back_two, grad_gain_two = norm_back(grad_normed_two, normed_two_f, rstat_two, gain_two)
    grad_middle = cotangent[0].astype(F32) + back_two
    grad_ffn_in = sum_grad(weight_grad(normed_two, grad_mid_low))
    grad_ffn_out = sum_grad(weight_grad(hidden, grad_out_low))

    grad_branch_low = grad_middle.astype(BF16)
    grad_gated = matmul_rows(grad_branch_low, full_out).astype(BF16)
    grad_gated = rows_to_columns(widen(grad_gated, padded)).astype(F32)
    grad_branch_own = rows_to_columns(widen(grad_branch_low, padded))
    grad_attn_low = (grad_gated * gate_value).astype(BF16)
    grad_gatelog_low = (grad_gated * attended * (gate_value * (1.0 - gate_value))).astype(BF16)

    grad_heads = grad_attn_low.reshape(seq_rows, own_heads, head_dim)
    grad_values = jnp.einsum(
        "hij,ihd->jhd", probabilities.astype(BF16), grad_heads, preferred_element_type=F32
    )
    grad_probs = jnp.einsum("ihd,jhd->hij", grad_heads, values, preferred_element_type=F32)
    row_inner = jnp.sum(probabilities * grad_probs, axis=-1, keepdims=True)
    grad_scores = (probabilities * (grad_probs - row_inner)).astype(BF16)
    grad_queries = (
        jnp.einsum("hij,jhd->ihd", grad_scores, keys, preferred_element_type=F32) * scaling
    )
    grad_keys = (
        jnp.einsum("hij,ihd->jhd", grad_scores, queries, preferred_element_type=F32) * scaling
    )
    score_sums = grad_scores.astype(F32)
    decay_grad = jnp.sum(score_sums, axis=2).T - jnp.sum(score_sums, axis=1).T
    later = jnp.flip(jnp.cumsum(jnp.flip(decay_grad, 0), axis=0), 0)
    grad_logits_low = (later * jax.nn.sigmoid(-forget_logits)).astype(BF16)
    bias_part = jnp.zeros((own_heads * n_ctx,), F32)
    bias_part = lax.dynamic_update_slice_in_dim(
        bias_part, jnp.sum(grad_logits_low.astype(F32), axis=0), me * own_heads, 0
    )[:n_heads]

    grad_mixed_low = jnp.concatenate(
        [
            g.astype(BF16).reshape(seq_rows, own_width)
            for g in (grad_queries, grad_keys, grad_values, grad_gatelog_low)
        ]
        + [grad_logits_low],
        axis=1,
    )
    grad_normed = sum_rows(matmul_rows(grad_mixed_low, mixed_in), 3)
    back_one, grad_gain_one = norm_back(grad_normed, normed_one, rstat_one, gain_one)
    grad_inputs = grad_middle + back_one

    grad_mixed_in = sum_grad(weight_grad(normed, grad_mixed_low))
    grad_out_part = sum_grad(weight_grad(gated_all, grad_branch_own))

    def spread(value):
        return lax.all_gather(value, "ctx", axis=0)

    def columns_of(pieces, size):
        full = jnp.moveaxis(pieces, 0, 1).reshape(pieces.shape[1], -1)
        return full[:, :size].astype(F32)

    spread_ffn_in = spread(grad_ffn_in)
    spread_ffn_out = spread(grad_ffn_out)
    grad_attn_part = jnp.concatenate([grad_mixed_in, grad_out_part], axis=1)
    spread_attn = gather_rows(grad_attn_part, 4).reshape((n_ctx,) + grad_attn_part.shape)

    def ffn_columns(pieces):
        pieces = pieces.reshape(n_ctx, shard_rows, n_fsdp, ffn_piece)
        return jnp.transpose(pieces, (1, 2, 0, 3)).reshape(shard_rows, -1).astype(F32)

    grad_weights = [
        columns_of(spread_attn[:, :, split[i] : split[i + 1]], width) for i in range(4)
    ]
    grad_forget = columns_of(spread_attn[:, :, split[4] : split[4] + own_heads], n_heads)
    grad_out_full = columns_of(spread_attn[:, :, split[4] + own_heads :], width)
    small = lax.psum((grad_gain_one, grad_gain_two, bias_part), ("ctx", "fsdp"))
    return (
        output.astype(BF16)[None],
        grad_inputs[None],
        small[0],
        grad_weights[0],
        grad_weights[1],
        grad_weights[2],
        grad_forget,
        small[2],
        grad_weights[3],
        grad_out_full,
        small[1],
        ffn_columns(spread_ffn_in[:, :, :ffn_width]),
        ffn_columns(spread_ffn_in[:, :, ffn_width:]),
        spread_ffn_out.reshape(ffn_rows, width).astype(F32),
    )


def solution(mesh):
    rows, blocks = P("fsdp", None), P("fsdp", "ctx", None)
    return jax.shard_map(
        shards,
        mesh=mesh,
        in_specs=(blocks, rows, P())
        + (rows,) * 4
        + (P(), rows, rows, P(), rows, rows, rows, blocks),
        out_specs=(blocks, blocks, P())
        + (rows,) * 4
        + (P(), rows, rows, P(), rows, rows, rows),
        check_vma=False,
    )
```

```python
import jax
import jax.numpy as jnp
from jax import lax
from jax.experimental import pallas as pl
from jax.experimental.pallas import tpu as pltpu
from jax.sharding import PartitionSpec as P

EPSILON = 1e-06
NEGATIVE = -1e30
BF16, F32 = jnp.bfloat16, jnp.float32


def matmul(left, right):
    return jnp.dot(left, right, preferred_element_type=F32)


def matmul_rows(left, right):
    return lax.dot_general(left, right, (((1,), (1,)), ((), ())), preferred_element_type=F32)


def weight_grad(left, right):
    return lax.dot_general(left, right, (((0,), (0,)), ((), ())), preferred_element_type=F32)


def rms_stats(values):
    rstat = lax.rsqrt(jnp.mean(values * values, axis=-1, keepdims=True) + EPSILON)
    return (values * rstat, rstat)


def norm_back(grad_in, normed, rstat, gain):
    grad_normed = grad_in * gain
    grad_gain = jnp.sum(grad_in * normed, axis=0)
    grad_values = rstat * (
        grad_normed - normed * jnp.mean(grad_normed * normed, axis=-1, keepdims=True)
    )
    return (grad_values, grad_gain)


MESH = pl.DeviceIdType.MESH
RING_PIECES = 4


def ring_place(ctx, count):
    odd = ctx % 2
    return ctx // 2 + odd * (count - 1 - 2 * (ctx // 2))


def ring_index(place, count):
    back = place // (count // 2)
    return 2 * place + back * (2 * (count - 1 - place) + 1 - 2 * place)


class Ring:
    def __init__(self, count):
        self.count, self.half = count, count // 2
        self.ctx, self.fsdp = lax.axis_index("ctx"), lax.axis_index("fsdp")
        self.place = ring_place(self.ctx, count)

    def at(self, offset):
        return ring_index((self.place + offset + self.count) % self.count, self.count)

    def device(self, offset):
        return (self.at(offset), self.fsdp)


def greet(devices):
    barrier = pltpu.get_barrier_semaphore()
    for device in devices:
        pl.semaphore_signal(barrier, inc=1, device_id=device, device_id_type=MESH)
    pl.semaphore_wait(barrier, len(devices))


def remote(src, dst, send, recv, device):
    return pltpu.make_async_remote_copy(
        src_ref=src, dst_ref=dst, send_sem=send, recv_sem=recv, device_id=device, device_id_type=MESH
    )


def carried(step, half, pieces, way):
    if step < half - 1:
        return range(pieces)
    return range(pieces // 2) if way == 0 else range(pieces // 2, pieces)


def ring_gather(ring, own, full, local_sem, send_sem, recv_sem, absolute=False, pieces=RING_PIECES):
    rows = own.shape[0] // pieces

    def part(k):
        return pl.ds(k * rows, rows)

    def slot(step, sign, holder=0):
        if absolute:
            return ring.at(-sign * step)
        return (sign * (step + holder)) % ring.count

    keep = pltpu.make_async_copy(own, full.at[slot(0, 1)], local_sem)
    keep.start()
    copies = {}
    for step in range(ring.half):
        for k in range(pieces):
            for way, sign in ((0, 1), (1, -1)):
                if k not in carried(step, ring.half, pieces, way):
                    continue
                if step > 0:
                    copies[step - 1, k, way].wait_recv()
                src = own.at[part(k)] if step == 0 else full.at[slot(step, sign), part(k)]
                copy = remote(
                    src,
                    full.at[slot(step, sign, 1), part(k)],
                    send_sem.at[step, k, way],
                    recv_sem.at[step, k, way],
                    ring.device(sign),
                )
                copy.start()
                copies[step, k, way] = copy
            yield
    for (step, k, way), copy in copies.items():
        if step == ring.half - 1 or k not in carried(step + 1, ring.half, pieces, way):
            copy.wait_recv()
    for copy in copies.values():
        copy.wait_send()
    keep.wait()


def ring_sum(ring, parts, held, total, send_sem, recv_sem, absolute, pieces=RING_PIECES):
    rows = parts.shape[1] // pieces

    def place(offset):
        return ring.at(offset) if absolute else -offset % ring.count

    def part(k):
        return pl.ds(k * rows, rows)

    copies = {}
    for step in range(ring.half):
        for k in range(pieces):
            for way, sign in ((0, 1), (1, -1)):
                if k not in carried(ring.half - 1 - step, ring.half, pieces, way):
                    continue
                block = place(sign * (ring.half - step))
                src = parts.at[block, part(k)]
                if (step - 1, k, way) in copies:
                    copies[step - 1, k, way].wait_recv()
                    slot = held.at[way, step - 1, part(k)]
                    slot[...] = (slot[...].astype(F32) + src[...].astype(F32)).astype(BF16)
                    src = slot
                copy = remote(
                    src,
                    held.at[way, step, part(k)],
                    send_sem.at[step, k, way],
                    recv_sem.at[step, k, way],
                    ring.device(sign),
                )
                copy.start()
                copies[step, k, way] = copy
            yield
    last = ring.half - 1
    for k in range(pieces):
        for way in range(2):
            copies[last, k, way].wait_recv()
        total[part(k)] = (
            parts[place(0), part(k)].astype(F32)
            + held[0, last, part(k)].astype(F32)
            + held[1, last, part(k)].astype(F32)
        )
    for copy in copies.values():
        copy.wait_send()


def ring_sems(count, pieces=RING_PIECES):
    shape = (count // 2, pieces, 2)
    return [pltpu.SemaphoreType.DMA(shape), pltpu.SemaphoreType.DMA(shape)]


def sems(*counts):
    return [pltpu.SemaphoreType.DMA((max(count, 1),)) for count in counts]


ANYWHERE, VMEM = pl.BlockSpec(memory_space=pl.ANY), pl.BlockSpec(memory_space=pltpu.VMEM)


class RingGather:
    def __init__(self, value, absolute=False):
        self.absolute = absolute
        count = lax.axis_size("ctx")
        self.ins, self.in_specs = [value], [ANYWHERE]
        self.outs, self.out_specs = (
            [jax.ShapeDtypeStruct((count,) + value.shape, value.dtype)],
            [ANYWHERE],
        )
        self.scratch = [pltpu.SemaphoreType.DMA] + ring_sems(count)

    def peers(self, ring):
        return [ring.device(1), ring.device(-1)]

    def run(self, ring, ins, outs, scratch):
        return ring_gather(ring, ins[0], outs[0], *scratch, absolute=self.absolute)


class RingSum:
    def __init__(self, partial, absolute=False):
        self.absolute = absolute
        count = lax.axis_size("ctx")
        rows, width = partial.shape[0] // count, partial.shape[1]
        self.ins, self.in_specs = [partial.astype(BF16).reshape(count, rows, width)], [VMEM]
        self.outs, self.out_specs = [jax.ShapeDtypeStruct((rows, width), F32)], [VMEM]
        self.scratch = [pltpu.VMEM((2, count // 2, rows, width), BF16)] + ring_sems(count)

    def peers(self, ring):
        return [ring.device(1), ring.device(-1)]

    def run(self, ring, ins, outs, scratch):
        return ring_sum(ring, ins[0], scratch[0], outs[0], *scratch[1:], self.absolute)


def shard_pair(ring, shards):
    me = ring.fsdp
    pair = me + 1 - 2 * (me % 2)
    return pair, [(me + 2 * hop) % shards for hop in range(1, shards // 2)]


def idle(turns):
    for _ in range(turns):
        yield


class ShardGather:
    def __init__(self, sources, piece=None):
        shards = lax.axis_size("fsdp")
        starts = None if piece is None else range(shards)
        self.starts, self.piece = starts, piece
        rows = sources[0].shape[0]
        width = sources[0].shape[1] if starts is None else len(sources) * len(starts) * piece
        self.ins, self.in_specs = list(sources), [ANYWHERE] * len(sources)
        self.outs = [jax.ShapeDtypeStruct((shards, rows, width), BF16)]
        self.out_specs = [ANYWHERE]
        parts = 1 if starts is None else len(sources) * len(starts)
        self.scratch = sems(parts, shards - 1, shards - 1)

    def peers(self, ring):
        pair, others = shard_pair(ring, lax.axis_size("fsdp"))
        return [(ring.ctx, to) for to in [pair] + others]

    def run(self, ring, ins, outs, scratch):
        whole, (local_sem, send_sem, recv_sem) = outs[0], scratch
        shards, me = lax.axis_size("fsdp"), ring.fsdp
        pair, others = shard_pair(ring, shards)
        local = []
        if self.starts is None:
            local.append(pltpu.make_async_copy(ins[0], whole.at[me], local_sem.at[0]))
        else:
            for i, source in enumerate(ins):
                for j, start in enumerate(self.starts):
                    at = i * len(self.starts) + j
                    start = (start * ring.count + ring.ctx) * self.piece
                    start = pl.multiple_of(start, self.piece)
                    local.append(
                        pltpu.make_async_copy(
                            source.at[:, pl.ds(start, self.piece)],
                            whole.at[me, :, pl.ds(at * self.piece, self.piece)],
                            local_sem.at[at],
                        )
                    )
        for copy in local:
            copy.start()
        yield
        if self.starts is None:
            block = ins[0]
        else:
            for copy in local:
                copy.wait()
            block = whole.at[me]
        copies = [
            remote(block, whole.at[me], send_sem.at[i], recv_sem.at[i], (ring.ctx, to))
            for i, to in enumerate([pair] + others)
        ]
        for copy in copies:
            copy.start()
        yield from idle(3 * RING_PIECES)
        passed = []
        for i in range(1, len(copies)):
            copies[i].wait_recv()
            origin = (me - 2 * i + shards) % shards
            at = shards // 2 - 1 + i
            copy = remote(
                whole.at[origin], whole.at[origin], send_sem.at[at], recv_sem.at[at], (ring.ctx, pair)
            )
            copy.start()
            passed.append(copy)
        yield from idle(2)
        copies[0].wait_recv()
        for copy in passed:
            copy.wait_recv()
        for copy in copies + passed:
            copy.wait_send()
        if self.starts is None:
            local[0].wait()


class ShardSum:
    def __init__(self, partial):
        shards = lax.axis_size("fsdp")
        rows, width = partial.shape[0] // shards, partial.shape[1]
        self.ins, self.in_specs = [partial.astype(BF16).reshape(shards, rows, width)], [VMEM]
        self.outs, self.out_specs = [jax.ShapeDtypeStruct((rows, width), BF16)], [VMEM]
        half = shards // 2
        self.scratch = [
            pltpu.VMEM((half, rows, width), BF16),
            pltpu.VMEM((max(half - 1, 1), rows, width), BF16),
        ] + sems(half, half, half - 1, half - 1)

    def peers(self, ring):
        pair, others = shard_pair(ring, lax.axis_size("fsdp"))
        return [(ring.ctx, to) for to in [pair] + others]

    def run(self, ring, ins, outs, scratch):
        parts, (near, far, near_send, near_recv, far_send, far_recv) = ins[0], scratch
        shards, me = lax.axis_size("fsdp"), ring.fsdp
        half, core, chip = shards // 2, me % 2, me // 2
        pair, others = shard_pair(ring, shards)
        first = [
            remote(
                parts.at[2 * i + 1 - core],
                near.at[i],
                near_send.at[i],
                near_recv.at[i],
                (ring.ctx, pair),
            )
            for i in range(half)
        ]
        for copy in first:
            copy.start()
        yield from idle(2)
        for copy in first:
            copy.wait_recv()
        second = []
        for hop in range(1, half):
            to = (chip + hop) % half
            near[to] = (near[to].astype(F32) + parts[2 * to + core].astype(F32)).astype(BF16)
            copy = remote(
                near.at[to],
                far.at[hop - 1],
                far_send.at[hop - 1],
                far_recv.at[hop - 1],
                (ring.ctx, others[hop - 1]),
            )
            copy.start()
            second.append(copy)
        yield from idle(3 * RING_PIECES)
        total = parts[me].astype(F32) + near[chip].astype(F32)
        for hop, copy in enumerate(second):
            copy.wait_recv()
            total = total + far[hop].astype(F32)
        outs[0][...] = total.astype(BF16)
        for copy in first + second:
            copy.wait_send()


class SmallSum:
    def __init__(self, small):
        count, shards = lax.axis_size("ctx"), lax.axis_size("fsdp")
        self.ins, self.in_specs = [small], [VMEM]
        self.outs, self.out_specs = [jax.ShapeDtypeStruct(small.shape, F32)], [VMEM]
        self.scratch = [
            pltpu.VMEM((shards,) + small.shape, F32),
            pltpu.VMEM((count,) + small.shape, F32),
        ] + sems(shards - 1, shards - 1, count - 1, count - 1)

    def devices(self, ring):
        count, shards = lax.axis_size("ctx"), lax.axis_size("fsdp")
        siblings = [(ring.ctx, (ring.fsdp + hop) % shards) for hop in range(1, shards)]
        return siblings, [((ring.ctx + hop) % count, ring.fsdp) for hop in range(1, count)]

    def peers(self, ring):
        return sum(self.devices(ring), [])

    def run(self, ring, ins, outs, scratch):
        near, far, near_send, near_recv, far_send, far_recv = scratch
        siblings, peers = self.devices(ring)
        me, row = ring.fsdp, ring.ctx
        near[me] = ins[0][...]
        first = [
            remote(ins[0], near.at[me], near_send.at[i], near_recv.at[i], to)
            for i, to in enumerate(siblings)
        ]
        for copy in first:
            copy.start()
        yield
        for copy in first:
            copy.wait()
        far[row] = sum([near[i] for i in range(len(siblings) + 1)])
        second = [
            remote(far.at[row], far.at[row], far_send.at[i], far_recv.at[i], to)
            for i, to in enumerate(peers)
        ]
        for copy in second:
            copy.start()
        yield
        yield
        for copy in second:
            copy.wait()
        outs[0][...] = sum([far[i] for i in range(len(peers) + 1)])


class Attention:
    def __init__(self, qkv, decay, seg, own_heads):
        self.rows, self.heads = qkv.shape[0], own_heads
        self.dim = qkv.shape[1] // 3 // own_heads
        self.scaling = self.dim ** (-0.5)
        self.tall = min(256, self.rows)
        self.ins = [qkv, decay, decay.T, seg[:, None], seg[None, :]]

    def block(self, index):
        rows = slice(index * self.tall, (index + 1) * self.tall)
        return rows, (index + 1) * self.tall

    def allowed(self, rows, wide, seg_rows, seg_cols):
        shape = (self.tall, wide)
        here = lax.broadcasted_iota(jnp.int32, shape, 0) + rows.start
        there = lax.broadcasted_iota(jnp.int32, shape, 1)
        return (there <= here) & (seg_rows[rows] == seg_cols[:, :wide])

    def part(self, qkv, which, head, rows):
        start = (which * self.heads + head) * self.dim
        return qkv[rows, start : start + self.dim]

    def scores(self, refs, head, rows, wide, allowed):
        qkv, decay, decay_cols = refs[:3]
        queries = self.part(qkv, 0, head, rows)
        keys = self.part(qkv, 1, head, slice(0, wide))
        scores = matmul_rows(queries, keys) * self.scaling
        scores = scores + decay[rows, head : head + 1] - decay_cols[head : head + 1, :wide]
        return queries, keys, jnp.where(allowed, scores, NEGATIVE)

    def peers(self, ring):
        return []


class AttentionForward(Attention):
    def __init__(self, qkv, decay, seg, own_heads):
        super().__init__(qkv, decay, seg, own_heads)
        self.in_specs = [VMEM] * 5
        self.outs = [
            jax.ShapeDtypeStruct((self.rows, own_heads * self.dim), F32),
            jax.ShapeDtypeStruct((self.rows, own_heads), F32),
        ]
        self.out_specs, self.scratch = [VMEM] * 2, []

    def run(self, ring, ins, outs, scratch):
        for index in range(self.rows // self.tall):
            rows, wide = self.block(index)
            allowed = self.allowed(rows, wide, *ins[3:])
            mixed, totals = [], []
            for head in range(self.heads):
                _, _, scores = self.scores(ins, head, rows, wide, allowed)
                row_max = jnp.max(scores, axis=1, keepdims=True)
                raised = jnp.exp(scores - row_max)
                row_total = jnp.sum(raised, axis=1, keepdims=True)
                probabilities = (raised * (1.0 / row_total)).astype(BF16)
                mixed.append(matmul(probabilities, self.part(ins[0], 2, head, slice(0, wide))))
                totals.append(row_max + jnp.log(row_total))
                if head < self.heads - 1:
                    yield
            outs[0][rows] = jnp.concatenate(mixed, axis=1)
            outs[1][rows] = jnp.concatenate(totals, axis=1)
            yield


class AttentionBackward(Attention):
    def __init__(self, qkv, decay, seg, own_heads, log_totals, grad_attn):
        super().__init__(qkv, decay, seg, own_heads)
        self.ins = self.ins + [log_totals, grad_attn]
        self.in_specs = [VMEM] * 7
        self.outs = [
            jax.ShapeDtypeStruct(qkv.shape, BF16),
            jax.ShapeDtypeStruct((self.rows, own_heads), F32),
            jax.ShapeDtypeStruct((own_heads, self.rows), F32),
        ]
        self.out_specs = [VMEM] * 3
        self.scratch = [pltpu.VMEM((3, own_heads, self.rows, self.dim), F32)]

    def run(self, ring, ins, outs, scratch):
        log_totals, grad_attn = ins[5:]
        grads, (sums,) = scratch, outs[2:]
        grad_q, grad_k, grad_v = [grads[0].at[i] for i in range(3)]
        blocks = self.rows // self.tall
        for index in reversed(range(blocks)):
            rows, wide = self.block(index)
            allowed = self.allowed(rows, wide, *ins[3:5])
            own = slice(0, wide)
            row_sums = []
            for head in range(self.heads):
                queries, keys, scores = self.scores(ins, head, rows, wide, allowed)
                probabilities = jnp.exp(scores - log_totals[rows, head : head + 1])
                grad_part = grad_attn[rows, head * self.dim : (head + 1) * self.dim]
                grad_probs = matmul_rows(grad_part, self.part(ins[0], 2, head, own))
                row_inner = jnp.sum(probabilities * grad_probs, axis=1, keepdims=True)
                grad_scores = (probabilities * (grad_probs - row_inner)).astype(BF16)
                grad_q[head, rows] = matmul(grad_scores, keys) * self.scaling
                from_k = weight_grad(grad_scores, queries) * self.scaling
                from_v = weight_grad(probabilities.astype(BF16), grad_part)
                wide_sums = grad_scores.astype(F32)
                row_sums.append(jnp.sum(wide_sums, axis=1, keepdims=True))
                column_sums = jnp.sum(wide_sums, axis=0, keepdims=True)
                if index == blocks - 1:
                    grad_k[head], grad_v[head] = from_k, from_v
                    sums[head : head + 1] = column_sums
                else:
                    grad_k[head, own] += from_k
                    grad_v[head, own] += from_v
                    sums[head : head + 1, own] += column_sums
                if head < self.heads - 1:
                    yield
            outs[1][rows] = jnp.concatenate(row_sums, axis=1)
            yield
        for index in range(blocks):
            rows, _ = self.block(index)
            outs[0][rows] = jnp.concatenate(
                [g[head, rows] for g in (grad_q, grad_k, grad_v) for head in range(self.heads)],
                axis=1,
            ).astype(BF16)


def running_sum(values, backward=False):
    tall = 128 if values.shape[0] % 128 == 0 else values.shape[0]
    blocks = values.reshape(-1, tall, values.shape[1])
    ones = jnp.ones((tall, tall), F32)
    wedge = jnp.triu(ones) if backward else jnp.tril(ones)
    inside = jnp.einsum("st,btk->bsk", wedge, blocks, precision=lax.Precision.HIGHEST)
    totals = jnp.sum(blocks, axis=1)
    count = totals.shape[0]
    before = jnp.tril(jnp.ones((count, count), F32), -1)
    before = before.T if backward else before
    return (inside + jnp.sum(before[:, :, None] * totals[None], axis=1)[:, None]).reshape(values.shape)


def exchange(ident, name, *tasks):
    count = lax.axis_size("ctx")

    def take(refs, sizes):
        groups, at = [], 0
        for size in sizes:
            groups.append(refs[at : at + size])
            at += size
        return groups

    ins = [len(task.ins) for task in tasks]
    outs = [len(task.outs) for task in tasks]
    scratch = [len(task.scratch) for task in tasks]

    def kernel(*refs):
        ring = Ring(count)
        greeted = []
        for kind in {type(task).__name__: task for task in tasks}.values():
            greeted.append(kind)
        near, along, small = [], [], []
        for task in greeted:
            if isinstance(task, SmallSum):
                small = task.peers(ring)
            elif isinstance(task, (RingGather, RingSum)):
                near = task.peers(ring)
            elif isinstance(task, (ShardGather, ShardSum)):
                along = task.peers(ring)
        greet(small if small else near + along)
        groups = [
            take(refs[: sum(ins)], ins),
            take(refs[sum(ins) : sum(ins) + sum(outs)], outs),
            take(refs[sum(ins) + sum(outs) :], scratch),
        ]
        walks = [task.run(ring, *parts) for task, *parts in zip(tasks, *groups)]
        while walks:
            walks = [walk for walk in walks if next(walk, walks) is None]

    results = pl.pallas_call(
        kernel,
        out_shape=sum([task.outs for task in tasks], []),
        in_specs=sum([task.in_specs for task in tasks], []),
        out_specs=sum([task.out_specs for task in tasks], []),
        scratch_shapes=sum([task.scratch for task in tasks], []),
        compiler_params=pltpu.CompilerParams(
            collective_id=ident, has_side_effects=True, vmem_limit_bytes=48 * 2**20
        ),
        cost_estimate=pl.CostEstimate(flops=0, bytes_accessed=100_000_000, transcendentals=0),
        name=name,
    )(*sum([task.ins for task in tasks], []))
    return take(list(results), outs)


def flat(blocks):
    return blocks.reshape(-1, blocks.shape[-1])


def ffn_columns(blocks, n_fsdp):
    count, rows, both = blocks.shape
    width, piece = both // 2, both // 2 // n_fsdp
    steps = 4
    tall = rows // steps

    def kernel(block_ref, *outs):
        for j in range(count):
            for half in range(2):
                for group in range(n_fsdp):
                    start, to = half * width + group * piece, (group * count + j) * piece
                    outs[half][:, to : to + piece] = block_ref[j, :, start : start + piece].astype(F32)

    wide = jax.ShapeDtypeStruct((rows, width * count), F32)
    spec = pl.BlockSpec((tall, width * count), lambda i: (i, 0))
    return pl.pallas_call(
        kernel,
        out_shape=(wide, wide),
        grid=(steps,),
        in_specs=[pl.BlockSpec((count, tall, both), lambda i: (0, i, 0))],
        out_specs=(spec, spec),
        compiler_params=pltpu.CompilerParams(vmem_limit_bytes=40 * 2**20),
        cost_estimate=pl.CostEstimate(
            flops=0, bytes_accessed=rows * both * count * 6, transcendentals=0
        ),
        name="ffn_columns",
    )(blocks)


def head_columns(blocks, sizes, widths):
    count, rows, total = blocks.shape
    steps = 4
    tall = rows // steps
    starts = [sum(sizes[:i]) for i in range(len(sizes))]

    def kernel(block_ref, *outs):
        for start, size, out in zip(starts, sizes, outs):
            for i in range(0, count, 2):
                pair = jnp.concatenate(
                    [block_ref[i + k][:, start : start + size].astype(F32) for k in range(2)], axis=1
                )
                at = i * size
                keep = min(2 * size, out.shape[1] - at)
                if keep > 0:
                    out[:, at : at + keep] = pair[:, :keep]

    return pl.pallas_call(
        kernel,
        out_shape=tuple(jax.ShapeDtypeStruct((rows, w), F32) for w in widths),
        grid=(steps,),
        in_specs=[pl.BlockSpec((count, tall, total), lambda i: (0, i, 0))],
        out_specs=tuple(pl.BlockSpec((tall, w), lambda i: (i, 0)) for w in widths),
        compiler_params=pltpu.CompilerParams(vmem_limit_bytes=40 * 2**20),
        cost_estimate=pl.CostEstimate(
            flops=0, bytes_accessed=count * rows * total * 6, transcendentals=0
        ),
        name="head_columns",
    )(blocks)


def rows_to_columns(value):
    return lax.all_to_all(value, "ctx", split_axis=1, concat_axis=0, tiled=True)


def columns_to_rows(value):
    return lax.all_to_all(value, "ctx", split_axis=0, concat_axis=1, tiled=True)


def shards(
    tokens,
    segments,
    gain_attn,
    w_query,
    w_key,
    w_value,
    w_forget,
    forget_bias,
    w_outgate,
    w_out,
    gain_ffn,
    w_gate,
    w_up,
    w_down,
    cotangent,
):
    n_ctx, me = lax.axis_size("ctx"), lax.axis_index("ctx")
    n_fsdp = lax.axis_size("fsdp")
    tok_rows, width = tokens.shape[1:]
    seq_rows = tok_rows * n_ctx
    n_heads = forget_bias.shape[0]
    head_dim = width // n_heads
    own_heads = -(-n_heads // n_ctx)
    own_width = own_heads * head_dim
    padded = own_width * n_ctx
    ffn_rows = w_down.shape[0]
    ffn_piece = ffn_rows // n_ctx
    ffn_width = ffn_piece * n_fsdp
    shard_rows = w_query.shape[0]

    def widen(value, size):
        return jnp.pad(value, ((0, 0), (0, size - value.shape[1])))

    def own_columns(weight, size):
        return lax.dynamic_slice_in_dim(widen(weight, size * n_ctx), me * size, size, 1)

    def own_ffn(weight):
        return [
            lax.dynamic_slice_in_dim(weight, (group * n_ctx + me) * ffn_piece, ffn_piece, 1)
            for group in range(n_fsdp)
        ]

    mixed_shard = jnp.concatenate(
        [own_columns(w, own_width) for w in (w_query, w_key, w_value, w_outgate)]
        + [own_columns(w_forget, own_heads)],
        axis=1,
    )
    bias_own = lax.dynamic_slice_in_dim(
        jnp.pad(forget_bias, (0, own_heads * n_ctx - n_heads)), me * own_heads, own_heads, 0
    )

    seg = segments[0]
    inputs = tokens[0].astype(F32)
    gain_one = gain_attn.astype(F32)
    normed_one, rstat_one = rms_stats(inputs)
    (normed,), (mixed_in,) = exchange(
        0,
        "gather_start",
        RingGather((normed_one * gain_one).astype(BF16), absolute=True),
        ShardGather([mixed_shard]),
    )
    normed, mixed_in = flat(normed), flat(mixed_in)
    normed, out_shard = lax.optimization_barrier((normed, w_out))
    full_out = lax.all_gather(out_shard, "fsdp", axis=0, tiled=True)

    split = [own_width * i for i in range(5)]
    qkv = matmul(normed, mixed_in[:, : split[3]]).astype(BF16)
    mixed = matmul(normed, mixed_in[:, split[3] :])
    gate_value = jax.nn.sigmoid(mixed[:, :own_width])
    forget_logits = mixed[:, own_width:] + bias_own
    decay = running_sum(jax.nn.log_sigmoid(forget_logits))

    (grad_out_low,), (attended, log_totals) = exchange(
        5,
        "attend",
        RingGather(cotangent[0], absolute=True),
        AttentionForward(qkv, decay, seg, own_heads),
    )
    grad_out_low = flat(grad_out_low)
    gated = columns_to_rows((attended * gate_value).astype(BF16))[:, :width]

    middle = inputs + matmul(gated, full_out)
    gain_two = gain_ffn.astype(F32)
    normed_two_f, rstat_two = rms_stats(middle)
    if ffn_piece % 128 == 0:
        ffn_in_task = ShardGather([w_gate, w_up], ffn_piece)
    else:
        ffn_in_task = ShardGather([jnp.concatenate(own_ffn(w_gate) + own_ffn(w_up), axis=1)])
    (normed_two,), (ffn_in,), (ffn_out,) = exchange(
        1,
        "gather_middle",
        RingGather((normed_two_f * gain_two).astype(BF16), absolute=True),
        ffn_in_task,
        ShardGather([lax.dynamic_slice_in_dim(w_down, me * ffn_piece, ffn_piece, 0)]),
    )
    normed_two, ffn_in, ffn_out = flat(normed_two), flat(ffn_in), flat(ffn_out)

    ffn_mid = matmul(normed_two, ffn_in)
    gate_part, up_part = ffn_mid[:, :ffn_width], ffn_mid[:, ffn_width:]
    sig_gate = jax.nn.sigmoid(gate_part)
    silu_gate = gate_part * sig_gate
    hidden = (silu_gate * up_part).astype(BF16)
    out_part = matmul(hidden, ffn_out).astype(BF16)

    grad_hidden = matmul_rows(grad_out_low, ffn_out)
    grad_gate_low = (
        grad_hidden * up_part * (sig_gate * (1.0 + gate_part * (1.0 - sig_gate)))
    ).astype(BF16)
    grad_up_low = (grad_hidden * silu_gate).astype(BF16)
    grad_mid_low = jnp.concatenate([grad_gate_low, grad_up_low], axis=1)
    (grad_normed_two,), (grad_ffn_in,), (grad_ffn_out,) = exchange(
        2,
        "sum_middle",
        RingSum(matmul_rows(grad_mid_low, ffn_in), absolute=True),
        ShardSum(weight_grad(normed_two, grad_mid_low)),
        ShardSum(weight_grad(hidden, grad_out_low)),
    )
    back_two, grad_gain_two = norm_back(grad_normed_two, normed_two_f, rstat_two, gain_two)
    grad_middle = cotangent[0].astype(F32) + back_two

    grad_branch_low = grad_middle.astype(BF16)
    grad_gated = matmul_rows(grad_branch_low, full_out).astype(BF16)
    grad_gated = rows_to_columns(widen(grad_gated, padded)).astype(F32)
    grad_branch_own = rows_to_columns(widen(grad_branch_low, padded))
    grad_attn_low = (grad_gated * gate_value).astype(BF16)
    grad_gatelog_low = (grad_gated * attended * (gate_value * (1.0 - gate_value))).astype(BF16)

    (spread_ffn_in,), (spread_ffn_out,), (out_sum,), (gated_all,), (grad_qkv, row_sums, column_sums) = exchange(
        6,
        "attend_back",
        RingGather(grad_ffn_in, absolute=True),
        RingGather(grad_ffn_out, absolute=True),
        RingSum(out_part, absolute=True),
        RingGather(gated, absolute=True),
        AttentionBackward(qkv, decay, seg, own_heads, log_totals, grad_attn_low),
    )
    output, gated_all = middle + out_sum, flat(gated_all)
    later = running_sum(row_sums - column_sums.T, backward=True)
    grad_logits_low = (later * jax.nn.sigmoid(-forget_logits)).astype(BF16)
    bias_part = jnp.zeros((own_heads * n_ctx,), F32)
    bias_part = lax.dynamic_update_slice_in_dim(
        bias_part, jnp.sum(grad_logits_low.astype(F32), axis=0), me * own_heads, 0
    )[:n_heads]

    grad_mixed_low = jnp.concatenate([grad_qkv, grad_gatelog_low, grad_logits_low], axis=1)
    (grad_normed,), (grad_mixed_in,), (grad_out_part,) = exchange(
        3,
        "sum_end",
        RingSum(matmul_rows(grad_mixed_low, mixed_in), absolute=True),
        ShardSum(weight_grad(normed, grad_mixed_low)),
        ShardSum(weight_grad(gated_all, grad_branch_own)),
    )
    back_one, grad_gain_one = norm_back(grad_normed, normed_one, rstat_one, gain_one)
    grad_inputs = grad_middle + back_one

    def pad_rows(rows):
        rows = [jnp.pad(row, (0, width - row.shape[0])) for row in rows]
        return jnp.stack(rows + [jnp.zeros((width,), F32)] * (8 - len(rows)))

    grad_attn_part = jnp.concatenate([grad_mixed_in, grad_out_part], axis=1)
    (spread_attn,), (small,) = exchange(
        4,
        "gather_end",
        RingGather(grad_attn_part, absolute=True),
        SmallSum(pad_rows([grad_gain_one, grad_gain_two, bias_part])),
    )
    sizes = [own_width] * 4 + [own_heads, own_width]
    if ffn_piece % 128 == 0:
        grad_gate, grad_up = ffn_columns(spread_ffn_in, n_fsdp)
    else:
        whole = spread_ffn_in.reshape(n_ctx, shard_rows, 2, n_fsdp, ffn_piece)
        whole = jnp.transpose(whole, (2, 1, 3, 0, 4)).reshape(2, shard_rows, -1).astype(F32)
        grad_gate, grad_up = whole[0], whole[1]
    grad_weights = head_columns(spread_attn, sizes, [width] * 4 + [n_heads, width])
    return (
        output.astype(BF16)[None],
        grad_inputs[None],
        small[0],
        grad_weights[0],
        grad_weights[1],
        grad_weights[2],
        grad_weights[4],
        small[2, :n_heads],
        grad_weights[3],
        grad_weights[5],
        small[1],
        grad_gate,
        grad_up,
        spread_ffn_out.reshape(ffn_rows, width).astype(F32),
    )


def solution(mesh):
    rows, blocks = P("fsdp", None), P("fsdp", "ctx", None)
    return jax.shard_map(
        shards,
        mesh=mesh,
        in_specs=(blocks, rows, P())
        + (rows,) * 4
        + (P(), rows, rows, P(), rows, rows, rows, blocks),
        out_specs=(blocks, blocks, P())
        + (rows,) * 4
        + (P(), rows, rows, P(), rows, rows, rows),
        check_vma=False,
    )
```

```python
import jax
import jax.numpy as jnp
from jax import lax
from jax.experimental import pallas as pl
from jax.experimental.pallas import tpu as pltpu
from jax.sharding import PartitionSpec as P

EPSILON = 1e-06
NEGATIVE = -1e30
BF16, F32 = jnp.bfloat16, jnp.float32


def matmul(left, right):
    return jnp.dot(left, right, preferred_element_type=F32)


def matmul_rows(left, right):
    return lax.dot_general(left, right, (((1,), (1,)), ((), ())), preferred_element_type=F32)


def weight_grad(left, right):
    return lax.dot_general(left, right, (((0,), (0,)), ((), ())), preferred_element_type=F32)


def rms_stats(values):
    rstat = lax.rsqrt(jnp.mean(values * values, axis=-1, keepdims=True) + EPSILON)
    return (values * rstat, rstat)


def norm_back(grad_in, normed, rstat, gain):
    grad_normed = grad_in * gain
    grad_gain = jnp.sum(grad_in * normed, axis=0)
    grad_values = rstat * (
        grad_normed - normed * jnp.mean(grad_normed * normed, axis=-1, keepdims=True)
    )
    return (grad_values, grad_gain)


MESH = pl.DeviceIdType.MESH
RING_PIECES = 4


def ring_place(ctx, count):
    odd = ctx % 2
    return ctx // 2 + odd * (count - 1 - 2 * (ctx // 2))


def ring_index(place, count):
    back = place // (count // 2)
    return 2 * place + back * (2 * (count - 1 - place) + 1 - 2 * place)


class Ring:
    def __init__(self, count):
        self.count, self.half = count, count // 2
        self.ctx, self.fsdp = lax.axis_index("ctx"), lax.axis_index("fsdp")
        self.place = ring_place(self.ctx, count)

    def at(self, offset):
        return ring_index((self.place + offset + self.count) % self.count, self.count)

    def device(self, offset):
        return (self.at(offset), self.fsdp)


def greet(devices):
    barrier = pltpu.get_barrier_semaphore()
    for device in devices:
        pl.semaphore_signal(barrier, inc=1, device_id=device, device_id_type=MESH)
    pl.semaphore_wait(barrier, len(devices))


def remote(src, dst, send, recv, device):
    return pltpu.make_async_remote_copy(
        src_ref=src, dst_ref=dst, send_sem=send, recv_sem=recv, device_id=device, device_id_type=MESH
    )


def carried(step, half, pieces, way):
    if step < half - 1:
        return range(pieces)
    return range(pieces // 2) if way == 0 else range(pieces // 2, pieces)


def ring_slot(ring, offset, absolute):
    if absolute:
        return ring.at(offset)
    if abs(offset) == ring.half:
        return ring.count - 1
    return 2 * offset - 1 if offset > 0 else -2 * offset


def ring_gather(ring, own, full, local_sem, send_sem, recv_sem, absolute, pieces=RING_PIECES):
    rows = own.shape[0] // pieces

    def part(k):
        return pl.ds(k * rows, rows)

    def slot(offset):
        return ring_slot(ring, offset, absolute)

    keep = pltpu.make_async_copy(own, full.at[slot(0)], local_sem)
    keep.start()
    copies = {}
    for step in range(ring.half):
        for k in range(pieces):
            for way, sign in ((0, 1), (1, -1)):
                if k not in carried(step, ring.half, pieces, way):
                    continue
                if step > 0:
                    copies[step - 1, k, way].wait_recv()
                src = own.at[part(k)] if step == 0 else full.at[slot(-sign * step), part(k)]
                to = slot(-sign * step if absolute else -sign * (step + 1))
                copy = remote(
                    src,
                    full.at[to, part(k)],
                    send_sem.at[step, k, way],
                    recv_sem.at[step, k, way],
                    ring.device(sign),
                )
                copy.start()
                copies[step, k, way] = copy
            yield
    for (step, k, way), copy in copies.items():
        if step == ring.half - 1 or k not in carried(step + 1, ring.half, pieces, way):
            copy.wait_recv()
    for copy in copies.values():
        copy.wait_send()
    keep.wait()


def ring_sum(ring, parts, held, total, send_sem, recv_sem, absolute, pieces=RING_PIECES):
    rows = parts.shape[1] // pieces

    def place(offset):
        return ring_slot(ring, offset, absolute)

    def part(k):
        return pl.ds(k * rows, rows)

    copies = {}
    for step in range(ring.half):
        for k in range(pieces):
            for way, sign in ((0, 1), (1, -1)):
                if k not in carried(ring.half - 1 - step, ring.half, pieces, way):
                    continue
                block = place(sign * (ring.half - step))
                src = parts.at[block, part(k)]
                if (step - 1, k, way) in copies:
                    copies[step - 1, k, way].wait_recv()
                    slot = held.at[way, step - 1, part(k)]
                    slot[...] = (slot[...].astype(F32) + src[...].astype(F32)).astype(BF16)
                    src = slot
                copy = remote(
                    src,
                    held.at[way, step, part(k)],
                    send_sem.at[step, k, way],
                    recv_sem.at[step, k, way],
                    ring.device(sign),
                )
                copy.start()
                copies[step, k, way] = copy
            yield
    last = ring.half - 1
    for k in range(pieces):
        for way in range(2):
            copies[last, k, way].wait_recv()
        total[part(k)] = (
            parts[place(0), part(k)].astype(F32)
            + held[0, last, part(k)].astype(F32)
            + held[1, last, part(k)].astype(F32)
        )
    for copy in copies.values():
        copy.wait_send()


def ring_sems(count, pieces=RING_PIECES):
    shape = (count // 2, pieces, 2)
    return [pltpu.SemaphoreType.DMA(shape), pltpu.SemaphoreType.DMA(shape)]


def sems(*counts):
    return [pltpu.SemaphoreType.DMA((max(count, 1),)) for count in counts]


ANYWHERE, VMEM = pl.BlockSpec(memory_space=pl.ANY), pl.BlockSpec(memory_space=pltpu.VMEM)


class RingGather:
    kinds = ("ring",)

    def __init__(self, value, absolute=False):
        self.absolute = absolute
        count = lax.axis_size("ctx")
        self.ins, self.in_specs = [value], [ANYWHERE]
        self.outs, self.out_specs = (
            [jax.ShapeDtypeStruct((count,) + value.shape, value.dtype)],
            [ANYWHERE],
        )
        self.scratch = [pltpu.SemaphoreType.DMA] + ring_sems(count)

    def run(self, ring, ins, outs, scratch):
        return ring_gather(ring, ins[0], outs[0], *scratch, absolute=self.absolute)


def shard_pair(ring, shards):
    me = ring.fsdp
    pair = me + 1 - 2 * (me % 2)
    return pair, [(me + 2 * hop) % shards for hop in range(1, shards // 2)]


def all_peers(ring):
    count, shards = lax.axis_size("ctx"), lax.axis_size("fsdp")
    siblings = [(ring.ctx, (ring.fsdp + hop) % shards) for hop in range(1, shards)]
    return siblings, [((ring.ctx + hop) % count, ring.fsdp) for hop in range(1, count)]


def idle(turns):
    for _ in range(turns):
        yield


def together(*walks):
    walks = list(walks)
    while walks:
        walks = [walk for walk in walks if next(walk, walks) is None]
        yield


def shard_gather(ring, fill, whole, local_sem, send_sem, recv_sem):
    shards, me = lax.axis_size("fsdp"), ring.fsdp
    rows = whole.shape[0] // shards
    pair, others = shard_pair(ring, shards)

    def shard(index):
        return whole.at[pl.ds(pl.multiple_of(index * rows, rows), rows)]

    local, source = fill(shard(me), local_sem)
    for copy in local:
        copy.start()
    yield
    if source is None:
        for copy in local:
            copy.wait()
    sent = shard(me) if source is None else source
    copies = [
        remote(sent, shard(me), send_sem.at[i], recv_sem.at[i], (ring.ctx, to))
        for i, to in enumerate([pair] + others)
    ]
    for copy in copies:
        copy.start()
    yield from idle(3 * RING_PIECES)
    passed = []
    for i in range(1, len(copies)):
        copies[i].wait_recv()
        origin = (me - 2 * i + shards) % shards
        at = shards // 2 - 1 + i
        copy = remote(
            shard(origin), shard(origin), send_sem.at[at], recv_sem.at[at], (ring.ctx, pair)
        )
        copy.start()
        passed.append(copy)
    yield from idle(2)
    copies[0].wait_recv()
    for copy in passed:
        copy.wait_recv()
    for copy in copies + passed:
        copy.wait_send()
    if source is not None:
        for copy in local:
            copy.wait()


def shard_gather_sems(parts):
    shards = lax.axis_size("fsdp")
    return sems(parts, shards - 1, shards - 1)


class ShardGather:
    kinds = ("shard",)

    def __init__(self, shard):
        shards = lax.axis_size("fsdp")
        self.ins, self.in_specs = [shard], [ANYWHERE]
        self.outs = [jax.ShapeDtypeStruct((shards * shard.shape[0], shard.shape[1]), BF16)]
        self.out_specs, self.scratch = [ANYWHERE], shard_gather_sems(1)

    def run(self, ring, ins, outs, scratch):
        def fill(shard, local_sem):
            return [pltpu.make_async_copy(ins[0], shard, local_sem.at[0])], ins[0]

        return shard_gather(ring, fill, outs[0], *scratch)


def shard_sum(ring, parts, total, near, far, near_send, near_recv, far_send, far_recv):
    shards, me = lax.axis_size("fsdp"), ring.fsdp
    half, core, chip = shards // 2, me % 2, me // 2
    pair, others = shard_pair(ring, shards)
    rows = parts.shape[0] // shards

    def shard(index):
        return pl.ds(pl.multiple_of(index * rows, rows), rows)

    first = [
        remote(
            parts.at[shard(2 * i + 1 - core)],
            near.at[i],
            near_send.at[i],
            near_recv.at[i],
            (ring.ctx, pair),
        )
        for i in range(half)
    ]
    for copy in first:
        copy.start()
    yield from idle(2)
    for copy in first:
        copy.wait_recv()
    second = []
    for hop in range(1, half):
        to = (chip + hop) % half
        near[to] = (near[to].astype(F32) + parts[shard(2 * to + core)].astype(F32)).astype(BF16)
        copy = remote(
            near.at[to],
            far.at[hop - 1],
            far_send.at[hop - 1],
            far_recv.at[hop - 1],
            (ring.ctx, others[hop - 1]),
        )
        copy.start()
        second.append(copy)
    yield from idle(3 * RING_PIECES)
    sums = parts[shard(me)].astype(F32) + near[chip].astype(F32)
    for hop, copy in enumerate(second):
        copy.wait_recv()
        sums = sums + far[hop].astype(F32)
    total[...] = sums.astype(BF16)
    for copy in first + second:
        copy.wait_send()


def shard_sum_scratch(rows, width):
    half = lax.axis_size("fsdp") // 2
    return [
        pltpu.VMEM((half, rows, width), BF16),
        pltpu.VMEM((max(half - 1, 1), rows, width), BF16),
    ] + sems(half, half, half - 1, half - 1)


class Ffn:
    kinds = ("ring", "shard")

    def __init__(self, normed, grad_out, w_in, w_out, piece):
        count, shards = lax.axis_size("ctx"), lax.axis_size("fsdp")
        rows, width = normed.shape
        self.aligned = len(w_in) == 2
        self.piece, self.inner = piece, piece * shards
        inner, both = self.inner, 2 * self.inner
        shard_rows = width // shards
        self.ins = [normed, grad_out, w_out] + list(w_in)
        self.in_specs = [ANYWHERE, VMEM] + [ANYWHERE] * (1 + len(w_in))
        self.outs = [
            jax.ShapeDtypeStruct((rows, width), F32),
            jax.ShapeDtypeStruct((rows, width), F32),
            jax.ShapeDtypeStruct((shard_rows, both), BF16),
            jax.ShapeDtypeStruct((piece, width), BF16),
        ]
        self.out_specs = [VMEM] * 4
        held = pltpu.VMEM((2, count // 2, rows, width), BF16)
        groups = [
            [pltpu.VMEM((count, rows, width), BF16), pltpu.SemaphoreType.DMA] + ring_sems(count),
            [pltpu.VMEM((width, both), BF16)] + shard_gather_sems(2 * shards),
            [pltpu.VMEM((inner, width), BF16)] + shard_gather_sems(1),
            [pltpu.VMEM((count, rows, inner), BF16), pltpu.VMEM((count, rows, both), BF16)],
            [pltpu.VMEM((count, rows, width), BF16), held] + ring_sems(count),
            [pltpu.VMEM((count, rows, width), BF16), held] + ring_sems(count),
            [pltpu.VMEM((width, both), BF16)] + shard_sum_scratch(shard_rows, both),
            [pltpu.VMEM((inner, width), BF16)] + shard_sum_scratch(piece, width),
        ]
        self.sizes = [len(group) for group in groups]
        self.scratch = sum(groups, [])

    def run(self, ring, ins, outs, scratch):
        normed, grad_out, w_out_rows = ins[:3]
        inner, piece = self.inner, self.piece
        groups, at = [], 0
        for size in self.sizes:
            groups.append(scratch[at : at + size])
            at += size
        (rows_all, *rows_sems), (w_in, *w_in_sems), (w_out, *w_out_sems) = groups[:3]
        hidden, grad_mid = groups[3]
        (out_part, out_held, *out_sems), (in_part, in_held, *in_sems) = groups[4:6]
        (grad_w_in, *grad_in_rest), (grad_w_out, *grad_out_rest) = groups[6:]
        count, tall = rows_all.shape[:2]
        width = rows_all.shape[2]

        def fill_in(shard, local_sem):
            if not self.aligned:
                return [pltpu.make_async_copy(ins[3], shard, local_sem.at[0])], ins[3]
            copies = []
            for i in range(2):
                for group in range(inner // piece):
                    at = i * (inner // piece) + group
                    start = pl.multiple_of((group * count + ring.ctx) * piece, piece)
                    copies.append(
                        pltpu.make_async_copy(
                            ins[3 + i].at[:, pl.ds(start, piece)],
                            shard.at[:, pl.ds(at * piece, piece)],
                            local_sem.at[at],
                        )
                    )
            return copies, None

        def fill_out(shard, local_sem):
            start = pl.multiple_of(ring.ctx * piece, piece)
            own = w_out_rows.at[pl.ds(start, piece)]
            return [pltpu.make_async_copy(own, shard, local_sem.at[0])], own

        def compute(slots):
            size = (slots.stop - slots.start) * tall

            def load(ref):
                return ref[slots].reshape(size, ref.shape[2])

            def store(ref, columns, value):
                ref[slots, :, columns] = value.astype(BF16).reshape(-1, tall, value.shape[1])

            tile = min(256, inner)

            @pl.loop(0, inner // tile)
            def _(index):
                def columns(start):
                    return pl.ds(pl.multiple_of(start + index * tile, tile), tile)

                gate = matmul(load(rows_all), w_in[:, columns(0)])
                up = matmul(load(rows_all), w_in[:, columns(inner)])
                grad_hidden = matmul_rows(load(grad_out), w_out[columns(0)])
                sig = jax.nn.sigmoid(gate)
                silu = gate * sig
                store(hidden, columns(0), silu * up)
                store(
                    grad_mid, columns(0), grad_hidden * up * (sig * (1.0 + gate * (1.0 - sig)))
                )
                store(grad_mid, columns(inner), grad_hidden * silu)

            wide = 256 if width % 256 == 0 else width

            @pl.loop(0, width // wide)
            def _(index):
                columns = pl.ds(pl.multiple_of(index * wide, wide), wide)
                store(in_part, columns, matmul_rows(load(grad_mid), w_in[columns]))
                store(out_part, columns, matmul(load(hidden), w_out[:, columns]))

        def weight_grads(left, right, grads):
            tile = 128 if left.shape[2] % 128 == 0 else left.shape[2]

            @pl.loop(0, left.shape[2] // tile)
            def _(index):
                columns = pl.ds(pl.multiple_of(index * tile, tile), tile)
                grads[columns] = weight_grad(
                    left[:, :, columns].reshape(count * tall, tile),
                    right[...].reshape(count * tall, right.shape[2]),
                ).astype(BF16)

        yield from together(
            ring_gather(ring, normed, rows_all, *rows_sems, False),
            shard_gather(ring, fill_in, w_in, *w_in_sems),
            shard_gather(ring, fill_out, w_out, *w_out_sems),
        )
        compute(slice(count - 1, count))
        sums = together(
            ring_sum(ring, in_part, in_held, outs[1], *in_sems, False),
            ring_sum(ring, out_part, out_held, outs[0], *out_sems, False),
        )
        for _ in range(RING_PIECES):
            next(sums)
        for pair in range(count // 2 - 1, 0, -1):
            compute(slice(2 * pair - 1, 2 * pair + 1))
            if pair == 2:
                for _ in range(RING_PIECES):
                    next(sums)
        compute(slice(0, 1))
        weight_grads(rows_all, grad_mid, grad_w_in)
        weight_grads(hidden, grad_out, grad_w_out)
        yield from together(
            sums,
            shard_sum(ring, grad_w_in, outs[2], *grad_in_rest),
            shard_sum(ring, grad_w_out, outs[3], *grad_out_rest),
        )


def small_sum_scratch(shape):
    count, shards = lax.axis_size("ctx"), lax.axis_size("fsdp")
    return [
        pltpu.VMEM((shards,) + shape, F32),
        pltpu.VMEM((count,) + shape, F32),
    ] + sems(shards - 1, shards - 1, count - 1, count - 1)


def small_sum(ring, small, total, near, far, near_send, near_recv, far_send, far_recv):
    siblings, peers = all_peers(ring)
    me, row = ring.fsdp, ring.ctx
    near[me] = small[...]
    first = [
        remote(small, near.at[me], near_send.at[i], near_recv.at[i], to)
        for i, to in enumerate(siblings)
    ]
    for copy in first:
        copy.start()
    yield from idle(RING_PIECES)
    for copy in first:
        copy.wait()
    far[row] = sum([near[i] for i in range(len(siblings) + 1)])
    second = [
        remote(far.at[row], far.at[row], far_send.at[i], far_recv.at[i], to)
        for i, to in enumerate(peers)
    ]
    for copy in second:
        copy.start()
    yield from idle(2 * RING_PIECES)
    for copy in second:
        copy.wait()
    total[...] = sum([far[i] for i in range(len(peers) + 1)])


class Attention:
    kinds = ()

    def __init__(self, qkv, decay, seg, own_heads):
        self.rows, self.heads = qkv.shape[0], own_heads
        self.dim = qkv.shape[1] // 3 // own_heads
        self.scaling = self.dim ** (-0.5)
        self.tall = min(256, self.rows)
        self.ins = [qkv, decay, decay.T, seg[:, None], seg[None, :]]

    def block(self, index):
        rows = slice(index * self.tall, (index + 1) * self.tall)
        return rows, (index + 1) * self.tall

    def allowed(self, rows, wide, seg_rows, seg_cols):
        shape = (self.tall, wide)
        here = lax.broadcasted_iota(jnp.int32, shape, 0) + rows.start
        there = lax.broadcasted_iota(jnp.int32, shape, 1)
        return (there <= here) & (seg_rows[rows] == seg_cols[:, :wide])

    def part(self, qkv, which, head, rows):
        start = (which * self.heads + head) * self.dim
        return qkv[rows, start : start + self.dim]

    def scores(self, refs, head, rows, wide, allowed):
        qkv, decay, decay_cols = refs[:3]
        queries = self.part(qkv, 0, head, rows)
        keys = self.part(qkv, 1, head, slice(0, wide))
        scores = matmul_rows(queries, keys) * self.scaling
        scores = scores + decay[rows, head : head + 1] - decay_cols[head : head + 1, :wide]
        return queries, keys, jnp.where(allowed, scores, NEGATIVE)


class AttentionForward(Attention):
    def __init__(self, qkv, decay, seg, own_heads):
        super().__init__(qkv, decay, seg, own_heads)
        self.in_specs = [VMEM] * 5
        self.outs = [
            jax.ShapeDtypeStruct((self.rows, own_heads * self.dim), F32),
            jax.ShapeDtypeStruct((self.rows, own_heads), F32),
        ]
        self.out_specs, self.scratch = [VMEM] * 2, []

    def run(self, ring, ins, outs, scratch):
        for index in range(self.rows // self.tall):
            rows, wide = self.block(index)
            allowed = self.allowed(rows, wide, *ins[3:])
            mixed, totals = [], []
            for head in range(self.heads):
                _, _, scores = self.scores(ins, head, rows, wide, allowed)
                row_max = jnp.max(scores, axis=1, keepdims=True)
                raised = jnp.exp(scores - row_max)
                row_total = jnp.sum(raised, axis=1, keepdims=True)
                probabilities = (raised * (1.0 / row_total)).astype(BF16)
                mixed.append(matmul(probabilities, self.part(ins[0], 2, head, slice(0, wide))))
                totals.append(row_max + jnp.log(row_total))
                if head < self.heads - 1:
                    yield
            outs[0][rows] = jnp.concatenate(mixed, axis=1)
            outs[1][rows] = jnp.concatenate(totals, axis=1)
            yield


def slow(walk, turns):
    for _ in walk:
        yield from idle(turns)


class Backward(Attention):
    kinds = ("all",)

    def __init__(self, qkv, decay, seg, own_heads, named):
        super().__init__(qkv, decay, seg, own_heads)
        self.names = list(named)
        hbm = ("gated", "grad_ffn_in", "grad_ffn_out")
        self.ins = self.ins + [named[name] for name in self.names]
        self.in_specs = [VMEM] * 5 + [ANYWHERE if name in hbm else VMEM for name in self.names]
        count, shards = lax.axis_size("ctx"), lax.axis_size("fsdp")
        tall, width = named["gated"].shape
        hidden = own_heads * self.dim
        self.main = 4 * hidden
        both = -(-(5 * hidden + own_heads) // 128) * 128
        ffn = [named["grad_ffn_in"], named["grad_ffn_out"]]
        shard_rows = width // shards
        self.outs = (
            [jax.ShapeDtypeStruct((tall, width), F32)]
            + [jax.ShapeDtypeStruct((count,) + grad.shape, BF16) for grad in ffn]
            + [jax.ShapeDtypeStruct((count, shard_rows, both), BF16)]
            + [jax.ShapeDtypeStruct((8, width), F32)]
        )
        self.out_specs = [VMEM] + [ANYWHERE] * 3 + [VMEM]
        ring = [pltpu.SemaphoreType.DMA] + ring_sems(count)
        groups = [
            [pltpu.VMEM((3, own_heads, self.rows, self.dim), F32)],
            [pltpu.VMEM((self.rows, 128), F32), pltpu.VMEM((8, self.rows), F32)],
            [pltpu.VMEM((self.rows, self.main + 128), BF16)],
            [pltpu.VMEM((count, tall, width), BF16)] + ring,
            [
                pltpu.VMEM((count, tall, width), BF16),
                pltpu.VMEM((2, count // 2, tall, width), BF16),
                pltpu.VMEM((tall, width), F32),
            ]
            + ring_sems(count),
            [pltpu.VMEM((width, both), BF16), pltpu.VMEM((shard_rows, both), BF16)]
            + shard_sum_scratch(shard_rows, both),
            ring,
            ring,
            ring,
            [pltpu.VMEM((8, width), F32)] + small_sum_scratch((8, width)),
        ]
        self.sizes = [len(group) for group in groups]
        self.scratch = sum(groups, [])

    def run(self, ring, ins, outs, scratch):
        groups, at = [], 0
        for size in self.sizes:
            groups.append(scratch[at : at + size])
            at += size
        named = dict(zip(self.names, ins[5:]))
        gated_all, *gated_sems = groups[3]
        rows_part, rows_held, rows_sum, *rows_sems = groups[4]
        grad_mixed = groups[2][0]
        grads_part, grads_sum, *grads_rest = groups[5]
        small, *small_rest = groups[9]
        count, tall, width = gated_all.shape

        def main():
            yield from together(
                self.attention(ins, named, *groups[0], *groups[1]),
                ring_gather(ring, named["gated"], gated_all, *gated_sems, True),
            )
            self.join(named, *groups[0], *groups[1], grad_mixed, small)
            block = 256 if width % 256 == 0 else width

            @pl.loop(0, width // block)
            def _(index):
                columns = pl.ds(pl.multiple_of(index * block, block), block)
                part = matmul_rows(grad_mixed[...], named["mixed_in"][columns])
                rows_part[:, :, columns] = part.astype(BF16).reshape(count, tall, block)

            yield from together(
                ring_sum(ring, rows_part, rows_held, rows_sum, *rows_sems, True),
                weights(),
            )

        def weights():
            yield from idle(RING_PIECES)
            self.weight_grads(named, gated_all, grad_mixed, grads_part)
            yield from shard_sum(ring, grads_part, grads_sum, *grads_rest)

        yield from together(
            main(),
            slow(ring_gather(ring, named["grad_ffn_in"], outs[1], *groups[6], True), 2),
            slow(ring_gather(ring, named["grad_ffn_out"], outs[2], *groups[7], True), 2),
        )
        self.norm_back(named, rows_sum, outs[0], small)
        yield from together(
            ring_gather(ring, grads_sum, outs[3], *groups[8], True),
            small_sum(ring, small, outs[4], *small_rest),
        )

    def attention(self, ins, named, grads, sums_rows, sums_columns):
        log_totals, grad_attn = named["log_totals"], named["grad_attn"]
        grad_q, grad_k, grad_v = [grads.at[i] for i in range(3)]
        blocks = self.rows // self.tall
        sums_columns[...] = jnp.zeros_like(sums_columns)
        pad = jnp.zeros((self.tall, 128 - self.heads), F32)
        for index in reversed(range(blocks)):
            rows, wide = self.block(index)
            allowed = self.allowed(rows, wide, *ins[3:5])
            own = slice(0, wide)
            row_sums = []
            for head in range(self.heads):
                queries, keys, scores = self.scores(ins, head, rows, wide, allowed)
                probabilities = jnp.exp(scores - log_totals[rows, head : head + 1])
                grad_part = grad_attn[rows, head * self.dim : (head + 1) * self.dim]
                grad_probs = matmul_rows(grad_part, self.part(ins[0], 2, head, own))
                row_inner = jnp.sum(probabilities * grad_probs, axis=1, keepdims=True)
                grad_scores = (probabilities * (grad_probs - row_inner)).astype(BF16)
                grad_q[head, rows] = matmul(grad_scores, keys) * self.scaling
                from_k = weight_grad(grad_scores, queries) * self.scaling
                from_v = weight_grad(probabilities.astype(BF16), grad_part)
                wide_sums = grad_scores.astype(F32)
                row_sums.append(jnp.sum(wide_sums, axis=1, keepdims=True))
                column_sums = jnp.sum(wide_sums, axis=0, keepdims=True)
                if index == blocks - 1:
                    grad_k[head], grad_v[head] = from_k, from_v
                    sums_columns[head : head + 1] = column_sums
                else:
                    grad_k[head, own] += from_k
                    grad_v[head, own] += from_v
                    sums_columns[head : head + 1, own] += column_sums
            sums_rows[rows] = jnp.concatenate(row_sums + [pad], axis=1)
            yield

    def join(self, named, grads, sums_rows, sums_columns, grad_mixed, small):
        for index in range(self.rows // self.tall):
            rows, _ = self.block(index)
            grad_mixed[rows, : self.main] = jnp.concatenate(
                [grads[i, head, rows].astype(BF16) for i in range(3) for head in range(self.heads)]
                + [named["grad_gatelog"][rows]],
                axis=1,
            )
        tall = 128
        here = lax.broadcasted_iota(jnp.int32, (tall, tall), 0)
        there = lax.broadcasted_iota(jnp.int32, (tall, tall), 1)
        wedge = (here <= there).astype(F32)
        later, bias = jnp.zeros((1, 8), F32), jnp.zeros((1, 8), F32)
        exact = dict(preferred_element_type=F32, precision=lax.Precision.HIGHEST)
        pad = jnp.zeros((tall, 120), BF16)
        for index in reversed(range(self.rows // tall)):
            rows = slice(index * tall, (index + 1) * tall)
            inside = jnp.dot(wedge, sums_rows[rows], **exact)[:, :8] - lax.dot_general(
                wedge, sums_columns[:, rows], (((1,), (1,)), ((), ())), **exact
            )
            logits = named["forget_logits"][rows]
            grad_logits = ((inside + later) * jax.nn.sigmoid(-logits)).astype(BF16)
            later = later + inside[:1]
            bias = bias + jnp.sum(grad_logits.astype(F32), axis=0, keepdims=True)
            grad_mixed[rows, self.main :] = jnp.concatenate([grad_logits, pad], axis=1)
        small[...] = named["small"][...]
        small[2:3] = sum(
            bias[:, head : head + 1] * named["places"][head : head + 1]
            for head in range(self.heads)
        )

    def weight_grads(self, named, gated_all, grad_mixed, parts):
        count, tall, width = gated_all.shape
        tile = 128
        hidden = named["grad_branch"].shape[1]
        tail = parts.shape[1] - self.main

        @pl.loop(0, width // tile)
        def _(index):
            columns = pl.ds(pl.multiple_of(index * tile, tile), tile)
            normed = named["normed"][:, :, columns].reshape(count * tall, tile)
            gated = gated_all[:, :, columns].reshape(count * tall, tile)
            parts[columns, : self.main] = weight_grad(normed, grad_mixed[:, : self.main]).astype(BF16)
            forget = weight_grad(normed, grad_mixed[:, self.main :])
            out = weight_grad(gated, named["grad_branch"][...])
            parts[columns, self.main :] = jnp.concatenate(
                [out, forget[:, : tail - hidden]], axis=1
            ).astype(BF16)

    def norm_back(self, named, rows_sum, grad_tokens, small):
        grad, normed = rows_sum[...], named["normed_one"][...]
        small[0:1] = jnp.sum(grad * normed, axis=0, keepdims=True)
        grad_normed = grad * named["gain_one"][...]
        inner = jnp.mean(grad_normed * normed, axis=1, keepdims=True)
        grad_tokens[...] = named["grad_middle"][...] + named["rstat_one"][...] * (
            grad_normed - normed * inner
        )


def running_sum(values):
    tall = 128 if values.shape[0] % 128 == 0 else values.shape[0]
    blocks = values.reshape(-1, tall, values.shape[1])
    wedge = jnp.tril(jnp.ones((tall, tall), F32))
    inside = jnp.einsum("st,btk->bsk", wedge, blocks, precision=lax.Precision.HIGHEST)
    totals = jnp.sum(blocks, axis=1)
    before = jnp.tril(jnp.ones((totals.shape[0],) * 2, F32), -1)
    before = jnp.sum(before[:, :, None] * totals[None], axis=1)
    return (inside + before[:, None]).reshape(values.shape)


def exchange(ident, name, *tasks):
    count = lax.axis_size("ctx")

    def take(refs, sizes):
        groups, at = [], 0
        for size in sizes:
            groups.append(refs[at : at + size])
            at += size
        return groups

    ins = [len(task.ins) for task in tasks]
    outs = [len(task.outs) for task in tasks]
    scratch = [len(task.scratch) for task in tasks]

    def kernel(*refs):
        ring = Ring(count)
        kinds = sum([task.kinds for task in tasks], ())
        peers = []
        if "all" in kinds:
            peers = sum(all_peers(ring), [])
        else:
            if "ring" in kinds:
                peers += [ring.device(1), ring.device(-1)]
            if "shard" in kinds:
                pair, others = shard_pair(ring, lax.axis_size("fsdp"))
                peers += [(ring.ctx, to) for to in [pair] + others]
        greet(peers)
        groups = [
            take(refs[: sum(ins)], ins),
            take(refs[sum(ins) : sum(ins) + sum(outs)], outs),
            take(refs[sum(ins) + sum(outs) :], scratch),
        ]
        for _ in together(*[task.run(ring, *parts) for task, *parts in zip(tasks, *groups)]):
            pass

    results = pl.pallas_call(
        kernel,
        out_shape=sum([task.outs for task in tasks], []),
        in_specs=sum([task.in_specs for task in tasks], []),
        out_specs=sum([task.out_specs for task in tasks], []),
        scratch_shapes=sum([task.scratch for task in tasks], []),
        compiler_params=pltpu.CompilerParams(
            collective_id=ident, has_side_effects=True, vmem_limit_bytes=58 * 2**20
        ),
        cost_estimate=pl.CostEstimate(flops=0, bytes_accessed=100_000_000, transcendentals=0),
        name=name,
    )(*sum([task.ins for task in tasks], []))
    return take(list(results), outs)


def flat(blocks):
    return blocks.reshape(-1, blocks.shape[-1])


def ffn_columns(blocks, n_fsdp):
    count, rows, both = blocks.shape
    width, piece = both // 2, both // 2 // n_fsdp
    steps = 4
    tall = rows // steps

    def kernel(block_ref, *outs):
        for j in range(count):
            for half in range(2):
                for group in range(n_fsdp):
                    start, to = half * width + group * piece, (group * count + j) * piece
                    outs[half][:, to : to + piece] = block_ref[j, :, start : start + piece].astype(F32)

    wide = jax.ShapeDtypeStruct((rows, width * count), F32)
    spec = pl.BlockSpec((tall, width * count), lambda i: (i, 0))
    return pl.pallas_call(
        kernel,
        out_shape=(wide, wide),
        grid=(steps,),
        in_specs=[pl.BlockSpec((count, tall, both), lambda i: (0, i, 0))],
        out_specs=(spec, spec),
        compiler_params=pltpu.CompilerParams(vmem_limit_bytes=40 * 2**20),
        cost_estimate=pl.CostEstimate(
            flops=0, bytes_accessed=rows * both * count * 6, transcendentals=0
        ),
        name="ffn_columns",
    )(blocks)


def head_columns(blocks, sizes, widths):
    count, rows, total = blocks.shape
    steps = 4
    tall = rows // steps
    starts = [sum(sizes[:i]) for i in range(len(sizes))]

    def kernel(block_ref, *outs):
        for start, size, out in zip(starts, sizes, outs):
            for i in range(0, count, 2):
                pair = jnp.concatenate(
                    [block_ref[i + k][:, start : start + size].astype(F32) for k in range(2)], axis=1
                )
                at = i * size
                keep = min(2 * size, out.shape[1] - at)
                if keep > 0:
                    out[:, at : at + keep] = pair[:, :keep]

    return pl.pallas_call(
        kernel,
        out_shape=tuple(jax.ShapeDtypeStruct((rows, w), F32) for w in widths),
        grid=(steps,),
        in_specs=[pl.BlockSpec((count, tall, total), lambda i: (0, i, 0))],
        out_specs=tuple(pl.BlockSpec((tall, w), lambda i: (i, 0)) for w in widths),
        compiler_params=pltpu.CompilerParams(vmem_limit_bytes=40 * 2**20),
        cost_estimate=pl.CostEstimate(
            flops=0, bytes_accessed=count * rows * total * 6, transcendentals=0
        ),
        name="head_columns",
    )(blocks)


def rows_to_columns(value):
    return lax.all_to_all(value, "ctx", split_axis=1, concat_axis=0, tiled=True)


def columns_to_rows(value):
    return lax.all_to_all(value, "ctx", split_axis=0, concat_axis=1, tiled=True)


def shards(
    tokens,
    segments,
    gain_attn,
    w_query,
    w_key,
    w_value,
    w_forget,
    forget_bias,
    w_outgate,
    w_out,
    gain_ffn,
    w_gate,
    w_up,
    w_down,
    cotangent,
):
    n_ctx, me = lax.axis_size("ctx"), lax.axis_index("ctx")
    n_fsdp = lax.axis_size("fsdp")
    tok_rows, width = tokens.shape[1:]
    seq_rows = tok_rows * n_ctx
    n_heads = forget_bias.shape[0]
    head_dim = width // n_heads
    own_heads = -(-n_heads // n_ctx)
    own_width = own_heads * head_dim
    padded = own_width * n_ctx
    ffn_rows = w_down.shape[0]
    ffn_piece = ffn_rows // n_ctx
    ffn_width = ffn_piece * n_fsdp
    shard_rows = w_query.shape[0]

    def widen(value, size):
        return jnp.pad(value, ((0, 0), (0, size - value.shape[1])))

    def own_columns(weight, size):
        return lax.dynamic_slice_in_dim(widen(weight, size * n_ctx), me * size, size, 1)

    def own_ffn(weight):
        return [
            lax.dynamic_slice_in_dim(weight, (group * n_ctx + me) * ffn_piece, ffn_piece, 1)
            for group in range(n_fsdp)
        ]

    mixed_shard = jnp.concatenate(
        [own_columns(w, own_width) for w in (w_query, w_key, w_value, w_outgate)]
        + [widen(own_columns(w_forget, own_heads), 128)],
        axis=1,
    )
    bias_own = lax.dynamic_slice_in_dim(
        jnp.pad(forget_bias, (0, own_heads * n_ctx - n_heads)), me * own_heads, own_heads, 0
    )
    bias_own = jnp.pad(bias_own, (0, 8 - own_heads))

    seg = segments[0]
    inputs = tokens[0].astype(F32)
    gain_one = gain_attn.astype(F32)
    normed_one, rstat_one = rms_stats(inputs)
    (normed,), (mixed_in,) = exchange(
        0,
        "gather_start",
        RingGather((normed_one * gain_one).astype(BF16), absolute=True),
        ShardGather(mixed_shard),
    )
    normed_rows = flat(normed)
    normed_rows, out_shard = lax.optimization_barrier((normed_rows, w_out))
    full_out = lax.all_gather(out_shard, "fsdp", axis=0, tiled=True)

    split = [own_width * i for i in range(5)]
    qkv = matmul(normed_rows, mixed_in[:, : split[3]]).astype(BF16)
    mixed = matmul(normed_rows, mixed_in[:, split[3] :])
    gate_value = jax.nn.sigmoid(mixed[:, :own_width])
    forget_logits = mixed[:, own_width : own_width + 8] + bias_own
    decay = running_sum(jax.nn.log_sigmoid(forget_logits))

    (grad_out_low,), (attended, log_totals) = exchange(
        5,
        "attend",
        RingGather(cotangent[0]),
        AttentionForward(qkv, decay, seg, own_heads),
    )
    gated = columns_to_rows((attended * gate_value).astype(BF16))[:, :width]

    middle = inputs + matmul(gated, full_out)
    gain_two = gain_ffn.astype(F32)
    normed_two_f, rstat_two = rms_stats(middle)
    w_in = [w_gate, w_up]
    if ffn_piece % 128 != 0:
        w_in = [jnp.concatenate(own_ffn(w_gate) + own_ffn(w_up), axis=1)]
    ((out_sum, grad_normed_two, grad_ffn_in, grad_ffn_out),) = exchange(
        1,
        "ffn",
        Ffn((normed_two_f * gain_two).astype(BF16), grad_out_low, w_in, w_down, ffn_piece),
    )
    output = middle + out_sum
    back_two, grad_gain_two = norm_back(grad_normed_two, normed_two_f, rstat_two, gain_two)
    grad_middle = cotangent[0].astype(F32) + back_two

    grad_branch_low = grad_middle.astype(BF16)
    grad_gated = matmul_rows(grad_branch_low, full_out).astype(BF16)
    grad_gated = rows_to_columns(widen(grad_gated, padded)).astype(F32)
    grad_branch_own = rows_to_columns(widen(grad_branch_low, padded))
    grad_attn_low = (grad_gated * gate_value).astype(BF16)
    grad_gatelog_low = (grad_gated * attended * (gate_value * (1.0 - gate_value))).astype(BF16)

    spots = jnp.arange(own_heads, dtype=jnp.int32)[:, None] + me * own_heads
    places = (spots == jnp.arange(width, dtype=jnp.int32)[None, :]).astype(F32)
    ((grad_inputs, spread_ffn_in, spread_ffn_out, spread_attn, small),) = exchange(
        2,
        "backward",
        Backward(
            qkv,
            decay,
            seg,
            own_heads,
            {
                "log_totals": log_totals,
                "grad_attn": grad_attn_low,
                "grad_gatelog": grad_gatelog_low,
                "forget_logits": forget_logits,
                "grad_branch": grad_branch_own,
                "gated": gated,
                "grad_ffn_in": grad_ffn_in,
                "grad_ffn_out": grad_ffn_out,
                "normed": normed,
                "mixed_in": mixed_in,
                "normed_one": normed_one,
                "rstat_one": rstat_one,
                "gain_one": gain_one[None],
                "grad_middle": grad_middle,
                "places": places,
                "small": jnp.pad(grad_gain_two[None], ((1, 6), (0, 0))),
            },
        ),
    )
    sizes = [own_width] * 5 + [own_heads]
    if ffn_piece % 128 == 0:
        grad_gate, grad_up = ffn_columns(spread_ffn_in, n_fsdp)
    else:
        whole = spread_ffn_in.reshape(n_ctx, shard_rows, 2, n_fsdp, ffn_piece)
        whole = jnp.transpose(whole, (2, 1, 3, 0, 4)).reshape(2, shard_rows, -1).astype(F32)
        grad_gate, grad_up = whole[0], whole[1]
    grad_weights = head_columns(spread_attn, sizes, [width] * 5 + [n_heads])
    return (
        output.astype(BF16)[None],
        grad_inputs[None],
        small[0],
        grad_weights[0],
        grad_weights[1],
        grad_weights[2],
        grad_weights[5],
        small[2, :n_heads],
        grad_weights[3],
        grad_weights[4],
        small[1],
        grad_gate,
        grad_up,
        spread_ffn_out.reshape(ffn_rows, width).astype(F32),
    )


def solution(mesh):
    rows, blocks = P("fsdp", None), P("fsdp", "ctx", None)
    return jax.shard_map(
        shards,
        mesh=mesh,
        in_specs=(blocks, rows, P())
        + (rows,) * 4
        + (P(), rows, rows, P(), rows, rows, rows, blocks),
        out_specs=(blocks, blocks, P())
        + (rows,) * 4
        + (P(), rows, rows, P(), rows, rows, rows),
        check_vma=False,
    )
```

```python
import jax
import jax.numpy as jnp
from jax import lax
from jax.experimental import pallas as pl
from jax.experimental.pallas import tpu as pltpu
from jax.sharding import PartitionSpec as P

EPSILON = 1e-06
NEGATIVE = -1e30
BF16, F32 = jnp.bfloat16, jnp.float32


def matmul(left, right):
    return jnp.dot(left, right, preferred_element_type=F32)


def matmul_rows(left, right):
    return lax.dot_general(left, right, (((1,), (1,)), ((), ())), preferred_element_type=F32)


def weight_grad(left, right):
    return lax.dot_general(left, right, (((0,), (0,)), ((), ())), preferred_element_type=F32)


def rms_stats(values):
    rstat = lax.rsqrt(jnp.mean(values * values, axis=-1, keepdims=True) + EPSILON)
    return (values * rstat, rstat)


MESH = pl.DeviceIdType.MESH
RING_PIECES = 4


def ring_place(ctx, count):
    odd = ctx % 2
    return ctx // 2 + odd * (count - 1 - 2 * (ctx // 2))


def ring_index(place, count):
    back = place // (count // 2)
    return 2 * place + back * (2 * (count - 1 - place) + 1 - 2 * place)


class Ring:
    def __init__(self, count):
        self.count, self.half = count, count // 2
        self.ctx, self.fsdp = lax.axis_index("ctx"), lax.axis_index("fsdp")
        self.place = ring_place(self.ctx, count)

    def at(self, offset):
        return ring_index((self.place + offset + self.count) % self.count, self.count)

    def device(self, offset):
        return (self.at(offset), self.fsdp)


def greet(devices):
    barrier = pltpu.get_barrier_semaphore()
    for device in devices:
        pl.semaphore_signal(barrier, inc=1, device_id=device, device_id_type=MESH)
    pl.semaphore_wait(barrier, len(devices))


def remote(src, dst, send, recv, device):
    return pltpu.make_async_remote_copy(
        src_ref=src, dst_ref=dst, send_sem=send, recv_sem=recv, device_id=device, device_id_type=MESH
    )


def carried(step, half, pieces, way):
    if step < half - 1:
        return range(pieces)
    return range(pieces // 2) if way == 0 else range(pieces // 2, pieces)


def ring_slot(ring, offset, absolute):
    if absolute:
        return ring.at(offset)
    if abs(offset) == ring.half:
        return ring.count - 1
    return 2 * offset - 1 if offset > 0 else -2 * offset


def ring_gather(ring, own, full, local_sem, send_sem, recv_sem, absolute, pieces=RING_PIECES):
    rows = own.shape[0] // pieces

    def part(k):
        return pl.ds(k * rows, rows)

    def slot(offset):
        return ring_slot(ring, offset, absolute)

    keep = pltpu.make_async_copy(own, full.at[slot(0)], local_sem)
    keep.start()
    copies = {}
    for step in range(ring.half):
        for k in range(pieces):
            for way, sign in ((0, 1), (1, -1)):
                if k not in carried(step, ring.half, pieces, way):
                    continue
                if step > 0:
                    copies[step - 1, k, way].wait_recv()
                src = own.at[part(k)] if step == 0 else full.at[slot(-sign * step), part(k)]
                to = slot(-sign * step if absolute else -sign * (step + 1))
                copy = remote(
                    src,
                    full.at[to, part(k)],
                    send_sem.at[step, k, way],
                    recv_sem.at[step, k, way],
                    ring.device(sign),
                )
                copy.start()
                copies[step, k, way] = copy
            yield
    for (step, k, way), copy in copies.items():
        if step == ring.half - 1 or k not in carried(step + 1, ring.half, pieces, way):
            copy.wait_recv()
    for copy in copies.values():
        copy.wait_send()
    keep.wait()


def ring_sum(ring, parts, held, total, send_sem, recv_sem, absolute, pieces=RING_PIECES):
    rows = parts.shape[1] // pieces

    def place(offset):
        return ring_slot(ring, offset, absolute)

    def part(k):
        return pl.ds(k * rows, rows)

    copies = {}
    for step in range(ring.half):
        for k in range(pieces):
            for way, sign in ((0, 1), (1, -1)):
                if k not in carried(ring.half - 1 - step, ring.half, pieces, way):
                    continue
                block = place(sign * (ring.half - step))
                src = parts.at[block, part(k)]
                if (step - 1, k, way) in copies:
                    copies[step - 1, k, way].wait_recv()
                    slot = held.at[way, step - 1, part(k)]
                    slot[...] = (slot[...].astype(F32) + src[...].astype(F32)).astype(BF16)
                    src = slot
                copy = remote(
                    src,
                    held.at[way, step, part(k)],
                    send_sem.at[step, k, way],
                    recv_sem.at[step, k, way],
                    ring.device(sign),
                )
                copy.start()
                copies[step, k, way] = copy
            yield
    last = ring.half - 1
    for k in range(pieces):
        for way in range(2):
            copies[last, k, way].wait_recv()
        total[part(k)] = (
            parts[place(0), part(k)].astype(F32)
            + held[0, last, part(k)].astype(F32)
            + held[1, last, part(k)].astype(F32)
        )
    for copy in copies.values():
        copy.wait_send()


def ring_sems(count, pieces=RING_PIECES):
    shape = (count // 2, pieces, 2)
    return [pltpu.SemaphoreType.DMA(shape), pltpu.SemaphoreType.DMA(shape)]


def sems(*counts):
    return [pltpu.SemaphoreType.DMA((max(count, 1),)) for count in counts]


ANYWHERE, VMEM = pl.BlockSpec(memory_space=pl.ANY), pl.BlockSpec(memory_space=pltpu.VMEM)


def shard_pair(ring, shards):
    me = ring.fsdp
    pair = me + 1 - 2 * (me % 2)
    return pair, [(me + 2 * hop) % shards for hop in range(1, shards // 2)]


def all_peers(ring):
    count, shards = lax.axis_size("ctx"), lax.axis_size("fsdp")
    siblings = [(ring.ctx, (ring.fsdp + hop) % shards) for hop in range(1, shards)]
    return siblings, [((ring.ctx + hop) % count, ring.fsdp) for hop in range(1, count)]


def idle(turns):
    for _ in range(turns):
        yield


def together(*walks):
    walks = list(walks)
    while walks:
        walks = [walk for walk in walks if next(walk, walks) is None]
        yield


def shard_gather(ring, fill, whole, local_sem, send_sem, recv_sem):
    shards, me = lax.axis_size("fsdp"), ring.fsdp
    rows = whole.shape[0] // shards
    pair, others = shard_pair(ring, shards)

    def shard(index):
        return whole.at[pl.ds(pl.multiple_of(index * rows, rows), rows)]

    local, source = fill(shard(me), local_sem)
    for copy in local:
        copy.start()
    yield
    if source is None:
        for copy in local:
            copy.wait()
    sent = shard(me) if source is None else source
    copies = [
        remote(sent, shard(me), send_sem.at[i], recv_sem.at[i], (ring.ctx, to))
        for i, to in enumerate([pair] + others)
    ]
    for copy in copies:
        copy.start()
    yield from idle(3 * RING_PIECES)
    passed = []
    for i in range(1, len(copies)):
        copies[i].wait_recv()
        origin = (me - 2 * i + shards) % shards
        at = shards // 2 - 1 + i
        copy = remote(
            shard(origin), shard(origin), send_sem.at[at], recv_sem.at[at], (ring.ctx, pair)
        )
        copy.start()
        passed.append(copy)
    yield from idle(2)
    copies[0].wait_recv()
    for copy in passed:
        copy.wait_recv()
    for copy in copies + passed:
        copy.wait_send()
    if source is not None:
        for copy in local:
            copy.wait()


def shard_gather_sems(parts):
    shards = lax.axis_size("fsdp")
    return sems(parts, shards - 1, shards - 1)


def shard_sum(ring, parts, total, near, far, near_send, near_recv, far_send, far_recv):
    shards, me = lax.axis_size("fsdp"), ring.fsdp
    half, core, chip = shards // 2, me % 2, me // 2
    pair, others = shard_pair(ring, shards)
    rows = parts.shape[0] // shards

    def shard(index):
        return pl.ds(pl.multiple_of(index * rows, rows), rows)

    first = [
        remote(
            parts.at[shard(2 * i + 1 - core)],
            near.at[i],
            near_send.at[i],
            near_recv.at[i],
            (ring.ctx, pair),
        )
        for i in range(half)
    ]
    for copy in first:
        copy.start()
    yield from idle(2)
    for copy in first:
        copy.wait_recv()
    second = []
    for hop in range(1, half):
        to = (chip + hop) % half
        near[to] = (near[to].astype(F32) + parts[shard(2 * to + core)].astype(F32)).astype(BF16)
        copy = remote(
            near.at[to],
            far.at[hop - 1],
            far_send.at[hop - 1],
            far_recv.at[hop - 1],
            (ring.ctx, others[hop - 1]),
        )
        copy.start()
        second.append(copy)
    yield from idle(3 * RING_PIECES)
    sums = parts[shard(me)].astype(F32) + near[chip].astype(F32)
    for hop, copy in enumerate(second):
        copy.wait_recv()
        sums = sums + far[hop].astype(F32)
    total[...] = sums.astype(BF16)
    for copy in first + second:
        copy.wait_send()


def shard_sum_scratch(rows, width):
    half = lax.axis_size("fsdp") // 2
    return [
        pltpu.VMEM((half, rows, width), BF16),
        pltpu.VMEM((max(half - 1, 1), rows, width), BF16),
    ] + sems(half, half, half - 1, half - 1)


class Ffn:
    kinds = ("ring", "shard")

    def __init__(self, tokens, gated, full_out, gain, grad_out, w_in, w_out, piece):
        count, shards = lax.axis_size("ctx"), lax.axis_size("fsdp")
        rows, width = tokens.shape
        self.aligned = len(w_in) == 2
        self.piece, self.inner = piece, piece * shards
        inner, both = self.inner, 2 * self.inner
        shard_rows = width // shards
        self.ins = [grad_out, tokens, gated, full_out, gain, w_out] + list(w_in)
        self.in_specs = [VMEM] * 5 + [ANYWHERE] * (1 + len(w_in))
        self.outs = [
            jax.ShapeDtypeStruct((rows, width), BF16),
            jax.ShapeDtypeStruct((rows, width), F32),
            jax.ShapeDtypeStruct((rows, width), F32),
            jax.ShapeDtypeStruct((rows, 1), F32),
            jax.ShapeDtypeStruct((shard_rows, both), BF16),
            jax.ShapeDtypeStruct((piece, width), BF16),
        ]
        self.out_specs = [VMEM] * 6
        held = pltpu.VMEM((2, count // 2, rows, width), BF16)
        groups = [
            [pltpu.VMEM((count, rows, width), BF16), pltpu.SemaphoreType.DMA] + ring_sems(count),
            [pltpu.VMEM((width, both), BF16)] + shard_gather_sems(2 * shards),
            [pltpu.VMEM((inner, width), BF16)] + shard_gather_sems(1),
            [pltpu.VMEM((count, rows, inner), BF16), pltpu.VMEM((count, rows, both), BF16)],
            [pltpu.VMEM((count, rows, width), BF16), held] + ring_sems(count),
            [pltpu.VMEM((count, rows, width), BF16), held] + ring_sems(count),
            [pltpu.VMEM((width, both), BF16)] + shard_sum_scratch(shard_rows, both),
            [pltpu.VMEM((inner, width), BF16)] + shard_sum_scratch(piece, width),
            [
                pltpu.VMEM((rows, width), F32),
                pltpu.VMEM((rows, width), BF16),
                pltpu.VMEM((rows, width), F32),
            ],
        ]
        self.sizes = [len(group) for group in groups]
        self.scratch = sum(groups, [])

    def run(self, ring, ins, outs, scratch):
        grad_out, tokens, gated, full_out, gain, w_out_rows = ins[:6]
        w_in_rows = ins[6:]
        inner, piece = self.inner, self.piece
        groups = split_refs(scratch, self.sizes)
        (rows_all, *rows_sems), (w_in, *w_in_sems), (w_out, *w_out_sems) = groups[:3]
        hidden, grad_mid = groups[3]
        (out_part, out_held, *out_sems), (in_part, in_held, *in_sems) = groups[4:6]
        (grad_w_in, *grad_in_rest), (grad_w_out, *grad_out_rest) = groups[6:8]
        middle, normed, out_sum = groups[8]
        count, tall = rows_all.shape[:2]
        width = rows_all.shape[2]

        def fill_in(shard, local_sem):
            if not self.aligned:
                return [pltpu.make_async_copy(w_in_rows[0], shard, local_sem.at[0])], w_in_rows[0]
            copies = []
            for i in range(2):
                for group in range(inner // piece):
                    at = i * (inner // piece) + group
                    start = pl.multiple_of((group * count + ring.ctx) * piece, piece)
                    copies.append(
                        pltpu.make_async_copy(
                            w_in_rows[i].at[:, pl.ds(start, piece)],
                            shard.at[:, pl.ds(at * piece, piece)],
                            local_sem.at[at],
                        )
                    )
            return copies, None

        def fill_out(shard, local_sem):
            start = pl.multiple_of(ring.ctx * piece, piece)
            own = w_out_rows.at[pl.ds(start, piece)]
            return [pltpu.make_async_copy(own, shard, local_sem.at[0])], own

        def compute(slots):
            size = (slots.stop - slots.start) * tall

            def load(ref):
                return ref[slots].reshape(size, ref.shape[2])

            def store(ref, columns, value):
                ref[slots, :, columns] = value.astype(BF16).reshape(-1, tall, value.shape[1])

            tile = min(256, inner)

            @pl.loop(0, inner // tile)
            def _(index):
                def columns(start):
                    return pl.ds(pl.multiple_of(start + index * tile, tile), tile)

                gate = matmul(load(rows_all), w_in[:, columns(0)])
                up = matmul(load(rows_all), w_in[:, columns(inner)])
                grad_hidden = matmul_rows(load(grad_out), w_out[columns(0)])
                sig = jax.nn.sigmoid(gate)
                silu = gate * sig
                store(hidden, columns(0), silu * up)
                store(
                    grad_mid, columns(0), grad_hidden * up * (sig * (1.0 + gate * (1.0 - sig)))
                )
                store(grad_mid, columns(inner), grad_hidden * silu)

            wide = 256 if width % 256 == 0 else width

            @pl.loop(0, width // wide)
            def _(index):
                columns = pl.ds(pl.multiple_of(index * wide, wide), wide)
                store(in_part, columns, matmul_rows(load(grad_mid), w_in[columns]))
                store(out_part, columns, matmul(load(hidden), w_out[:, columns]))

        def weight_grads(left, right, grads):
            tile = 128 if left.shape[2] % 128 == 0 else left.shape[2]

            @pl.loop(0, left.shape[2] // tile)
            def _(index):
                columns = pl.ds(pl.multiple_of(index * tile, tile), tile)
                grads[columns] = weight_grad(
                    left[:, :, columns].reshape(count * tall, tile),
                    right[...].reshape(count * tall, right.shape[2]),
                ).astype(BF16)

        def first():
            block = 256 if width % 256 == 0 else width

            @pl.loop(0, width // block)
            def _(index):
                columns = pl.ds(pl.multiple_of(index * block, block), block)
                middle[:, columns] = tokens[:, columns].astype(F32) + matmul(
                    gated[:, :width], full_out[:, columns]
                )

            value = middle[...]
            rstat = lax.rsqrt(jnp.mean(value * value, axis=1, keepdims=True) + EPSILON)
            outs[2][...] = value * rstat
            outs[3][...] = rstat
            normed[...] = (outs[2][...] * gain[...]).astype(BF16)

        weights = together(
            shard_gather(ring, fill_in, w_in, *w_in_sems),
            shard_gather(ring, fill_out, w_out, *w_out_sems),
        )
        next(weights)
        first()
        yield from together(weights, ring_gather(ring, normed, rows_all, *rows_sems, False))
        compute(slice(count - 1, count))
        sums = together(
            ring_sum(ring, in_part, in_held, outs[1], *in_sems, False),
            ring_sum(ring, out_part, out_held, out_sum, *out_sems, False),
        )
        for _ in range(RING_PIECES):
            next(sums)
        for pair in range(count // 2 - 1, 0, -1):
            compute(slice(2 * pair - 1, 2 * pair + 1))
            if pair == 2:
                for _ in range(RING_PIECES):
                    next(sums)
        compute(slice(0, 1))
        weight_grads(rows_all, grad_mid, grad_w_in)
        weight_grads(hidden, grad_out, grad_w_out)
        yield from together(
            sums,
            shard_sum(ring, grad_w_in, outs[4], *grad_in_rest),
            shard_sum(ring, grad_w_out, outs[5], *grad_out_rest),
        )
        outs[0][...] = (middle[...] + out_sum[...]).astype(BF16)


def swap_sems(count):
    return sems(count - 1, count - 1)


def swap(ring, sent, received, send_sem, recv_sem):
    _, peers = all_peers(ring)
    copies = [
        remote(sent.at[to[0]], received.at[ring.ctx], send_sem.at[i], recv_sem.at[i], to)
        for i, to in enumerate(peers)
    ]
    for copy in copies:
        copy.start()
    received[ring.ctx] = sent[ring.ctx]
    yield from idle(RING_PIECES)
    for copy in copies:
        copy.wait()


def small_sum_scratch(shape):
    count, shards = lax.axis_size("ctx"), lax.axis_size("fsdp")
    return [
        pltpu.VMEM((shards,) + shape, F32),
        pltpu.VMEM((count,) + shape, F32),
    ] + sems(shards - 1, shards - 1, count - 1, count - 1)


def small_sum(ring, small, total, near, far, near_send, near_recv, far_send, far_recv):
    siblings, peers = all_peers(ring)
    me, row = ring.fsdp, ring.ctx
    near[me] = small[...]
    first = [
        remote(small, near.at[me], near_send.at[i], near_recv.at[i], to)
        for i, to in enumerate(siblings)
    ]
    for copy in first:
        copy.start()
    yield from idle(RING_PIECES)
    for copy in first:
        copy.wait()
    far[row] = sum([near[i] for i in range(len(siblings) + 1)])
    second = [
        remote(far.at[row], far.at[row], far_send.at[i], far_recv.at[i], to)
        for i, to in enumerate(peers)
    ]
    for copy in second:
        copy.start()
    yield from idle(2 * RING_PIECES)
    for copy in second:
        copy.wait()
    total[...] = sum([far[i] for i in range(len(peers) + 1)])


class Attention:
    kinds = ("all",)

    def __init__(self, rows, heads, dim):
        self.rows, self.heads, self.dim = rows, heads, dim
        self.scaling = dim ** (-0.5)
        self.tall = min(256 if rows <= 1024 else 128, rows)

    def block(self, index):
        rows = slice(index * self.tall, (index + 1) * self.tall)
        return rows, (index + 1) * self.tall

    def allowed(self, rows, wide, info, across):
        shape = (self.tall, wide)
        here = lax.broadcasted_iota(jnp.int32, shape, 0) + rows.start
        there = lax.broadcasted_iota(jnp.int32, shape, 1)
        return (there <= here) & (info[rows, 24:25] == across[8:9, :wide])

    def part(self, qkv, which, head, rows):
        start = (which * self.heads + head) * self.dim
        return qkv[rows, start : start + self.dim]

    def scores(self, qkv, info, across, head, rows, wide, allowed):
        queries = self.part(qkv, 0, head, rows)
        keys = self.part(qkv, 1, head, slice(0, wide))
        scores = matmul_rows(queries, keys) * self.scaling
        scores = scores + info[rows, head : head + 1] - across[head : head + 1, :wide]
        return queries, keys, jnp.where(allowed, scores, NEGATIVE)


def split_refs(refs, sizes):
    groups, at = [], 0
    for size in sizes:
        groups.append(list(refs[at : at + size]))
        at += size
    return groups


EXACT = dict(preferred_element_type=F32, precision=lax.Precision.HIGHEST)


class Forward(Attention):
    def __init__(self, normed, cotangent, mixed_shard, w_out, bias, seg, heads, dim):
        count, shards = lax.axis_size("ctx"), lax.axis_size("fsdp")
        tall, width = normed.shape
        rows = tall * count
        super().__init__(rows, heads, dim)
        hidden = heads * dim
        self.hidden = hidden
        documents = seg.astype(F32)
        self.ins = [normed, cotangent, mixed_shard, w_out, bias]
        self.in_specs = [ANYWHERE] * 4 + [VMEM] * 3
        self.ins += [documents[:, None], documents[None, :]]
        everyone = jax.ShapeDtypeStruct((count, tall, width), BF16)
        self.outs = [
            everyone,
            everyone,
            jax.ShapeDtypeStruct((width, mixed_shard.shape[1]), BF16),
            jax.ShapeDtypeStruct((width, width), BF16),
            jax.ShapeDtypeStruct((rows, 3 * hidden), BF16),
            jax.ShapeDtypeStruct((rows, hidden), F32),
            jax.ShapeDtypeStruct((rows, hidden), F32),
            jax.ShapeDtypeStruct((rows, 128), F32),
            jax.ShapeDtypeStruct((16, rows), F32),
            jax.ShapeDtypeStruct((tall, count * hidden), BF16),
        ]
        self.out_specs = [VMEM, ANYWHERE, VMEM, ANYWHERE] + [VMEM] * 6
        ring = [pltpu.SemaphoreType.DMA] + ring_sems(count)
        swapped = pltpu.VMEM((count, tall, hidden), BF16)
        groups = [
            ring,
            ring,
            shard_gather_sems(1),
            shard_gather_sems(1),
            [swapped, swapped] + swap_sems(count),
        ]
        self.sizes = [len(group) for group in groups]
        self.scratch = sum(groups, [])

    def run(self, ring, ins, outs, scratch):
        rows_sems, cotangent_sems, mixed_sems, out_sems, swapping = split_refs(scratch, self.sizes)
        own, cotangent, mixed_shard, w_out, bias, seg_rows, seg_columns = ins
        normed, grad_out, mixed_in, full_out, qkv, attended, gate, info, across, gated = outs
        sent, received = swapping[:2]
        count, tall, _ = normed.shape

        def filled_from(source):
            def fill(shard, local_sem):
                return [pltpu.make_async_copy(source, shard, local_sem.at[0])], source

            return fill

        def later(turns, walk):
            yield from idle(turns)
            yield from walk

        def main():
            yield from together(
                ring_gather(ring, own, normed, *rows_sems, True),
                shard_gather(ring, filled_from(mixed_shard), mixed_in, *mixed_sems),
            )
            self.project(normed, mixed_in, bias, qkv, gate, info)
            self.decay(info, across, seg_rows, seg_columns)
            yield
            yield from self.attend(qkv, info, across, attended)
            for i in range(count):
                rows = slice(i * tall, (i + 1) * tall)
                sent[i] = (attended[rows] * gate[rows]).astype(BF16)
            yield from swap(ring, *swapping)
            gated[...] = jnp.concatenate([received[i] for i in range(count)], axis=1)

        turns = count // 2 * RING_PIECES
        yield from together(
            main(),
            later(turns - 1, ring_gather(ring, cotangent, grad_out, *cotangent_sems, False)),
            later(turns // 2, shard_gather(ring, filled_from(w_out), full_out, *out_sems)),
        )

    def project(self, normed, mixed_in, bias, qkv, gate, info):
        count, tall, width = normed.shape
        pair = 2 if count % 2 == 0 else 1
        hidden = self.hidden

        @pl.loop(0, count // pair)
        def _(index):
            block = normed[pl.ds(index * pair, pair)].reshape(pair * tall, width)
            rows = pl.ds(pl.multiple_of(index * pair * tall, pair * tall), pair * tall)
            mixed = matmul(block, mixed_in[...])
            qkv[rows] = mixed[:, : 3 * hidden].astype(BF16)
            gate[rows] = jax.nn.sigmoid(mixed[:, 3 * hidden : 4 * hidden])
            info[rows] = mixed[:, 4 * hidden : 4 * hidden + 128]
            info[rows, 8:16] = info[rows, 0:8] + bias[...]

    def decay(self, info, across, seg_rows, seg_columns):
        tall = 128
        here = lax.broadcasted_iota(jnp.int32, (tall, tall), 0)
        there = lax.broadcasted_iota(jnp.int32, (tall, tall), 1)
        wedge = (there <= here).astype(F32)
        before = jnp.zeros((1, 8), F32)
        pad = jnp.zeros((tall, 120), F32)
        for index in range(self.rows // tall):
            rows = slice(index * tall, (index + 1) * tall)
            logs = jax.nn.log_sigmoid(info[rows, 8:16])
            sums = jnp.dot(wedge, jnp.concatenate([logs, pad], axis=1), **EXACT)[:, :8] + before
            before = sums[tall - 1 :]
            info[rows, 0:8] = sums
            across[0:8, rows] = jnp.concatenate([sums, pad], axis=1).T[:8]
        info[:, 24:25] = seg_rows[...]
        across[8:9] = seg_columns[...]

    def attend(self, qkv, info, across, attended):
        for index in range(self.rows // self.tall):
            rows, wide = self.block(index)
            allowed = self.allowed(rows, wide, info, across)
            mixed = []
            for head in range(self.heads):
                _, _, scores = self.scores(qkv, info, across, head, rows, wide, allowed)
                row_max = jnp.max(scores, axis=1, keepdims=True)
                raised = jnp.exp(scores - row_max)
                row_total = jnp.sum(raised, axis=1, keepdims=True)
                probabilities = (raised * (1.0 / row_total)).astype(BF16)
                mixed.append(matmul(probabilities, self.part(qkv, 2, head, slice(0, wide))))
                info[rows, 16 + head : 17 + head] = row_max + jnp.log(row_total)
                if head < self.heads - 1:
                    yield
            attended[rows] = jnp.concatenate(mixed, axis=1)
            yield


def slow(walk, turns):
    for _ in walk:
        yield from idle(turns)


class Backward(Attention):
    def __init__(self, own_heads, named):
        rows = named["qkv"].shape[0]
        super().__init__(rows, own_heads, named["qkv"].shape[1] // 3 // own_heads)
        self.names = list(named)
        hbm = ("gated", "grad_ffn_in", "grad_ffn_out")
        self.ins = [named[name] for name in self.names]
        self.in_specs = [ANYWHERE if name in hbm else VMEM for name in self.names]
        count, shards = lax.axis_size("ctx"), lax.axis_size("fsdp")
        tall, width = named["gated"].shape
        hidden = own_heads * self.dim
        self.main = 4 * hidden
        both = -(-(5 * hidden + own_heads) // 128) * 128
        ffn = [named["grad_ffn_in"], named["grad_ffn_out"]]
        shard_rows = width // shards
        swapped = pltpu.VMEM((count, tall, 2 * hidden), BF16)
        heads = pltpu.VMEM((self.rows, hidden), BF16)
        self.outs = (
            [jax.ShapeDtypeStruct((tall, width), F32)]
            + [jax.ShapeDtypeStruct((count,) + grad.shape, BF16) for grad in ffn]
            + [jax.ShapeDtypeStruct((count, shard_rows, both), BF16)]
            + [jax.ShapeDtypeStruct((8, width), F32)]
        )
        self.out_specs = [VMEM] + [ANYWHERE] * 3 + [VMEM]
        ring = [pltpu.SemaphoreType.DMA] + ring_sems(count)
        groups = [
            [pltpu.VMEM((3, own_heads, self.rows, self.dim), F32)],
            [pltpu.VMEM((self.rows, 128), F32), pltpu.VMEM((8, self.rows), F32)],
            [pltpu.VMEM((self.rows, self.main + 128), BF16)],
            [pltpu.VMEM((count, tall, width), BF16)] + ring,
            [
                pltpu.VMEM((count, tall, width), BF16),
                pltpu.VMEM((2, count // 2, tall, width), BF16),
                pltpu.VMEM((tall, width), F32),
            ]
            + ring_sems(count),
            [pltpu.VMEM((width, both), BF16), pltpu.VMEM((shard_rows, both), BF16)]
            + shard_sum_scratch(shard_rows, both),
            ring,
            ring,
            ring,
            [pltpu.VMEM((8, width), F32)] + small_sum_scratch((8, width)),
            [pltpu.VMEM((tall, width), F32), pltpu.VMEM((tall, count * hidden), BF16)],
            [swapped, swapped] + swap_sems(count),
            [heads, heads, heads],
        ]
        self.sizes = [len(group) for group in groups]
        self.scratch = sum(groups, [])

    def run(self, ring, ins, outs, scratch):
        groups = split_refs(scratch, self.sizes)
        named = dict(zip(self.names, ins))
        gated_all, *gated_sems = groups[3]
        rows_part, rows_held, rows_sum, *rows_sems = groups[4]
        grad_mixed = groups[2][0]
        grads_part, grads_sum, *grads_rest = groups[5]
        small, *small_rest = groups[9]
        named["grad_middle"], grad_gated = groups[10]
        named["grad_attn"], named["grad_gatelog"], named["grad_branch"] = groups[12]
        count, tall, width = gated_all.shape

        def main():
            yield
            self.branch_back(named, grad_gated, groups[11][0], small)
            yield from together(
                swap(ring, *groups[11]),
                idle(RING_PIECES),
            )
            self.gate_back(named, groups[11][1])
            yield from together(
                self.attention(named, *groups[0], *groups[1]),
                ring_gather(ring, named["gated"], gated_all, *gated_sems, True),
            )
            self.join(named, *groups[0], *groups[1], grad_mixed, small)
            block = 256 if width % 256 == 0 else width

            @pl.loop(0, width // block)
            def _(index):
                columns = pl.ds(pl.multiple_of(index * block, block), block)
                part = matmul_rows(grad_mixed[...], named["mixed_in"][columns])
                rows_part[:, :, columns] = part.astype(BF16).reshape(count, tall, block)

            yield from together(
                ring_sum(ring, rows_part, rows_held, rows_sum, *rows_sems, True),
                weights(),
            )

        def weights():
            yield from idle(RING_PIECES)
            self.weight_grads(named, gated_all, grad_mixed, grads_part)
            yield from shard_sum(ring, grads_part, grads_sum, *grads_rest)

        yield from together(
            slow(ring_gather(ring, named["grad_ffn_in"], outs[1], *groups[6], True), 2),
            slow(ring_gather(ring, named["grad_ffn_out"], outs[2], *groups[7], True), 2),
            main(),
        )
        self.norm_back(named, rows_sum, outs[0], small)
        yield from together(
            ring_gather(ring, grads_sum, outs[3], *groups[8], True),
            small_sum(ring, small, outs[4], *small_rest),
        )

    def branch_back(self, named, grad_gated, sent, small):
        grad, normed = named["grad_normed_two"][...], named["normed_two"][...]
        small[...] = jnp.zeros_like(small)
        small[1:2] = jnp.sum(grad * normed, axis=0, keepdims=True)
        grad_normed = grad * named["gain_two"][...]
        inner = jnp.mean(grad_normed * normed, axis=1, keepdims=True)
        named["grad_middle"][...] = named["cotangent"][...].astype(F32) + named["rstat_two"][...] * (
            grad_normed - normed * inner
        )
        count, tall, both = sent.shape
        width = grad.shape[1]
        block = 256 if width % 256 == 0 else width
        if grad_gated.shape[1] > width:
            grad_gated[...] = jnp.zeros_like(grad_gated)

        @pl.loop(0, width // block)
        def _(index):
            columns = pl.ds(pl.multiple_of(index * block, block), block)
            low = named["grad_middle"][...].astype(BF16)
            grad_gated[:, columns] = matmul_rows(low, named["full_out"][columns]).astype(BF16)

        low = named["grad_middle"][...].astype(BF16)
        if grad_gated.shape[1] > width:
            low = jnp.concatenate(
                [low, jnp.zeros((tall, grad_gated.shape[1] - width), BF16)], axis=1
            )
        for i in range(count):
            own = slice(i * both // 2, (i + 1) * both // 2)
            sent[i] = jnp.concatenate([grad_gated[:, own], low[:, own]], axis=1)

    def gate_back(self, named, received):
        count, tall, both = received.shape
        for i in range(count):
            rows = slice(i * tall, (i + 1) * tall)
            grad = received[i, :, : both // 2].astype(F32)
            gate = named["gate_value"][rows]
            named["grad_attn"][rows] = (grad * gate).astype(BF16)
            named["grad_gatelog"][rows] = (
                grad * named["attended"][rows] * (gate * (1.0 - gate))
            ).astype(BF16)
            named["grad_branch"][rows] = received[i, :, both // 2 :]

    def attention(self, named, grads, sums_rows, sums_columns):
        qkv, info, across, grad_attn = [
            named[name] for name in ("qkv", "info", "across", "grad_attn")
        ]
        grad_q, grad_k, grad_v = [grads.at[i] for i in range(3)]
        blocks = self.rows // self.tall
        sums_columns[...] = jnp.zeros_like(sums_columns)
        pad = jnp.zeros((self.tall, 128 - self.heads), F32)
        for index in reversed(range(blocks)):
            rows, wide = self.block(index)
            allowed = self.allowed(rows, wide, info, across)
            own = slice(0, wide)
            row_sums = []
            for head in range(self.heads):
                queries, keys, scores = self.scores(
                    qkv, info, across, head, rows, wide, allowed
                )
                probabilities = jnp.exp(scores - info[rows, 16 + head : 17 + head])
                grad_part = grad_attn[rows, head * self.dim : (head + 1) * self.dim]
                grad_probs = matmul_rows(grad_part, self.part(qkv, 2, head, own))
                row_inner = jnp.sum(probabilities * grad_probs, axis=1, keepdims=True)
                grad_scores = (probabilities * (grad_probs - row_inner)).astype(BF16)
                grad_q[head, rows] = matmul(grad_scores, keys) * self.scaling
                from_k = weight_grad(grad_scores, queries) * self.scaling
                from_v = weight_grad(probabilities.astype(BF16), grad_part)
                wide_sums = grad_scores.astype(F32)
                row_sums.append(jnp.sum(wide_sums, axis=1, keepdims=True))
                column_sums = jnp.sum(wide_sums, axis=0, keepdims=True)
                if index == blocks - 1:
                    grad_k[head], grad_v[head] = from_k, from_v
                    sums_columns[head : head + 1] = column_sums
                else:
                    grad_k[head, own] += from_k
                    grad_v[head, own] += from_v
                    sums_columns[head : head + 1, own] += column_sums
            sums_rows[rows] = jnp.concatenate(row_sums + [pad], axis=1)
            yield

    def join(self, named, grads, sums_rows, sums_columns, grad_mixed, small):
        for index in range(self.rows // self.tall):
            rows, _ = self.block(index)
            grad_mixed[rows, : self.main] = jnp.concatenate(
                [grads[i, head, rows].astype(BF16) for i in range(3) for head in range(self.heads)]
                + [named["grad_gatelog"][rows]],
                axis=1,
            )
        tall = 128
        here = lax.broadcasted_iota(jnp.int32, (tall, tall), 0)
        there = lax.broadcasted_iota(jnp.int32, (tall, tall), 1)
        wedge = (here <= there).astype(F32)
        later, bias = jnp.zeros((1, 8), F32), jnp.zeros((1, 8), F32)
        pad = jnp.zeros((tall, 120), BF16)
        for index in reversed(range(self.rows // tall)):
            rows = slice(index * tall, (index + 1) * tall)
            inside = jnp.dot(wedge, sums_rows[rows], **EXACT)[:, :8] - lax.dot_general(
                wedge, sums_columns[:, rows], (((1,), (1,)), ((), ())), **EXACT
            )
            logits = named["info"][rows, 8:16]
            grad_logits = ((inside + later) * jax.nn.sigmoid(-logits)).astype(BF16)
            later = later + inside[:1]
            bias = bias + jnp.sum(grad_logits.astype(F32), axis=0, keepdims=True)
            grad_mixed[rows, self.main :] = jnp.concatenate([grad_logits, pad], axis=1)
        small[2:3] = sum(
            bias[:, head : head + 1] * named["places"][head : head + 1]
            for head in range(self.heads)
        )

    def weight_grads(self, named, gated_all, grad_mixed, parts):
        count, tall, width = gated_all.shape
        tile = 128
        hidden = named["grad_branch"].shape[1]
        tail = parts.shape[1] - self.main

        @pl.loop(0, width // tile)
        def _(index):
            columns = pl.ds(pl.multiple_of(index * tile, tile), tile)
            normed = named["normed"][:, :, columns].reshape(count * tall, tile)
            gated = gated_all[:, :, columns].reshape(count * tall, tile)
            parts[columns, : self.main] = weight_grad(normed, grad_mixed[:, : self.main]).astype(BF16)
            forget = weight_grad(normed, grad_mixed[:, self.main :])
            out = weight_grad(gated, named["grad_branch"][...])
            parts[columns, self.main :] = jnp.concatenate(
                [out, forget[:, : tail - hidden]], axis=1
            ).astype(BF16)

    def norm_back(self, named, rows_sum, grad_tokens, small):
        grad, normed = rows_sum[...], named["normed_one"][...]
        small[0:1] = jnp.sum(grad * normed, axis=0, keepdims=True)
        grad_normed = grad * named["gain_one"][...]
        inner = jnp.mean(grad_normed * normed, axis=1, keepdims=True)
        grad_tokens[...] = named["grad_middle"][...] + named["rstat_one"][...] * (
            grad_normed - normed * inner
        )


def exchange(ident, name, *tasks):
    count = lax.axis_size("ctx")

    def take(refs, sizes):
        groups, at = [], 0
        for size in sizes:
            groups.append(refs[at : at + size])
            at += size
        return groups

    ins = [len(task.ins) for task in tasks]
    outs = [len(task.outs) for task in tasks]
    scratch = [len(task.scratch) for task in tasks]

    def kernel(*refs):
        ring = Ring(count)
        kinds = sum([task.kinds for task in tasks], ())
        peers = []
        if "all" in kinds:
            peers = sum(all_peers(ring), [])
        else:
            if "ring" in kinds:
                peers += [ring.device(1), ring.device(-1)]
            if "shard" in kinds:
                pair, others = shard_pair(ring, lax.axis_size("fsdp"))
                peers += [(ring.ctx, to) for to in [pair] + others]
        greet(peers)
        groups = [
            take(refs[: sum(ins)], ins),
            take(refs[sum(ins) : sum(ins) + sum(outs)], outs),
            take(refs[sum(ins) + sum(outs) :], scratch),
        ]
        for _ in together(*[task.run(ring, *parts) for task, *parts in zip(tasks, *groups)]):
            pass

    results = pl.pallas_call(
        kernel,
        out_shape=sum([task.outs for task in tasks], []),
        in_specs=sum([task.in_specs for task in tasks], []),
        out_specs=sum([task.out_specs for task in tasks], []),
        scratch_shapes=sum([task.scratch for task in tasks], []),
        compiler_params=pltpu.CompilerParams(
            collective_id=ident, has_side_effects=True, vmem_limit_bytes=62 * 2**20
        ),
        cost_estimate=pl.CostEstimate(flops=0, bytes_accessed=100_000_000, transcendentals=0),
        name=name,
    )(*sum([task.ins for task in tasks], []))
    return take(list(results), outs)


def flat(blocks):
    return blocks.reshape(-1, blocks.shape[-1])


def ffn_columns(blocks, n_fsdp):
    count, rows, both = blocks.shape
    width, piece = both // 2, both // 2 // n_fsdp
    steps = 4
    tall = rows // steps

    def kernel(block_ref, *outs):
        for j in range(count):
            for half in range(2):
                for group in range(n_fsdp):
                    start, to = half * width + group * piece, (group * count + j) * piece
                    outs[half][:, to : to + piece] = block_ref[j, :, start : start + piece].astype(F32)

    wide = jax.ShapeDtypeStruct((rows, width * count), F32)
    spec = pl.BlockSpec((tall, width * count), lambda i: (i, 0))
    return pl.pallas_call(
        kernel,
        out_shape=(wide, wide),
        grid=(steps,),
        in_specs=[pl.BlockSpec((count, tall, both), lambda i: (0, i, 0))],
        out_specs=(spec, spec),
        compiler_params=pltpu.CompilerParams(vmem_limit_bytes=40 * 2**20),
        cost_estimate=pl.CostEstimate(
            flops=0, bytes_accessed=rows * both * count * 6, transcendentals=0
        ),
        name="ffn_columns",
    )(blocks)


def head_columns(blocks, sizes, widths):
    count, rows, total = blocks.shape
    steps = 4
    tall = rows // steps
    starts = [sum(sizes[:i]) for i in range(len(sizes))]

    def kernel(block_ref, *outs):
        for start, size, out in zip(starts, sizes, outs):
            for i in range(0, count, 2):
                pair = jnp.concatenate(
                    [block_ref[i + k][:, start : start + size].astype(F32) for k in range(2)], axis=1
                )
                at = i * size
                keep = min(2 * size, out.shape[1] - at)
                if keep > 0:
                    out[:, at : at + keep] = pair[:, :keep]

    return pl.pallas_call(
        kernel,
        out_shape=tuple(jax.ShapeDtypeStruct((rows, w), F32) for w in widths),
        grid=(steps,),
        in_specs=[pl.BlockSpec((count, tall, total), lambda i: (0, i, 0))],
        out_specs=tuple(pl.BlockSpec((tall, w), lambda i: (i, 0)) for w in widths),
        compiler_params=pltpu.CompilerParams(vmem_limit_bytes=40 * 2**20),
        cost_estimate=pl.CostEstimate(
            flops=0, bytes_accessed=count * rows * total * 6, transcendentals=0
        ),
        name="head_columns",
    )(blocks)


def shards(
    tokens,
    segments,
    gain_attn,
    w_query,
    w_key,
    w_value,
    w_forget,
    forget_bias,
    w_outgate,
    w_out,
    gain_ffn,
    w_gate,
    w_up,
    w_down,
    cotangent,
):
    n_ctx, me = lax.axis_size("ctx"), lax.axis_index("ctx")
    n_fsdp = lax.axis_size("fsdp")
    tok_rows, width = tokens.shape[1:]
    seq_rows = tok_rows * n_ctx
    n_heads = forget_bias.shape[0]
    head_dim = width // n_heads
    own_heads = -(-n_heads // n_ctx)
    own_width = own_heads * head_dim
    padded = own_width * n_ctx
    ffn_rows = w_down.shape[0]
    ffn_piece = ffn_rows // n_ctx
    ffn_width = ffn_piece * n_fsdp
    shard_rows = w_query.shape[0]

    def widen(value, size):
        return jnp.pad(value, ((0, 0), (0, size - value.shape[1])))

    def own_columns(weight, size):
        return lax.dynamic_slice_in_dim(widen(weight, size * n_ctx), me * size, size, 1)

    def own_ffn(weight):
        return [
            lax.dynamic_slice_in_dim(weight, (group * n_ctx + me) * ffn_piece, ffn_piece, 1)
            for group in range(n_fsdp)
        ]

    mixed_shard = jnp.concatenate(
        [own_columns(w, own_width) for w in (w_query, w_key, w_value, w_outgate)]
        + [widen(own_columns(w_forget, own_heads), 128)],
        axis=1,
    )
    bias_own = lax.dynamic_slice_in_dim(
        jnp.pad(forget_bias, (0, own_heads * n_ctx - n_heads)), me * own_heads, own_heads, 0
    )
    bias_own = jnp.pad(bias_own, (0, 8 - own_heads))

    seg = segments[0]
    inputs = tokens[0].astype(F32)
    gain_one = gain_attn.astype(F32)
    normed_one, rstat_one = rms_stats(inputs)
    (
        (
            normed,
            grad_out_low,
            mixed_in,
            full_out,
            qkv,
            attended,
            gate_value,
            info,
            across,
            gated,
        ),
    ) = exchange(
        0,
        "forward",
        Forward(
            (normed_one * gain_one).astype(BF16),
            cotangent[0],
            mixed_shard,
            w_out,
            bias_own[None],
            segments[0],
            own_heads,
            head_dim,
        ),
    )
    gain_two = gain_ffn.astype(F32)[None]
    w_in = [w_gate, w_up]
    if ffn_piece % 128 != 0:
        w_in = [jnp.concatenate(own_ffn(w_gate) + own_ffn(w_up), axis=1)]
    ((output, grad_normed_two, normed_two, rstat_two, grad_ffn_in, grad_ffn_out),) = exchange(
        1,
        "ffn",
        Ffn(tokens[0], gated, full_out, gain_two, grad_out_low, w_in, w_down, ffn_piece),
    )
    spots = jnp.arange(own_heads, dtype=jnp.int32)[:, None] + me * own_heads
    places = (spots == jnp.arange(width, dtype=jnp.int32)[None, :]).astype(F32)
    ((grad_inputs, spread_ffn_in, spread_ffn_out, spread_attn, small),) = exchange(
        2,
        "backward",
        Backward(
            own_heads,
            {
                "qkv": qkv,
                "info": info,
                "across": across,
                "attended": attended,
                "gate_value": gate_value,
                "grad_normed_two": grad_normed_two,
                "normed_two": normed_two,
                "rstat_two": rstat_two,
                "gain_two": gain_two,
                "cotangent": cotangent[0],
                "full_out": full_out,
                "gated": gated[:, :width],
                "grad_ffn_in": grad_ffn_in,
                "grad_ffn_out": grad_ffn_out,
                "normed": normed,
                "mixed_in": mixed_in,
                "normed_one": normed_one,
                "rstat_one": rstat_one,
                "gain_one": gain_one[None],
                "places": places,
            },
        ),
    )
    sizes = [own_width] * 5 + [own_heads]
    if ffn_piece % 128 == 0:
        grad_gate, grad_up = ffn_columns(spread_ffn_in, n_fsdp)
    else:
        whole = spread_ffn_in.reshape(n_ctx, shard_rows, 2, n_fsdp, ffn_piece)
        whole = jnp.transpose(whole, (2, 1, 3, 0, 4)).reshape(2, shard_rows, -1).astype(F32)
        grad_gate, grad_up = whole[0], whole[1]
    grad_weights = head_columns(spread_attn, sizes, [width] * 5 + [n_heads])
    return (
        output[None],
        grad_inputs[None],
        small[0],
        grad_weights[0],
        grad_weights[1],
        grad_weights[2],
        grad_weights[5],
        small[2, :n_heads],
        grad_weights[3],
        grad_weights[4],
        small[1],
        grad_gate,
        grad_up,
        spread_ffn_out.reshape(ffn_rows, width).astype(F32),
    )


def solution(mesh):
    rows, blocks = P("fsdp", None), P("fsdp", "ctx", None)
    return jax.shard_map(
        shards,
        mesh=mesh,
        in_specs=(blocks, rows, P())
        + (rows,) * 4
        + (P(), rows, rows, P(), rows, rows, rows, blocks),
        out_specs=(blocks, blocks, P())
        + (rows,) * 4
        + (P(), rows, rows, P(), rows, rows, rows),
        check_vma=False,
    )
```

```python
import jax
import jax.numpy as jnp
from jax import lax
from jax.experimental import pallas as pl
from jax.experimental.pallas import tpu as pltpu
from jax.sharding import PartitionSpec as P

EPSILON = 1e-06
NEGATIVE = -1e30
BF16, F32 = jnp.bfloat16, jnp.float32


def matmul(left, right):
    return jnp.dot(left, right, preferred_element_type=F32)


def matmul_rows(left, right):
    return lax.dot_general(left, right, (((1,), (1,)), ((), ())), preferred_element_type=F32)


def weight_grad(left, right):
    return lax.dot_general(left, right, (((0,), (0,)), ((), ())), preferred_element_type=F32)


def rms_stats(values):
    rstat = lax.rsqrt(jnp.mean(values * values, axis=-1, keepdims=True) + EPSILON)
    return (values * rstat, rstat)


MESH = pl.DeviceIdType.MESH
RING_PIECES = 4


def ring_place(ctx, count):
    odd = ctx % 2
    return ctx // 2 + odd * (count - 1 - 2 * (ctx // 2))


def ring_index(place, count):
    back = place // (count // 2)
    return 2 * place + back * (2 * (count - 1 - place) + 1 - 2 * place)


class Ring:
    def __init__(self, count):
        self.count, self.half = count, count // 2
        self.ctx, self.fsdp = lax.axis_index("ctx"), lax.axis_index("fsdp")
        self.place = ring_place(self.ctx, count)

    def at(self, offset):
        return ring_index((self.place + offset + self.count) % self.count, self.count)

    def device(self, offset):
        return (self.at(offset), self.fsdp)


def greet(devices):
    barrier = pltpu.get_barrier_semaphore()
    for device in devices:
        pl.semaphore_signal(barrier, inc=1, device_id=device, device_id_type=MESH)
    pl.semaphore_wait(barrier, len(devices))


def remote(src, dst, send, recv, device):
    return pltpu.make_async_remote_copy(
        src_ref=src, dst_ref=dst, send_sem=send, recv_sem=recv, device_id=device, device_id_type=MESH
    )


def carried(step, half, pieces, way):
    if step < half - 1:
        return range(pieces)
    return range(pieces // 2) if way == 0 else range(pieces // 2, pieces)


def ring_slot(ring, offset, absolute):
    if absolute:
        return ring.at(offset)
    if abs(offset) == ring.half:
        return ring.count - 1
    return 2 * offset - 1 if offset > 0 else -2 * offset


def ring_gather(ring, own, full, local_sem, send_sem, recv_sem, absolute, pieces=RING_PIECES):
    rows = own.shape[0] // pieces

    def part(k):
        return pl.ds(k * rows, rows)

    def slot(offset):
        return ring_slot(ring, offset, absolute)

    keep = pltpu.make_async_copy(own, full.at[slot(0)], local_sem)
    keep.start()
    copies = {}
    for step in range(ring.half):
        for k in range(pieces):
            for way, sign in ((0, 1), (1, -1)):
                if step > 0:
                    copies[step - 1, k, way].wait_recv()
                if k not in carried(step, ring.half, pieces, way):
                    continue
                src = own.at[part(k)] if step == 0 else full.at[slot(-sign * step), part(k)]
                to = slot(-sign * step if absolute else -sign * (step + 1))
                copy = remote(
                    src,
                    full.at[to, part(k)],
                    send_sem.at[step, k, way],
                    recv_sem.at[step, k, way],
                    ring.device(sign),
                )
                copy.start()
                copies[step, k, way] = copy
            yield
    for (step, _, _), copy in copies.items():
        if step == ring.half - 1:
            copy.wait_recv()
    for copy in copies.values():
        copy.wait_send()
    keep.wait()


def ring_sum(
    ring, parts, held, total, send_sem, recv_sem, absolute, ahead=False, pieces=RING_PIECES
):
    rows = parts.shape[1] // pieces

    def place(offset):
        return ring_slot(ring, offset, absolute)

    def part(k):
        return pl.ds(k * rows, rows)

    copies = {}

    def send(step, k, way, sign):
        src = parts.at[place(sign * (ring.half - step)), part(k)]
        if (step - 1, k, way) in copies:
            copies[step - 1, k, way].wait_recv()
            slot = held.at[way, step - 1, part(k)]
            slot[...] = (slot[...].astype(F32) + src[...].astype(F32)).astype(BF16)
            src = slot
        copy = remote(
            src,
            held.at[way, step, part(k)],
            send_sem.at[step, k, way],
            recv_sem.at[step, k, way],
            ring.device(sign),
        )
        copy.start()
        copies[step, k, way] = copy

    def farthest(k, way):
        return k in carried(ring.half - 1, ring.half, pieces, way)

    for step in ([None] if ahead else []) + list(range(ring.half)):
        for k in range(pieces):
            for way, sign in ((0, 1), (1, -1)):
                if step is None and not farthest(k, way):
                    send(1, k, way, sign)
                elif step == 0 and farthest(k, way):
                    send(0, k, way, sign)
                elif step == 1 and (farthest(k, way) or not ahead):
                    send(1, k, way, sign)
                elif step is not None and step > 1:
                    send(step, k, way, sign)
            yield
    last = ring.half - 1
    for k in range(pieces):
        for way in range(2):
            copies[last, k, way].wait_recv()
        total[part(k)] = (
            parts[place(0), part(k)].astype(F32)
            + held[0, last, part(k)].astype(F32)
            + held[1, last, part(k)].astype(F32)
        )
    for copy in copies.values():
        copy.wait_send()


def ring_sems(count, pieces=RING_PIECES):
    shape = (count // 2, pieces, 2)
    return [pltpu.SemaphoreType.DMA(shape), pltpu.SemaphoreType.DMA(shape)]


def sems(*counts):
    return [pltpu.SemaphoreType.DMA((max(count, 1),)) for count in counts]


ANYWHERE, VMEM = pl.BlockSpec(memory_space=pl.ANY), pl.BlockSpec(memory_space=pltpu.VMEM)


def shard_pair(ring, shards):
    me = ring.fsdp
    pair = me + 1 - 2 * (me % 2)
    return pair, [(me + 2 * hop) % shards for hop in range(1, shards // 2)]


def all_peers(ring):
    count, shards = lax.axis_size("ctx"), lax.axis_size("fsdp")
    siblings = [(ring.ctx, (ring.fsdp + hop) % shards) for hop in range(1, shards)]
    return siblings, [((ring.ctx + hop) % count, ring.fsdp) for hop in range(1, count)]


def idle(turns):
    for _ in range(turns):
        yield


def together(*walks):
    walks = list(walks)
    while walks:
        walks = [walk for walk in walks if next(walk, walks) is None]
        yield


def shard_gather(ring, fill, whole, local_sem, send_sem, recv_sem, turns=3 * RING_PIECES):
    shards, me = lax.axis_size("fsdp"), ring.fsdp
    rows = whole.shape[0] // shards
    pair, others = shard_pair(ring, shards)

    def shard(index):
        return whole.at[pl.ds(pl.multiple_of(index * rows, rows), rows)]

    local, source = fill(shard(me), local_sem)
    for copy in local:
        copy.start()
    yield
    if source is None:
        for copy in local:
            copy.wait()
    sent = shard(me) if source is None else source
    copies = [
        remote(sent, shard(me), send_sem.at[i], recv_sem.at[i], (ring.ctx, to))
        for i, to in enumerate([pair] + others)
    ]
    for copy in copies:
        copy.start()
    yield from idle(turns)
    passed = []
    for i in range(1, len(copies)):
        copies[i].wait_recv()
        origin = (me - 2 * i + shards) % shards
        at = shards // 2 - 1 + i
        copy = remote(
            shard(origin), shard(origin), send_sem.at[at], recv_sem.at[at], (ring.ctx, pair)
        )
        copy.start()
        passed.append(copy)
    yield from idle(2)
    copies[0].wait_recv()
    for copy in passed:
        copy.wait_recv()
    for copy in copies + passed:
        copy.wait_send()
    if source is not None:
        for copy in local:
            copy.wait()


def shard_gather_sems(parts):
    shards = lax.axis_size("fsdp")
    return sems(parts, shards - 1, shards - 1)


def shard_sum(ring, parts, total, near, far, near_send, near_recv, far_send, far_recv):
    shards, me = lax.axis_size("fsdp"), ring.fsdp
    half, core, chip = shards // 2, me % 2, me // 2
    pair, others = shard_pair(ring, shards)
    rows = parts.shape[0] // shards

    def shard(index):
        return pl.ds(pl.multiple_of(index * rows, rows), rows)

    first = [
        remote(
            parts.at[shard(2 * i + 1 - core)],
            near.at[i],
            near_send.at[i],
            near_recv.at[i],
            (ring.ctx, pair),
        )
        for i in range(half)
    ]
    for copy in first:
        copy.start()
    yield from idle(2)
    for copy in first:
        copy.wait_recv()
    second = []
    for hop in range(1, half):
        to = (chip + hop) % half
        near[to] = (near[to].astype(F32) + parts[shard(2 * to + core)].astype(F32)).astype(BF16)
        copy = remote(
            near.at[to],
            far.at[hop - 1],
            far_send.at[hop - 1],
            far_recv.at[hop - 1],
            (ring.ctx, others[hop - 1]),
        )
        copy.start()
        second.append(copy)
    yield from idle(3 * RING_PIECES)
    sums = parts[shard(me)].astype(F32) + near[chip].astype(F32)
    for hop, copy in enumerate(second):
        copy.wait_recv()
        sums = sums + far[hop].astype(F32)
    total[...] = sums.astype(BF16)
    for copy in first + second:
        copy.wait_send()


def shard_sum_scratch(rows, width):
    half = lax.axis_size("fsdp") // 2
    return [
        pltpu.VMEM((half, rows, width), BF16),
        pltpu.VMEM((max(half - 1, 1), rows, width), BF16),
    ] + sems(half, half, half - 1, half - 1)


class Ffn:
    kinds = ("ring", "shard")

    def __init__(self, tokens, gated, full_out, gain, grad_out, w_in, w_out, piece):
        count, shards = lax.axis_size("ctx"), lax.axis_size("fsdp")
        rows, width = tokens.shape
        self.aligned = len(w_in) == 2
        self.piece, self.inner = piece, piece * shards
        inner, both = self.inner, 2 * self.inner
        shard_rows = width // shards
        self.ins = [grad_out, tokens, gated, full_out, gain, w_out] + list(w_in)
        self.in_specs = [ANYWHERE, VMEM, VMEM, ANYWHERE, VMEM] + [ANYWHERE] * (1 + len(w_in))
        self.late = Late([full_out, grad_out])
        self.outs = [
            jax.ShapeDtypeStruct((rows, width), BF16),
            jax.ShapeDtypeStruct((rows, width), F32),
            jax.ShapeDtypeStruct((rows, width), F32),
            jax.ShapeDtypeStruct((rows, 1), F32),
            jax.ShapeDtypeStruct((shard_rows, both), BF16),
            jax.ShapeDtypeStruct((piece, width), BF16),
        ]
        self.out_specs = [VMEM] * 6
        held = pltpu.VMEM((2, count // 2, rows, width), BF16)
        groups = [
            [pltpu.VMEM((count, rows, width), BF16), pltpu.SemaphoreType.DMA] + ring_sems(count),
            [pltpu.VMEM((width, both), BF16)] + shard_gather_sems(2 * shards),
            [pltpu.VMEM((inner, width), BF16)] + shard_gather_sems(1),
            [pltpu.VMEM((count, rows, inner), BF16), pltpu.VMEM((count, rows, both), BF16)],
            [pltpu.VMEM((count, rows, width), BF16), held] + ring_sems(count),
            [pltpu.VMEM((count, rows, width), BF16), held] + ring_sems(count),
            [pltpu.VMEM((width, both), BF16)] + shard_sum_scratch(shard_rows, both),
            [pltpu.VMEM((inner, width), BF16)] + shard_sum_scratch(piece, width),
            [
                pltpu.VMEM((rows, width), F32),
                pltpu.VMEM((rows, width), BF16),
                pltpu.VMEM((rows, width), F32),
            ],
            self.late.scratch,
        ]
        self.sizes = [len(group) for group in groups]
        self.scratch = sum(groups, [])

    def run(self, ring, ins, outs, scratch):
        _, tokens, gated, _, gain, w_out_rows = ins[:6]
        w_in_rows = ins[6:]
        inner, piece = self.inner, self.piece
        groups = split_refs(scratch, self.sizes)
        late = self.late.start([ins[3], ins[0]], groups[9])
        full_out, grad_out = late.held
        (rows_all, *rows_sems), (w_in, *w_in_sems), (w_out, *w_out_sems) = groups[:3]
        hidden, grad_mid = groups[3]
        (out_part, out_held, *out_sems), (in_part, in_held, *in_sems) = groups[4:6]
        (grad_w_in, *grad_in_rest), (grad_w_out, *grad_out_rest) = groups[6:8]
        middle, normed, out_sum = groups[8]
        count, tall = rows_all.shape[:2]
        width = rows_all.shape[2]

        def fill_in(shard, local_sem):
            if not self.aligned:
                return [pltpu.make_async_copy(w_in_rows[0], shard, local_sem.at[0])], w_in_rows[0]
            copies = []
            for i in range(2):
                for group in range(inner // piece):
                    at = i * (inner // piece) + group
                    start = pl.multiple_of((group * count + ring.ctx) * piece, piece)
                    copies.append(
                        pltpu.make_async_copy(
                            w_in_rows[i].at[:, pl.ds(start, piece)],
                            shard.at[:, pl.ds(at * piece, piece)],
                            local_sem.at[at],
                        )
                    )
            return copies, None

        def fill_out(shard, local_sem):
            start = pl.multiple_of(ring.ctx * piece, piece)
            own = w_out_rows.at[pl.ds(start, piece)]
            return [pltpu.make_async_copy(own, shard, local_sem.at[0])], own

        def compute(slots):
            size = (slots.stop - slots.start) * tall

            def load(ref):
                return ref[slots].reshape(size, ref.shape[2])

            def store(ref, columns, value):
                ref[slots, :, columns] = value.astype(BF16).reshape(-1, tall, value.shape[1])

            tile = min(256, inner)

            @pl.loop(0, inner // tile)
            def _(index):
                def columns(start):
                    return pl.ds(pl.multiple_of(start + index * tile, tile), tile)

                gate = matmul(load(rows_all), w_in[:, columns(0)])
                up = matmul(load(rows_all), w_in[:, columns(inner)])
                grad_hidden = matmul_rows(load(grad_out), w_out[columns(0)])
                sig = jax.nn.sigmoid(gate)
                silu = gate * sig
                store(hidden, columns(0), silu * up)
                store(
                    grad_mid, columns(0), grad_hidden * up * (sig * (1.0 + gate * (1.0 - sig)))
                )
                store(grad_mid, columns(inner), grad_hidden * silu)

            wide = 256 if width % 256 == 0 else width

            @pl.loop(0, width // wide)
            def _(index):
                columns = pl.ds(pl.multiple_of(index * wide, wide), wide)
                store(in_part, columns, matmul_rows(load(grad_mid), w_in[columns]))
                store(out_part, columns, matmul(load(hidden), w_out[:, columns]))

        def weight_grads(left, right, grads):
            tile = 128 if left.shape[2] % 128 == 0 else left.shape[2]

            @pl.loop(0, left.shape[2] // tile)
            def _(index):
                columns = pl.ds(pl.multiple_of(index * tile, tile), tile)
                grads[columns] = weight_grad(
                    left[:, :, columns].reshape(count * tall, tile),
                    right[...].reshape(count * tall, right.shape[2]),
                ).astype(BF16)

        def first():
            block = 256 if width % 256 == 0 else width
            late.need(0)

            @pl.loop(0, width // block)
            def _(index):
                columns = pl.ds(pl.multiple_of(index * block, block), block)
                middle[:, columns] = tokens[:, columns].astype(F32) + matmul(
                    gated[:, :width], full_out[:, columns]
                )

            value = middle[...]
            rstat = lax.rsqrt(jnp.mean(value * value, axis=1, keepdims=True) + EPSILON)
            outs[2][...] = value * rstat
            outs[3][...] = rstat
            normed[...] = (outs[2][...] * gain[...]).astype(BF16)

        weights = together(
            shard_gather(ring, fill_in, w_in, *w_in_sems),
            shard_gather(ring, fill_out, w_out, *w_out_sems),
        )
        next(weights)
        next(weights)
        first()
        yield from together(weights, ring_gather(ring, normed, rows_all, *rows_sems, False))
        sums = together(
            ring_sum(ring, in_part, in_held, outs[1], *in_sems, False, True),
            ring_sum(ring, out_part, out_held, out_sum, *out_sems, False, True),
        )

        def turn():
            for _ in range(RING_PIECES):
                next(sums)

        late.need(1)
        nearest = count // 2 - 1
        compute(slice(2 * nearest - 1, 2 * nearest + 1))
        turn()
        compute(slice(count - 1, count))
        turn()
        for pair in range(nearest - 1, 0, -1):
            compute(slice(2 * pair - 1, 2 * pair + 1))
        compute(slice(0, 1))
        turn()
        weight_grads(hidden, grad_out, grad_w_out)
        weight_grads(rows_all, grad_mid, grad_w_in)
        yield from together(
            sums,
            shard_sum(ring, grad_w_in, outs[4], *grad_in_rest),
            shard_sum(ring, grad_w_out, outs[5], *grad_out_rest),
        )
        outs[0][...] = (middle[...] + out_sum[...]).astype(BF16)


def fold(block):
    half = block.shape[0] // 2
    return jnp.concatenate([block[:half], block[half:]], axis=1)


def unfold(block):
    half = block.shape[1] // 2
    return jnp.concatenate([block[:, :half], block[:, half:]], axis=0)


def swap_sems(count):
    return sems(count - 1, count - 1)


def swap(ring, sent, received, send_sem, recv_sem):
    _, peers = all_peers(ring)
    copies = [
        remote(sent.at[to[0]], received.at[ring.ctx], send_sem.at[i], recv_sem.at[i], to)
        for i, to in enumerate(peers)
    ]
    for copy in copies:
        copy.start()
    received[ring.ctx] = sent[ring.ctx]
    yield from idle(RING_PIECES)
    for copy in copies:
        copy.wait()


def small_sum_scratch(shape):
    count, shards = lax.axis_size("ctx"), lax.axis_size("fsdp")
    return [
        pltpu.VMEM((shards,) + shape, F32),
        pltpu.VMEM((count,) + shape, F32),
    ] + sems(shards - 1, shards - 1, count - 1, count - 1)


def small_sum(ring, small, total, near, far, near_send, near_recv, far_send, far_recv):
    siblings, peers = all_peers(ring)
    me, row = ring.fsdp, ring.ctx
    near[me] = small[...]
    first = [
        remote(small, near.at[me], near_send.at[i], near_recv.at[i], to)
        for i, to in enumerate(siblings)
    ]
    for copy in first:
        copy.start()
    yield from idle(RING_PIECES)
    for copy in first:
        copy.wait()
    far[row] = sum([near[i] for i in range(len(siblings) + 1)])
    second = [
        remote(far.at[row], far.at[row], far_send.at[i], far_recv.at[i], to)
        for i, to in enumerate(peers)
    ]
    for copy in second:
        copy.start()
    yield from idle(2 * RING_PIECES)
    for copy in second:
        copy.wait()
    total[...] = sum([far[i] for i in range(len(peers) + 1)])


class Attention:
    kinds = ("all",)

    def __init__(self, rows, heads, dim):
        self.rows, self.heads, self.dim = rows, heads, dim
        self.scaling = dim ** (-0.5)
        self.tall = min(256 if rows <= 1024 else 128, rows)

    def block(self, index):
        rows = slice(index * self.tall, (index + 1) * self.tall)
        return rows, (index + 1) * self.tall

    def allowed(self, rows, wide, info, across):
        shape = (self.tall, wide)
        here = lax.broadcasted_iota(jnp.int32, shape, 0) + rows.start
        there = lax.broadcasted_iota(jnp.int32, shape, 1)
        return (there <= here) & (info[rows, 24:25] == across[8:9, :wide])

    def part(self, qkv, which, head, rows):
        start = (which * self.heads + head) * self.dim
        return qkv[rows, start : start + self.dim]

    def scores(self, qkv, info, across, head, rows, wide, allowed):
        queries = self.part(qkv, 0, head, rows)
        keys = self.part(qkv, 1, head, slice(0, wide))
        scores = matmul_rows(queries, keys) * self.scaling
        scores = scores + info[rows, head : head + 1] - across[head : head + 1, :wide]
        return queries, keys, jnp.where(allowed, scores, NEGATIVE)


class Late:
    def __init__(self, arrays):
        self.count = len(arrays)
        self.scratch = [pltpu.VMEM(a.shape, a.dtype) for a in arrays]
        self.scratch += [pltpu.SemaphoreType.DMA((self.count,))]

    def start(self, refs, scratch):
        self.held, self.waiting = list(scratch[: self.count]), {}
        for i, ref in enumerate(refs):
            copy = pltpu.make_async_copy(ref, self.held[i], scratch[self.count].at[i])
            copy.start()
            self.waiting[i] = copy
        return self

    def need(self, *which):
        for i in which:
            if i in self.waiting:
                self.waiting.pop(i).wait()


class Early:
    def __init__(self, shapes):
        self.count = len(shapes)
        self.scratch = [pltpu.VMEM(a.shape, a.dtype) for a in shapes]
        self.scratch += [pltpu.SemaphoreType.DMA((self.count,))]

    def begin(self, refs, scratch):
        self.refs, self.held, self.sem = refs, list(scratch[: self.count]), scratch[self.count]
        self.leaving = []
        return self

    def ready(self, *which):
        for i in which:
            copy = pltpu.make_async_copy(self.held[i], self.refs[i], self.sem.at[i])
            copy.start()
            self.leaving.append(copy)

    def finish(self):
        for copy in self.leaving:
            copy.wait()


def split_refs(refs, sizes):
    groups, at = [], 0
    for size in sizes:
        groups.append(list(refs[at : at + size]))
        at += size
    return groups


EXACT = dict(preferred_element_type=F32, precision=lax.Precision.HIGHEST)


class Forward(Attention):
    def __init__(self, normed, cotangent, mixed_shard, w_out, bias, seg, heads, dim):
        count, shards = lax.axis_size("ctx"), lax.axis_size("fsdp")
        tall, width = normed.shape
        rows = tall * count
        super().__init__(rows, heads, dim)
        hidden = heads * dim
        self.hidden = hidden
        documents = seg.astype(F32)
        self.ins = [normed, cotangent, mixed_shard, w_out, bias]
        self.in_specs = [ANYWHERE] * 4 + [VMEM] * 3
        self.ins += [documents[:, None], documents[None, :]]
        everyone = jax.ShapeDtypeStruct((count, tall, width), BF16)
        self.outs = [
            everyone,
            everyone,
            jax.ShapeDtypeStruct((width, mixed_shard.shape[1]), BF16),
            jax.ShapeDtypeStruct((width, width), BF16),
            jax.ShapeDtypeStruct((rows, 3 * hidden), BF16),
            jax.ShapeDtypeStruct((rows, hidden), F32),
            jax.ShapeDtypeStruct((rows, hidden), F32),
            jax.ShapeDtypeStruct((rows, 128), F32),
            jax.ShapeDtypeStruct((16, rows), F32),
            jax.ShapeDtypeStruct((tall, count * hidden), BF16),
        ]
        self.out_specs = [ANYWHERE] * 7 + [VMEM] * 3
        self.early = Early([self.outs[i] for i in (0, 2, 4, 5, 6)])
        ring = [pltpu.SemaphoreType.DMA] + ring_sems(count)
        swapped = pltpu.VMEM((count, tall // 2, 2 * hidden), BF16)
        groups = [
            ring,
            ring,
            shard_gather_sems(1),
            shard_gather_sems(1),
            [swapped, swapped] + swap_sems(count),
            self.early.scratch,
        ]
        self.sizes = [len(group) for group in groups]
        self.scratch = sum(groups, [])

    def run(self, ring, ins, outs, scratch):
        rows_sems, cotangent_sems, mixed_sems, out_sems, swapping, held = split_refs(
            scratch, self.sizes
        )
        own, cotangent, mixed_shard, w_out, bias, seg_rows, seg_columns = ins
        _, grad_out, _, full_out, _, _, _, info, across, gated = outs
        early = self.early.begin([outs[i] for i in (0, 2, 4, 5, 6)], held)
        normed, mixed_in, qkv, attended, gate = early.held
        sent, received = swapping[:2]
        count, tall, _ = normed.shape

        def filled_from(source):
            def fill(shard, local_sem):
                return [pltpu.make_async_copy(source, shard, local_sem.at[0])], source

            return fill

        def later(turns, walk):
            yield from idle(turns)
            yield from walk

        def main():
            yield from together(
                ring_gather(ring, own, normed, *rows_sems, True),
                shard_gather(ring, filled_from(mixed_shard), mixed_in, *mixed_sems),
            )
            early.ready(0, 1)
            self.project(normed, mixed_in, bias, qkv, gate, info)
            early.ready(2, 4)
            self.decay(info, across, seg_rows, seg_columns)
            yield
            yield from self.attend(qkv, info, across, attended)
            early.ready(3)
            for i in range(count):
                rows = slice(i * tall, (i + 1) * tall)
                sent[i] = fold((attended[rows] * gate[rows]).astype(BF16))
            yield from swap(ring, *swapping)
            gated[...] = jnp.concatenate([unfold(received[i]) for i in range(count)], axis=1)

        turns = count // 2 * RING_PIECES
        yield from together(
            main(),
            later(turns - 1, ring_gather(ring, cotangent, grad_out, *cotangent_sems, False)),
            later(turns // 2, shard_gather(ring, filled_from(w_out), full_out, *out_sems)),
        )
        early.finish()

    def project(self, normed, mixed_in, bias, qkv, gate, info):
        count, tall, width = normed.shape
        pair = 2 if count % 2 == 0 else 1
        hidden = self.hidden

        @pl.loop(0, count // pair)
        def _(index):
            block = normed[pl.ds(index * pair, pair)].reshape(pair * tall, width)
            rows = pl.ds(pl.multiple_of(index * pair * tall, pair * tall), pair * tall)
            mixed = matmul(block, mixed_in[...])
            qkv[rows] = mixed[:, : 3 * hidden].astype(BF16)
            gate[rows] = jax.nn.sigmoid(mixed[:, 3 * hidden : 4 * hidden])
            info[rows] = mixed[:, 4 * hidden : 4 * hidden + 128]
            info[rows, 8:16] = info[rows, 0:8] + bias[...]

    def decay(self, info, across, seg_rows, seg_columns):
        tall = 128
        here = lax.broadcasted_iota(jnp.int32, (tall, tall), 0)
        there = lax.broadcasted_iota(jnp.int32, (tall, tall), 1)
        wedge = (there <= here).astype(F32)
        before = jnp.zeros((1, 8), F32)
        pad = jnp.zeros((tall, 120), F32)
        for index in range(self.rows // tall):
            rows = slice(index * tall, (index + 1) * tall)
            logs = jax.nn.log_sigmoid(info[rows, 8:16])
            sums = jnp.dot(wedge, jnp.concatenate([logs, pad], axis=1), **EXACT)[:, :8] + before
            before = sums[tall - 1 :]
            info[rows, 0:8] = sums
            across[0:8, rows] = jnp.concatenate([sums, pad], axis=1).T[:8]
        info[:, 24:25] = seg_rows[...]
        across[8:9] = seg_columns[...]

    def attend(self, qkv, info, across, attended):
        for index in range(self.rows // self.tall):
            rows, wide = self.block(index)
            allowed = self.allowed(rows, wide, info, across)
            mixed = []
            for head in range(self.heads):
                _, _, scores = self.scores(qkv, info, across, head, rows, wide, allowed)
                row_max = jnp.max(scores, axis=1, keepdims=True)
                raised = jnp.exp(scores - row_max)
                row_total = jnp.sum(raised, axis=1, keepdims=True)
                probabilities = (raised * (1.0 / row_total)).astype(BF16)
                mixed.append(matmul(probabilities, self.part(qkv, 2, head, slice(0, wide))))
                info[rows, 16 + head : 17 + head] = row_max + jnp.log(row_total)
                if head < self.heads - 1:
                    yield
            attended[rows] = jnp.concatenate(mixed, axis=1)
            yield


def slow(walk, turns):
    for _ in walk:
        yield from idle(turns)


class Backward(Attention):
    def __init__(self, own_heads, named):
        rows = named["qkv"].shape[0]
        super().__init__(rows, own_heads, named["qkv"].shape[1] // 3 // own_heads)
        self.names = list(named)
        hbm = ("gated", "grad_ffn_in")
        self.loaded = ("full_out", "qkv", "attended", "gate_value", "mixed_in", "normed", "normed_one")
        self.late = Late([named[name] for name in self.loaded])
        self.ins = [named[name] for name in self.names]
        self.in_specs = [
            ANYWHERE if name in hbm + self.loaded else VMEM for name in self.names
        ]
        count, shards = lax.axis_size("ctx"), lax.axis_size("fsdp")
        tall, width = named["gated"].shape
        hidden = own_heads * self.dim
        self.main = 4 * hidden
        both = -(-(5 * hidden + own_heads) // 128) * 128
        ffn = [named["grad_ffn_in"]]
        shard_rows = width // shards
        swapped = pltpu.VMEM((count, tall // 2, 2 * hidden), BF16)
        block = pltpu.VMEM((shards * tall, width), BF16)
        heads = pltpu.VMEM((self.rows, hidden), BF16)
        self.outs = (
            [jax.ShapeDtypeStruct((tall, width), F32)]
            + [jax.ShapeDtypeStruct((count,) + grad.shape, BF16) for grad in ffn]
            + [jax.ShapeDtypeStruct((count, shard_rows, both), BF16)]
            + [jax.ShapeDtypeStruct((8, width), F32)]
        )
        self.out_specs = [VMEM] + [ANYWHERE] * 2 + [VMEM]
        ring = [pltpu.SemaphoreType.DMA] + ring_sems(count)
        groups = [
            [pltpu.VMEM((3, own_heads, self.rows, self.dim), F32)],
            [pltpu.VMEM((self.rows, 128), F32), pltpu.VMEM((8, self.rows), F32)],
            [pltpu.VMEM((self.rows, self.main + 128), BF16)],
            [
                pltpu.VMEM((count, shard_rows, hidden), BF16),
                pltpu.VMEM((2, count // 2, shard_rows, hidden), BF16),
                pltpu.VMEM((shard_rows, hidden), F32),
            ]
            + ring_sems(count),
            [
                pltpu.VMEM((count, tall, width), BF16),
                pltpu.VMEM((2, count // 2, tall, width), BF16),
                pltpu.VMEM((tall, width), F32),
            ]
            + ring_sems(count),
            [
                pltpu.VMEM((shard_rows, both), BF16),
                pltpu.VMEM((width, self.main + 128), BF16),
                pltpu.VMEM((shard_rows, self.main + 128), BF16),
            ]
            + shard_sum_scratch(shard_rows, self.main + 128),
            ring,
            ring,
            ring,
            [pltpu.VMEM((8, width), F32)] + small_sum_scratch((8, width)),
            [pltpu.VMEM((tall, width), F32), pltpu.VMEM((tall, count * hidden), BF16)],
            [swapped, swapped] + swap_sems(count),
            [heads, heads],
            [block] + shard_gather_sems(1),
            [block] + shard_gather_sems(1),
            [pltpu.VMEM((tall, width), BF16), pltpu.VMEM((shards * tall, shard_rows), BF16)],
            self.late.scratch,
        ]
        self.sizes = [len(group) for group in groups]
        self.scratch = sum(groups, [])

    def run(self, ring, ins, outs, scratch):
        groups = split_refs(scratch, self.sizes)
        named = dict(zip(self.names, ins))
        late = self.late.start([named[name] for name in self.loaded], groups[16])
        named.update(zip(self.loaded, late.held))
        out_part, out_held, out_sum, *out_sems = groups[3]
        rows_part, rows_held, rows_sum, *rows_sems = groups[4]
        grad_mixed = groups[2][0]
        grads_all, grads_part, grads_sum, *grads_rest = groups[5]
        small, *small_rest = groups[9]
        named["grad_middle"], grad_gated = groups[10]
        named["grad_attn"], named["grad_gatelog"] = groups[12]
        gated_block, *gated_sems = groups[13]
        branch_block, *branch_sems = groups[14]
        branch, gated_columns = groups[15]
        count, tall, width = rows_part.shape

        def filled_from(source):
            def fill(shard, local_sem):
                return [pltpu.make_async_copy(source, shard, local_sem.at[0])], source

            return fill

        gather_gated = shard_gather(
            ring, filled_from(named["gated"]), gated_block, *gated_sems, turns=1
        )

        def main():
            next(gather_gated)
            next(gather_gated)
            late.need(0)
            self.branch_back(named, grad_gated, groups[11][0], branch, small)
            yield from together(
                swap(ring, *groups[11]),
                shard_gather(ring, filled_from(branch), branch_block, *branch_sems, turns=2),
                gather_gated,
            )
            late.need(1, 2, 3)
            self.gate_back(named, groups[11][1])
            self.out_grads(ring, gated_block, branch_block, gated_columns, out_part)
            yield from together(
                self.attention(named, *groups[0], *groups[1]),
                ring_sum(ring, out_part, out_held, out_sum, *out_sems, True),
            )
            self.join(named, *groups[0], *groups[1], grad_mixed, small)
            block = 256 if width % 256 == 0 else width
            late.need(4)

            @pl.loop(0, width // block)
            def _(index):
                columns = pl.ds(pl.multiple_of(index * block, block), block)
                part = matmul_rows(grad_mixed[...], named["mixed_in"][columns])
                rows_part[:, :, columns] = part.astype(BF16).reshape(count, tall, block)

            yield from together(
                ring_sum(ring, rows_part, rows_held, rows_sum, *rows_sems, True),
                weights(),
            )

        def weights():
            yield from idle(RING_PIECES)
            late.need(5)
            self.weight_grads(named, grad_mixed, grads_part)
            yield from shard_sum(ring, grads_part, grads_sum, *grads_rest)
            tail = grads_all.shape[1] - self.main - out_sum.shape[1]
            grads_all[:, : self.main] = grads_sum[:, : self.main]
            grads_all[:, self.main :] = jnp.concatenate(
                [out_sum[...].astype(BF16), grads_sum[:, self.main : self.main + tail]], axis=1
            )

        yield from together(
            slow(ring_gather(ring, named["grad_ffn_in"], outs[1], *groups[6], True), 2),
            main(),
        )
        late.need(6)
        self.norm_back(named, rows_sum, outs[0], small)
        yield from together(
            ring_gather(ring, grads_all, outs[2], *groups[8], True),
            small_sum(ring, small, outs[3], *small_rest),
        )

    def branch_back(self, named, grad_gated, sent, branch, small):
        grad, normed = named["grad_normed_two"][...], named["normed_two"][...]
        small[...] = jnp.zeros_like(small)
        small[1:2] = jnp.sum(grad * normed, axis=0, keepdims=True)
        grad_normed = grad * named["gain_two"][...]
        inner = jnp.mean(grad_normed * normed, axis=1, keepdims=True)
        named["grad_middle"][...] = named["cotangent"][...].astype(F32) + named["rstat_two"][...] * (
            grad_normed - normed * inner
        )
        branch[...] = named["grad_middle"][...].astype(BF16)
        count, hidden = sent.shape[0], sent.shape[2] // 2
        width = grad.shape[1]
        block = 256 if width % 256 == 0 else width
        if grad_gated.shape[1] > width:
            grad_gated[...] = jnp.zeros_like(grad_gated)

        @pl.loop(0, width // block)
        def _(index):
            columns = pl.ds(pl.multiple_of(index * block, block), block)
            part = matmul_rows(branch[...], named["full_out"][columns])
            grad_gated[:, columns] = part.astype(BF16)

        for i in range(count):
            sent[i] = fold(grad_gated[:, i * hidden : (i + 1) * hidden])

    def gate_back(self, named, received):
        count, tall = received.shape[0], 2 * received.shape[1]
        for i in range(count):
            rows = slice(i * tall, (i + 1) * tall)
            grad = unfold(received[i]).astype(F32)
            gate = named["gate_value"][rows]
            named["grad_attn"][rows] = (grad * gate).astype(BF16)
            named["grad_gatelog"][rows] = (
                grad * named["attended"][rows] * (gate * (1.0 - gate))
            ).astype(BF16)

    def attention(self, named, grads, sums_rows, sums_columns):
        qkv, info, across, grad_attn = [
            named[name] for name in ("qkv", "info", "across", "grad_attn")
        ]
        grad_q, grad_k, grad_v = [grads.at[i] for i in range(3)]
        blocks = self.rows // self.tall
        sums_columns[...] = jnp.zeros_like(sums_columns)
        pad = jnp.zeros((self.tall, 128 - self.heads), F32)
        for index in reversed(range(blocks)):
            rows, wide = self.block(index)
            allowed = self.allowed(rows, wide, info, across)
            own = slice(0, wide)
            row_sums = []
            for head in range(self.heads):
                queries, keys, scores = self.scores(
                    qkv, info, across, head, rows, wide, allowed
                )
                probabilities = jnp.exp(scores - info[rows, 16 + head : 17 + head])
                grad_part = grad_attn[rows, head * self.dim : (head + 1) * self.dim]
                grad_probs = matmul_rows(grad_part, self.part(qkv, 2, head, own))
                row_inner = jnp.sum(probabilities * grad_probs, axis=1, keepdims=True)
                grad_scores = (probabilities * (grad_probs - row_inner)).astype(BF16)
                grad_q[head, rows] = matmul(grad_scores, keys) * self.scaling
                from_k = weight_grad(grad_scores, queries) * self.scaling
                from_v = weight_grad(probabilities.astype(BF16), grad_part)
                wide_sums = grad_scores.astype(F32)
                row_sums.append(jnp.sum(wide_sums, axis=1, keepdims=True))
                column_sums = jnp.sum(wide_sums, axis=0, keepdims=True)
                if index == blocks - 1:
                    grad_k[head], grad_v[head] = from_k, from_v
                    sums_columns[head : head + 1] = column_sums
                else:
                    grad_k[head, own] += from_k
                    grad_v[head, own] += from_v
                    sums_columns[head : head + 1, own] += column_sums
                if head < self.heads - 1:
                    yield
            sums_rows[rows] = jnp.concatenate(row_sums + [pad], axis=1)
            yield

    def join(self, named, grads, sums_rows, sums_columns, grad_mixed, small):
        for index in range(self.rows // self.tall):
            rows, _ = self.block(index)
            grad_mixed[rows, : self.main] = jnp.concatenate(
                [grads[i, head, rows].astype(BF16) for i in range(3) for head in range(self.heads)]
                + [named["grad_gatelog"][rows]],
                axis=1,
            )
        tall = 128
        here = lax.broadcasted_iota(jnp.int32, (tall, tall), 0)
        there = lax.broadcasted_iota(jnp.int32, (tall, tall), 1)
        wedge = (here <= there).astype(F32)
        later, bias = jnp.zeros((1, 8), F32), jnp.zeros((1, 8), F32)
        pad = jnp.zeros((tall, 120), BF16)
        for index in reversed(range(self.rows // tall)):
            rows = slice(index * tall, (index + 1) * tall)
            inside = jnp.dot(wedge, sums_rows[rows], **EXACT)[:, :8] - lax.dot_general(
                wedge, sums_columns[:, rows], (((1,), (1,)), ((), ())), **EXACT
            )
            logits = named["info"][rows, 8:16]
            grad_logits = ((inside + later) * jax.nn.sigmoid(-logits)).astype(BF16)
            later = later + inside[:1]
            bias = bias + jnp.sum(grad_logits.astype(F32), axis=0, keepdims=True)
            grad_mixed[rows, self.main :] = jnp.concatenate([grad_logits, pad], axis=1)
        small[2:3] = sum(
            bias[:, head : head + 1] * named["places"][head : head + 1]
            for head in range(self.heads)
        )

    def out_grads(self, ring, gated_block, branch_block, gated_columns, parts):
        count, rows, hidden = parts.shape
        for i in range(lax.axis_size("fsdp")):

            @pl.when(ring.fsdp == i)
            def _():
                gated_columns[...] = gated_block[:, i * rows : (i + 1) * rows]

        for i in range(count):
            stop = min((i + 1) * hidden, branch_block.shape[1])
            if stop > i * hidden:
                part = weight_grad(gated_columns[...], branch_block[:, i * hidden : stop])
                parts[i] = part.astype(BF16)
            else:
                parts[i] = jnp.zeros((rows, hidden), BF16)

    def weight_grads(self, named, grad_mixed, parts):
        count, tall, width = named["normed"].shape
        tile = 128

        @pl.loop(0, width // tile)
        def _(index):
            columns = pl.ds(pl.multiple_of(index * tile, tile), tile)
            normed = named["normed"][:, :, columns].reshape(count * tall, tile)
            parts[columns] = weight_grad(normed, grad_mixed[...]).astype(BF16)

    def norm_back(self, named, rows_sum, grad_tokens, small):
        grad, normed = rows_sum[...], named["normed_one"][...]
        small[0:1] = jnp.sum(grad * normed, axis=0, keepdims=True)
        grad_normed = grad * named["gain_one"][...]
        inner = jnp.mean(grad_normed * normed, axis=1, keepdims=True)
        grad_tokens[...] = named["grad_middle"][...] + named["rstat_one"][...] * (
            grad_normed - normed * inner
        )


def exchange(ident, name, *tasks):
    count = lax.axis_size("ctx")

    def take(refs, sizes):
        groups, at = [], 0
        for size in sizes:
            groups.append(refs[at : at + size])
            at += size
        return groups

    ins = [len(task.ins) for task in tasks]
    outs = [len(task.outs) for task in tasks]
    scratch = [len(task.scratch) for task in tasks]

    def kernel(*refs):
        ring = Ring(count)
        kinds = sum([task.kinds for task in tasks], ())
        peers = []
        if "all" in kinds:
            peers = sum(all_peers(ring), [])
        else:
            if "ring" in kinds:
                peers += [ring.device(1), ring.device(-1)]
            if "shard" in kinds:
                pair, others = shard_pair(ring, lax.axis_size("fsdp"))
                peers += [(ring.ctx, to) for to in [pair] + others]
        greet(peers)
        groups = [
            take(refs[: sum(ins)], ins),
            take(refs[sum(ins) : sum(ins) + sum(outs)], outs),
            take(refs[sum(ins) + sum(outs) :], scratch),
        ]
        for _ in together(*[task.run(ring, *parts) for task, *parts in zip(tasks, *groups)]):
            pass

    results = pl.pallas_call(
        kernel,
        out_shape=sum([task.outs for task in tasks], []),
        in_specs=sum([task.in_specs for task in tasks], []),
        out_specs=sum([task.out_specs for task in tasks], []),
        scratch_shapes=sum([task.scratch for task in tasks], []),
        compiler_params=pltpu.CompilerParams(
            collective_id=ident, has_side_effects=True, vmem_limit_bytes=62 * 2**20
        ),
        cost_estimate=pl.CostEstimate(flops=0, bytes_accessed=100_000_000, transcendentals=0),
        name=name,
    )(*sum([task.ins for task in tasks], []))
    return take(list(results), outs)


def flat(blocks):
    return blocks.reshape(-1, blocks.shape[-1])


def permute_rows(value, beside):
    count, me = lax.axis_size("ctx"), lax.axis_index("ctx")
    order = [ring_index(place, count) for place in range(count)]
    rows, half = value.shape[0], value.shape[0] // 2
    ways = [[(order[i], order[(i + sign) % count]) for i in range(count)] for sign in (1, -1)]

    parts, offsets = [value], [0]
    blocks, results, beside = [value, value], [], list(beside)
    for hops in range(1, count // 2 + 1):
        work = None
        if hops > 1 and beside:
            work, operand = beside.pop(0)
            blocks[0], blocks[1], operand = lax.optimization_barrier((*blocks, operand))
        last = hops == count // 2
        sent = [blocks[0][:half], blocks[1][half:]] if last else blocks
        blocks = [lax.ppermute(block, "ctx", way) for block, way in zip(sent, ways)]
        if work is not None:
            result = work(operand)
            blocks[0], blocks[1], result = lax.optimization_barrier((*blocks, result))
            results.append(result)
        parts += blocks
        offsets += [-hops, hops]
    place = (ring_place(me, count) + jnp.asarray(offsets[:-1], jnp.int32) + count) % count
    return place_rows(parts, ring_index(place, count)), results


def place_rows(parts, sources):
    rows, width = parts[0].shape
    count = len(parts) - 1
    half = rows // 2

    def kernel(source_ref, *refs):
        ins, out = refs[:-1], refs[-1]
        step = pl.program_id(0)
        for j in range(count):

            @pl.when(step == j)
            def _():
                if j < count - 1:
                    out[...] = ins[j][...].astype(F32)
                else:
                    out[:half] = ins[j][...].astype(F32)
                    out[half:] = ins[j + 1][...].astype(F32)

    return pl.pallas_call(
        kernel,
        out_shape=jax.ShapeDtypeStruct((rows * count, width), F32),
        grid_spec=pltpu.PrefetchScalarGridSpec(
            num_scalar_prefetch=1,
            grid=(count,),
            in_specs=[pl.BlockSpec(part.shape, lambda i, _: (0, 0)) for part in parts],
            out_specs=pl.BlockSpec((rows, width), lambda i, source: (source[i], 0)),
        ),
        compiler_params=pltpu.CompilerParams(vmem_limit_bytes=60 * 2**20),
        cost_estimate=pl.CostEstimate(
            flops=0, bytes_accessed=rows * width * count * 6, transcendentals=0
        ),
        name="place_rows",
    )(sources, *parts)


def ffn_columns(blocks, n_fsdp):
    count, rows, both = blocks.shape
    width, piece = both // 2, both // 2 // n_fsdp
    steps = 4
    tall = rows // steps

    def kernel(block_ref, *outs):
        for j in range(count):
            for half in range(2):
                for group in range(n_fsdp):
                    start, to = half * width + group * piece, (group * count + j) * piece
                    outs[half][:, to : to + piece] = block_ref[j, :, start : start + piece].astype(F32)

    wide = jax.ShapeDtypeStruct((rows, width * count), F32)
    spec = pl.BlockSpec((tall, width * count), lambda i: (i, 0))
    return pl.pallas_call(
        kernel,
        out_shape=(wide, wide),
        grid=(steps,),
        in_specs=[pl.BlockSpec((count, tall, both), lambda i: (0, i, 0))],
        out_specs=(spec, spec),
        compiler_params=pltpu.CompilerParams(vmem_limit_bytes=40 * 2**20),
        cost_estimate=pl.CostEstimate(
            flops=0, bytes_accessed=rows * both * count * 6, transcendentals=0
        ),
        name="ffn_columns",
    )(blocks)


def head_columns(blocks, sizes, widths):
    count, rows, total = blocks.shape
    steps = 4
    tall = rows // steps
    starts = [sum(sizes[:i]) for i in range(len(sizes))]

    def kernel(block_ref, *outs):
        for start, size, out in zip(starts, sizes, outs):
            for i in range(0, count, 2):
                pair = jnp.concatenate(
                    [block_ref[i + k][:, start : start + size].astype(F32) for k in range(2)], axis=1
                )
                at = i * size
                keep = min(2 * size, out.shape[1] - at)
                if keep > 0:
                    out[:, at : at + keep] = pair[:, :keep]

    return pl.pallas_call(
        kernel,
        out_shape=tuple(jax.ShapeDtypeStruct((rows, w), F32) for w in widths),
        grid=(steps,),
        in_specs=[pl.BlockSpec((count, tall, total), lambda i: (0, i, 0))],
        out_specs=tuple(pl.BlockSpec((tall, w), lambda i: (i, 0)) for w in widths),
        compiler_params=pltpu.CompilerParams(vmem_limit_bytes=40 * 2**20),
        cost_estimate=pl.CostEstimate(
            flops=0, bytes_accessed=count * rows * total * 6, transcendentals=0
        ),
        name="head_columns",
    )(blocks)


def shards(
    tokens,
    segments,
    gain_attn,
    w_query,
    w_key,
    w_value,
    w_forget,
    forget_bias,
    w_outgate,
    w_out,
    gain_ffn,
    w_gate,
    w_up,
    w_down,
    cotangent,
):
    n_ctx, me = lax.axis_size("ctx"), lax.axis_index("ctx")
    n_fsdp = lax.axis_size("fsdp")
    tok_rows, width = tokens.shape[1:]
    seq_rows = tok_rows * n_ctx
    n_heads = forget_bias.shape[0]
    head_dim = width // n_heads
    own_heads = -(-n_heads // n_ctx)
    own_width = own_heads * head_dim
    padded = own_width * n_ctx
    ffn_rows = w_down.shape[0]
    ffn_piece = ffn_rows // n_ctx
    ffn_width = ffn_piece * n_fsdp
    shard_rows = w_query.shape[0]

    def widen(value, size):
        return jnp.pad(value, ((0, 0), (0, size - value.shape[1])))

    def own_columns(weight, size):
        return lax.dynamic_slice_in_dim(widen(weight, size * n_ctx), me * size, size, 1)

    def own_ffn(weight):
        return [
            lax.dynamic_slice_in_dim(weight, (group * n_ctx + me) * ffn_piece, ffn_piece, 1)
            for group in range(n_fsdp)
        ]

    mixed_shard = jnp.concatenate(
        [own_columns(w, own_width) for w in (w_query, w_key, w_value, w_outgate)]
        + [widen(own_columns(w_forget, own_heads), 128)],
        axis=1,
    )
    bias_own = lax.dynamic_slice_in_dim(
        jnp.pad(forget_bias, (0, own_heads * n_ctx - n_heads)), me * own_heads, own_heads, 0
    )
    bias_own = jnp.pad(bias_own, (0, 8 - own_heads))

    seg = segments[0]
    inputs = tokens[0].astype(F32)
    gain_one = gain_attn.astype(F32)
    normed_one, rstat_one = rms_stats(inputs)
    (
        (
            normed,
            grad_out_low,
            mixed_in,
            full_out,
            qkv,
            attended,
            gate_value,
            info,
            across,
            gated,
        ),
    ) = exchange(
        0,
        "forward",
        Forward(
            (normed_one * gain_one).astype(BF16),
            cotangent[0],
            mixed_shard,
            w_out,
            bias_own[None],
            segments[0],
            own_heads,
            head_dim,
        ),
    )
    gain_two = gain_ffn.astype(F32)[None]
    w_in = [w_gate, w_up]
    if ffn_piece % 128 != 0:
        w_in = [jnp.concatenate(own_ffn(w_gate) + own_ffn(w_up), axis=1)]
    ((output, grad_normed_two, normed_two, rstat_two, grad_ffn_in, grad_ffn_out),) = exchange(
        1,
        "ffn",
        Ffn(tokens[0], gated, full_out, gain_two, grad_out_low, w_in, w_down, ffn_piece),
    )
    spots = jnp.arange(own_heads, dtype=jnp.int32)[:, None] + me * own_heads
    places = (spots == jnp.arange(width, dtype=jnp.int32)[None, :]).astype(F32)
    ((grad_inputs, spread_ffn_in, spread_attn, small),) = exchange(
        2,
        "backward",
        Backward(
            own_heads,
            {
                "qkv": qkv,
                "info": info,
                "across": across,
                "attended": attended,
                "gate_value": gate_value,
                "grad_normed_two": grad_normed_two,
                "normed_two": normed_two,
                "rstat_two": rstat_two,
                "gain_two": gain_two,
                "cotangent": cotangent[0],
                "full_out": full_out,
                "gated": gated[:, :width],
                "grad_ffn_in": grad_ffn_in,
                "normed": normed,
                "mixed_in": mixed_in,
                "normed_one": normed_one,
                "rstat_one": rstat_one,
                "gain_one": gain_one[None],
                "places": places,
            },
        ),
    )
    sizes = [own_width] * 5 + [own_heads]

    def place_ffn(blocks):
        if ffn_piece % 128 == 0:
            return ffn_columns(blocks, n_fsdp)
        whole = blocks.reshape(n_ctx, shard_rows, 2, n_fsdp, ffn_piece)
        whole = jnp.transpose(whole, (2, 1, 3, 0, 4)).reshape(2, shard_rows, -1).astype(F32)
        return whole[0], whole[1]

    def place_heads(blocks):
        return head_columns(blocks, sizes, [width] * 5 + [n_heads])

    grad_down, ((grad_gate, grad_up), grad_weights) = permute_rows(
        grad_ffn_out, [(place_ffn, spread_ffn_in), (place_heads, spread_attn)]
    )
    return (
        output[None],
        grad_inputs[None],
        small[0],
        grad_weights[0],
        grad_weights[1],
        grad_weights[2],
        grad_weights[5],
        small[2, :n_heads],
        grad_weights[3],
        grad_weights[4],
        small[1],
        grad_gate,
        grad_up,
        grad_down,
    )


def solution(mesh):
    rows, blocks = P("fsdp", None), P("fsdp", "ctx", None)
    return jax.shard_map(
        shards,
        mesh=mesh,
        in_specs=(blocks, rows, P())
        + (rows,) * 4
        + (P(), rows, rows, P(), rows, rows, rows, blocks),
        out_specs=(blocks, blocks, P())
        + (rows,) * 4
        + (P(), rows, rows, P(), rows, rows, rows),
        check_vma=False,
    )
```

```python
import jax
import jax.numpy as jnp
from jax import lax
from jax.experimental import pallas as pl
from jax.experimental.pallas import tpu as pltpu
from jax.sharding import PartitionSpec as P

EPSILON = 1e-06
NEGATIVE = -1e30
BF16, F32 = jnp.bfloat16, jnp.float32


def matmul(left, right):
    return jnp.dot(left, right, preferred_element_type=F32)


def matmul_rows(left, right):
    return lax.dot_general(left, right, (((1,), (1,)), ((), ())), preferred_element_type=F32)


def weight_grad(left, right):
    return lax.dot_general(left, right, (((0,), (0,)), ((), ())), preferred_element_type=F32)


MESH = pl.DeviceIdType.MESH
RING_PIECES = 4


def ring_place(ctx, count):
    odd = ctx % 2
    return ctx // 2 + odd * (count - 1 - 2 * (ctx // 2))


def ring_index(place, count):
    back = place // (count // 2)
    return 2 * place + back * (2 * (count - 1 - place) + 1 - 2 * place)


class Ring:
    def __init__(self, count):
        self.count, self.half = count, count // 2
        self.ctx, self.fsdp = lax.axis_index("ctx"), lax.axis_index("fsdp")
        self.place = ring_place(self.ctx, count)

    def at(self, offset):
        return ring_index((self.place + offset + self.count) % self.count, self.count)

    def device(self, offset):
        return (self.at(offset), self.fsdp)


def greet(devices):
    barrier = pltpu.get_barrier_semaphore()
    for device in devices:
        pl.semaphore_signal(barrier, inc=1, device_id=device, device_id_type=MESH)
    pl.semaphore_wait(barrier, len(devices))


def remote(src, dst, send, recv, device):
    return pltpu.make_async_remote_copy(
        src_ref=src, dst_ref=dst, send_sem=send, recv_sem=recv, device_id=device, device_id_type=MESH
    )


def carried(step, half, pieces, way):
    if step < half - 1:
        return range(pieces)
    return range(pieces // 2) if way == 0 else range(pieces // 2, pieces)


def ring_slot(ring, offset, absolute):
    if absolute:
        return ring.at(offset)
    if abs(offset) == ring.half:
        return ring.count - 1
    return 2 * offset - 1 if offset > 0 else -2 * offset


def ring_gather(ring, own, full, local_sem, send_sem, recv_sem, absolute, pieces=RING_PIECES):
    rows = full.shape[1] // pieces

    def part(k):
        return pl.ds(k * rows, rows)

    def slot(offset):
        return ring_slot(ring, offset, absolute)

    keep = None
    if own is None:
        own = full.at[slot(0)]
    else:
        keep = pltpu.make_async_copy(own, full.at[slot(0)], local_sem)
        keep.start()
    copies = {}
    for step in range(ring.half):
        for k in range(pieces):
            for way, sign in ((0, 1), (1, -1)):
                if step > 0:
                    copies[step - 1, k, way].wait_recv()
                if k not in carried(step, ring.half, pieces, way):
                    continue
                src = own.at[part(k)] if step == 0 else full.at[slot(-sign * step), part(k)]
                to = slot(-sign * step if absolute else -sign * (step + 1))
                copy = remote(
                    src,
                    full.at[to, part(k)],
                    send_sem.at[step, k, way],
                    recv_sem.at[step, k, way],
                    ring.device(sign),
                )
                copy.start()
                copies[step, k, way] = copy
            yield
    for (step, _, _), copy in copies.items():
        if step == ring.half - 1:
            copy.wait_recv()
    for copy in copies.values():
        copy.wait_send()
    if keep is not None:
        keep.wait()


def ring_sum(
    ring, parts, held, total, send_sem, recv_sem, absolute, ahead=False, pieces=RING_PIECES
):
    rows = parts.shape[1] // pieces

    def place(offset):
        return ring_slot(ring, offset, absolute)

    def part(k):
        return pl.ds(k * rows, rows)

    copies = {}

    def send(step, k, way, sign):
        src = parts.at[place(sign * (ring.half - step)), part(k)]
        if (step - 1, k, way) in copies:
            copies[step - 1, k, way].wait_recv()
            slot = held.at[way, step - 1, part(k)]
            slot[...] = (slot[...].astype(F32) + src[...].astype(F32)).astype(BF16)
            src = slot
        copy = remote(
            src,
            held.at[way, step, part(k)],
            send_sem.at[step, k, way],
            recv_sem.at[step, k, way],
            ring.device(sign),
        )
        copy.start()
        copies[step, k, way] = copy

    def farthest(k, way):
        return k in carried(ring.half - 1, ring.half, pieces, way)

    for step in ([None] if ahead else []) + list(range(ring.half)):
        for k in range(pieces):
            for way, sign in ((0, 1), (1, -1)):
                if step is None and not farthest(k, way):
                    send(1, k, way, sign)
                elif step == 0 and farthest(k, way):
                    send(0, k, way, sign)
                elif step == 1 and (farthest(k, way) or not ahead):
                    send(1, k, way, sign)
                elif step is not None and step > 1:
                    send(step, k, way, sign)
            yield
    last = ring.half - 1
    for k in range(pieces):
        for way in range(2):
            copies[last, k, way].wait_recv()
        total[part(k)] = (
            parts[place(0), part(k)].astype(F32)
            + held[0, last, part(k)].astype(F32)
            + held[1, last, part(k)].astype(F32)
        )
    for copy in copies.values():
        copy.wait_send()


def ring_sems(count, pieces=RING_PIECES):
    shape = (count // 2, pieces, 2)
    return [pltpu.SemaphoreType.DMA(shape), pltpu.SemaphoreType.DMA(shape)]


def sems(*counts):
    return [pltpu.SemaphoreType.DMA((max(count, 1),)) for count in counts]


ANYWHERE, VMEM = pl.BlockSpec(memory_space=pl.ANY), pl.BlockSpec(memory_space=pltpu.VMEM)


def shard_pair(ring, shards):
    me = ring.fsdp
    pair = me + 1 - 2 * (me % 2)
    return pair, [(me + 2 * hop) % shards for hop in range(1, shards // 2)]


def all_peers(ring):
    count, shards = lax.axis_size("ctx"), lax.axis_size("fsdp")
    siblings = [(ring.ctx, (ring.fsdp + hop) % shards) for hop in range(1, shards)]
    return siblings, [((ring.ctx + hop) % count, ring.fsdp) for hop in range(1, count)]


def idle(turns):
    for _ in range(turns):
        yield


def together(*walks):
    walks = list(walks)
    while walks:
        walks = [walk for walk in walks if next(walk, walks) is None]
        yield


def shard_gather(ring, fill, whole, local_sem, send_sem, recv_sem, turns=3 * RING_PIECES):
    shards, me = lax.axis_size("fsdp"), ring.fsdp
    rows = whole.shape[0] // shards
    pair, others = shard_pair(ring, shards)

    def shard(index):
        return whole.at[pl.ds(pl.multiple_of(index * rows, rows), rows)]

    local, source = fill(shard(me), local_sem)
    for copy in local:
        copy.start()
    yield
    if source is None:
        for copy in local:
            copy.wait()
    sent = shard(me) if source is None else source
    copies = [
        remote(sent, shard(me), send_sem.at[i], recv_sem.at[i], (ring.ctx, to))
        for i, to in enumerate([pair] + others)
    ]
    for copy in copies:
        copy.start()
    yield from idle(turns)
    passed = []
    for i in range(1, len(copies)):
        copies[i].wait_recv()
        origin = (me - 2 * i + shards) % shards
        at = shards // 2 - 1 + i
        copy = remote(
            shard(origin), shard(origin), send_sem.at[at], recv_sem.at[at], (ring.ctx, pair)
        )
        copy.start()
        passed.append(copy)
    yield from idle(2)
    copies[0].wait_recv()
    for copy in passed:
        copy.wait_recv()
    for copy in copies + passed:
        copy.wait_send()
    if source is not None:
        for copy in local:
            copy.wait()


def shard_gather_sems(parts):
    shards = lax.axis_size("fsdp")
    return sems(parts, shards - 1, shards - 1)


def shard_sum(ring, parts, total, near, far, near_send, near_recv, far_send, far_recv):
    shards, me = lax.axis_size("fsdp"), ring.fsdp
    half, core, chip = shards // 2, me % 2, me // 2
    pair, others = shard_pair(ring, shards)
    rows = parts.shape[0] // shards

    def shard(index):
        return pl.ds(pl.multiple_of(index * rows, rows), rows)

    first = [
        remote(
            parts.at[shard(2 * i + 1 - core)],
            near.at[i],
            near_send.at[i],
            near_recv.at[i],
            (ring.ctx, pair),
        )
        for i in range(half)
    ]
    for copy in first:
        copy.start()
    yield from idle(2)
    for copy in first:
        copy.wait_recv()
    second = []
    for hop in range(1, half):
        to = (chip + hop) % half
        near[to] = (near[to].astype(F32) + parts[shard(2 * to + core)].astype(F32)).astype(BF16)
        copy = remote(
            near.at[to],
            far.at[hop - 1],
            far_send.at[hop - 1],
            far_recv.at[hop - 1],
            (ring.ctx, others[hop - 1]),
        )
        copy.start()
        second.append(copy)
    yield from idle(3 * RING_PIECES)
    sums = parts[shard(me)].astype(F32) + near[chip].astype(F32)
    for hop, copy in enumerate(second):
        copy.wait_recv()
        sums = sums + far[hop].astype(F32)
    total[...] = sums.astype(BF16)
    for copy in first + second:
        copy.wait_send()


def shard_sum_scratch(rows, width):
    half = lax.axis_size("fsdp") // 2
    return [
        pltpu.VMEM((half, rows, width), BF16),
        pltpu.VMEM((max(half - 1, 1), rows, width), BF16),
    ] + sems(half, half, half - 1, half - 1)


class Ffn:
    kinds = ("ring", "shard")

    def __init__(self, tokens, gated, full_out, gain, grad_out, w_in, w_out, piece):
        count, shards = lax.axis_size("ctx"), lax.axis_size("fsdp")
        rows, width = tokens.shape
        self.aligned = len(w_in) == 2
        self.piece, self.inner = piece, piece * shards
        inner, both = self.inner, 2 * self.inner
        shard_rows = width // shards
        self.ins = [grad_out, tokens, gated, full_out, gain, w_out] + list(w_in)
        self.in_specs = [ANYWHERE, VMEM, VMEM, ANYWHERE, VMEM] + [ANYWHERE] * (1 + len(w_in))
        self.late = Late([full_out, grad_out])
        self.outs = [
            jax.ShapeDtypeStruct((rows, width), BF16),
            jax.ShapeDtypeStruct((rows, width), F32),
            jax.ShapeDtypeStruct((rows, width), F32),
            jax.ShapeDtypeStruct((rows, 1), F32),
            jax.ShapeDtypeStruct((shard_rows, both), BF16),
            jax.ShapeDtypeStruct((piece, width), BF16),
        ]
        self.out_specs = [VMEM] * 6
        held = pltpu.VMEM((2, count // 2, rows, width), BF16)
        groups = [
            [pltpu.VMEM((count, rows, width), BF16), pltpu.SemaphoreType.DMA] + ring_sems(count),
            [pltpu.VMEM((width, both), BF16)] + shard_gather_sems(2 * shards),
            [pltpu.VMEM((inner, width), BF16)] + shard_gather_sems(1),
            [pltpu.VMEM((count, rows, inner), BF16), pltpu.VMEM((count, rows, both), BF16)],
            [pltpu.VMEM((count, rows, width), BF16), held] + ring_sems(count),
            [pltpu.VMEM((count, rows, width), BF16), held] + ring_sems(count),
            [pltpu.VMEM((width, both), BF16)] + shard_sum_scratch(shard_rows, both),
            [pltpu.VMEM((inner, width), BF16)] + shard_sum_scratch(piece, width),
            [
                pltpu.VMEM((rows, width), F32),
                pltpu.VMEM((rows, width), BF16),
                pltpu.VMEM((rows, width), F32),
            ],
            self.late.scratch,
        ]
        self.sizes = [len(group) for group in groups]
        self.scratch = sum(groups, [])

    def run(self, ring, ins, outs, scratch):
        _, tokens, gated, _, gain, w_out_rows = ins[:6]
        w_in_rows = ins[6:]
        inner, piece = self.inner, self.piece
        groups = split_refs(scratch, self.sizes)
        late = self.late.start([ins[3], ins[0]], groups[9])
        full_out, grad_out = late.held
        (rows_all, *rows_sems), (w_in, *w_in_sems), (w_out, *w_out_sems) = groups[:3]
        hidden, grad_mid = groups[3]
        (out_part, out_held, *out_sems), (in_part, in_held, *in_sems) = groups[4:6]
        (grad_w_in, *grad_in_rest), (grad_w_out, *grad_out_rest) = groups[6:8]
        middle, normed, out_sum = groups[8]
        count, tall = rows_all.shape[:2]
        width = rows_all.shape[2]

        def fill_in(shard, local_sem):
            if not self.aligned:
                return [pltpu.make_async_copy(w_in_rows[0], shard, local_sem.at[0])], w_in_rows[0]
            copies = []
            for i in range(2):
                for group in range(inner // piece):
                    at = i * (inner // piece) + group
                    start = pl.multiple_of((group * count + ring.ctx) * piece, piece)
                    copies.append(
                        pltpu.make_async_copy(
                            w_in_rows[i].at[:, pl.ds(start, piece)],
                            shard.at[:, pl.ds(at * piece, piece)],
                            local_sem.at[at],
                        )
                    )
            return copies, None

        def fill_out(shard, local_sem):
            start = pl.multiple_of(ring.ctx * piece, piece)
            own = w_out_rows.at[pl.ds(start, piece)]
            return [pltpu.make_async_copy(own, shard, local_sem.at[0])], own

        def compute(slots):
            size = (slots.stop - slots.start) * tall

            def load(ref):
                return ref[slots].reshape(size, ref.shape[2])

            def store(ref, columns, value):
                ref[slots, :, columns] = value.astype(BF16).reshape(-1, tall, value.shape[1])

            tile = min(256, inner)

            @pl.loop(0, inner // tile)
            def _(index):
                def columns(start):
                    return pl.ds(pl.multiple_of(start + index * tile, tile), tile)

                gate = matmul(load(rows_all), w_in[:, columns(0)])
                up = matmul(load(rows_all), w_in[:, columns(inner)])
                grad_hidden = matmul_rows(load(grad_out), w_out[columns(0)])
                sig = jax.nn.sigmoid(gate)
                silu = gate * sig
                store(hidden, columns(0), silu * up)
                store(
                    grad_mid, columns(0), grad_hidden * up * (sig * (1.0 + gate * (1.0 - sig)))
                )
                store(grad_mid, columns(inner), grad_hidden * silu)

            wide = 256 if width % 256 == 0 else width

            @pl.loop(0, width // wide)
            def _(index):
                columns = pl.ds(pl.multiple_of(index * wide, wide), wide)
                store(in_part, columns, matmul_rows(load(grad_mid), w_in[columns]))
                store(out_part, columns, matmul(load(hidden), w_out[:, columns]))

        def weight_grads(left, right, grads):
            tile = 128 if left.shape[2] % 128 == 0 else left.shape[2]

            @pl.loop(0, left.shape[2] // tile)
            def _(index):
                columns = pl.ds(pl.multiple_of(index * tile, tile), tile)
                grads[columns] = weight_grad(
                    left[:, :, columns].reshape(count * tall, tile),
                    right[...].reshape(count * tall, right.shape[2]),
                ).astype(BF16)

        def first():
            block = 256 if width % 256 == 0 else width
            late.need(0)

            @pl.loop(0, width // block)
            def _(index):
                columns = pl.ds(pl.multiple_of(index * block, block), block)
                middle[:, columns] = tokens[:, columns].astype(F32) + matmul(
                    gated[:, :width], full_out[:, columns]
                )

            value = middle[...]
            rstat = lax.rsqrt(jnp.mean(value * value, axis=1, keepdims=True) + EPSILON)
            outs[2][...] = value * rstat
            outs[3][...] = rstat
            normed[...] = (outs[2][...] * gain[...].astype(F32)).astype(BF16)

        weights = together(
            shard_gather(ring, fill_in, w_in, *w_in_sems),
            shard_gather(ring, fill_out, w_out, *w_out_sems),
        )
        next(weights)
        next(weights)
        first()
        yield from together(weights, ring_gather(ring, normed, rows_all, *rows_sems, False))
        sums = together(
            ring_sum(ring, in_part, in_held, outs[1], *in_sems, False, True),
            ring_sum(ring, out_part, out_held, out_sum, *out_sems, False, True),
        )

        def turn():
            for _ in range(RING_PIECES):
                next(sums)

        late.need(1)
        nearest = count // 2 - 1
        compute(slice(2 * nearest - 1, 2 * nearest + 1))
        turn()
        compute(slice(count - 1, count))
        turn()
        for pair in range(nearest - 1, 0, -1):
            compute(slice(2 * pair - 1, 2 * pair + 1))
        compute(slice(0, 1))
        turn()
        weight_grads(hidden, grad_out, grad_w_out)
        weight_grads(rows_all, grad_mid, grad_w_in)
        yield from together(
            sums,
            shard_sum(ring, grad_w_in, outs[4], *grad_in_rest),
            shard_sum(ring, grad_w_out, outs[5], *grad_out_rest),
        )
        outs[0][...] = (middle[...] + out_sum[...]).astype(BF16)


def fold(block):
    half = block.shape[0] // 2
    return jnp.concatenate([block[:half], block[half:]], axis=1)


def unfold(block):
    half = block.shape[1] // 2
    return jnp.concatenate([block[:, :half], block[:, half:]], axis=0)


def swap_sems(count):
    return sems(count - 1, count - 1)


def swap(ring, sent, received, send_sem, recv_sem):
    _, peers = all_peers(ring)
    copies = [
        remote(sent.at[to[0]], received.at[ring.ctx], send_sem.at[i], recv_sem.at[i], to)
        for i, to in enumerate(peers)
    ]
    for copy in copies:
        copy.start()
    received[ring.ctx] = sent[ring.ctx]
    yield from idle(RING_PIECES)
    for copy in copies:
        copy.wait()


def small_sum_scratch(shape):
    count, shards = lax.axis_size("ctx"), lax.axis_size("fsdp")
    return [
        pltpu.VMEM((shards,) + shape, F32),
        pltpu.VMEM((count,) + shape, F32),
    ] + sems(shards - 1, shards - 1, count - 1, count - 1)


def small_sum(ring, small, total, near, far, near_send, near_recv, far_send, far_recv):
    siblings, peers = all_peers(ring)
    me, row = ring.fsdp, ring.ctx
    near[me] = small[...]
    first = [
        remote(small, near.at[me], near_send.at[i], near_recv.at[i], to)
        for i, to in enumerate(siblings)
    ]
    for copy in first:
        copy.start()
    yield from idle(RING_PIECES)
    for copy in first:
        copy.wait()
    far[row] = sum([near[i] for i in range(len(siblings) + 1)])
    second = [
        remote(far.at[row], far.at[row], far_send.at[i], far_recv.at[i], to)
        for i, to in enumerate(peers)
    ]
    for copy in second:
        copy.start()
    yield from idle(2 * RING_PIECES)
    for copy in second:
        copy.wait()
    total[...] = sum([far[i] for i in range(len(peers) + 1)])


class Attention:
    kinds = ("all",)

    def __init__(self, rows, heads, dim):
        self.rows, self.heads, self.dim = rows, heads, dim
        self.scaling = dim ** (-0.5)
        self.tall = min(256 if rows <= 1024 else 128, rows)

    def block(self, index):
        rows = slice(index * self.tall, (index + 1) * self.tall)
        return rows, (index + 1) * self.tall

    def allowed(self, rows, wide, info, across):
        shape = (self.tall, wide)
        here = lax.broadcasted_iota(jnp.int32, shape, 0) + rows.start
        there = lax.broadcasted_iota(jnp.int32, shape, 1)
        return (there <= here) & (info[rows, 24:25] == across[8:9, :wide])

    def part(self, qkv, which, head, rows):
        start = (which * self.heads + head) * self.dim
        return qkv[rows, start : start + self.dim]

    def scores(self, qkv, info, across, head, rows, wide, allowed):
        queries = self.part(qkv, 0, head, rows)
        keys = self.part(qkv, 1, head, slice(0, wide))
        scores = matmul_rows(queries, keys) * self.scaling
        scores = scores + info[rows, head : head + 1] - across[head : head + 1, :wide]
        return queries, keys, jnp.where(allowed, scores, NEGATIVE)


class Late:
    def __init__(self, arrays):
        self.count = len(arrays)
        self.scratch = [pltpu.VMEM(a.shape, a.dtype) for a in arrays]
        self.scratch += [pltpu.SemaphoreType.DMA((self.count,))]

    def start(self, refs, scratch):
        self.held, self.waiting = list(scratch[: self.count]), {}
        for i, ref in enumerate(refs):
            copy = pltpu.make_async_copy(ref, self.held[i], scratch[self.count].at[i])
            copy.start()
            self.waiting[i] = copy
        return self

    def need(self, *which):
        for i in which:
            if i in self.waiting:
                self.waiting.pop(i).wait()


class Early:
    def __init__(self, shapes):
        self.count = len(shapes)
        self.scratch = [pltpu.VMEM(a.shape, a.dtype) for a in shapes]
        self.scratch += [pltpu.SemaphoreType.DMA((self.count,))]

    def begin(self, refs, scratch):
        self.refs, self.held, self.sem = refs, list(scratch[: self.count]), scratch[self.count]
        self.leaving = []
        return self

    def ready(self, *which):
        for i in which:
            copy = pltpu.make_async_copy(self.held[i], self.refs[i], self.sem.at[i])
            copy.start()
            self.leaving.append(copy)

    def finish(self):
        for copy in self.leaving:
            copy.wait()


def split_refs(refs, sizes):
    groups, at = [], 0
    for size in sizes:
        groups.append(list(refs[at : at + size]))
        at += size
    return groups


EXACT = dict(preferred_element_type=F32, precision=lax.Precision.HIGHEST)


class Forward(Attention):
    def __init__(self, tokens, gain, cotangent, weights, w_out, bias, seg, heads, dim):
        count, shards = lax.axis_size("ctx"), lax.axis_size("fsdp")
        tall, width = tokens.shape
        rows = tall * count
        super().__init__(rows, heads, dim)
        hidden = heads * dim
        self.hidden = hidden
        self.whole = len(weights) > 1
        self.ins = [tokens, gain, bias, seg, cotangent, w_out] + list(weights)
        self.in_specs = [VMEM] * 4 + [ANYWHERE] * 2
        self.in_specs += [ANYWHERE] * 4 + [VMEM] if self.whole else [ANYWHERE]
        shard_rows = width // shards
        joined = (shard_rows, 4 * hidden + 128)
        window = hidden if hidden % 128 == 0 else hidden + 64
        everyone = jax.ShapeDtypeStruct((count, tall, width), BF16)
        self.outs = [
            everyone,
            everyone,
            jax.ShapeDtypeStruct((width, joined[1]), BF16),
            jax.ShapeDtypeStruct((width, width), BF16),
            jax.ShapeDtypeStruct((rows, 3 * hidden), BF16),
            jax.ShapeDtypeStruct((rows, hidden), F32),
            jax.ShapeDtypeStruct((rows, hidden), F32),
            jax.ShapeDtypeStruct((rows, 128), F32),
            jax.ShapeDtypeStruct((16, rows), F32),
            jax.ShapeDtypeStruct((tall, count * hidden), BF16),
        ]
        self.out_specs = [ANYWHERE] * 7 + [VMEM] * 3
        self.early = Early([self.outs[i] for i in (0, 2, 4, 5, 6)])
        ring = [pltpu.SemaphoreType.DMA] + ring_sems(count)
        swapped = pltpu.VMEM((count, tall // 2, 2 * hidden), BF16)
        groups = [
            ring,
            ring,
            shard_gather_sems(1),
            shard_gather_sems(1),
            [swapped, swapped] + swap_sems(count),
            self.early.scratch,
            [pltpu.VMEM((4, shard_rows, window), BF16), pltpu.VMEM(joined, BF16)] + sems(4),
            [pltpu.VMEM((8, 128), F32)],
        ]
        self.sizes = [len(group) for group in groups]
        self.scratch = sum(groups, [])

    def run(self, ring, ins, outs, scratch):
        rows_sems, cotangent_sems, mixed_sems, out_sems, swapping, held, joining, own_bias = (
            split_refs(scratch, self.sizes)
        )
        tokens, gain, bias, seg, cotangent, w_out, *weights = ins
        (bias_own,) = own_bias
        _, grad_out, _, full_out, _, _, _, info, across, gated = outs
        early = self.early.begin([outs[i] for i in (0, 2, 4, 5, 6)], held)
        normed, mixed_in, qkv, attended, gate = early.held
        sent, received = swapping[:2]
        count, tall, _ = normed.shape

        def filled_from(source):
            def fill(shard, local_sem):
                return [pltpu.make_async_copy(source, shard, local_sem.at[0])], source

            return fill

        def later(turns, walk):
            yield from idle(turns)
            yield from walk

        def main():
            fetched = self.fetch(ring, weights, *joining) if self.whole else []
            value = tokens[...].astype(F32)
            rstat = lax.rsqrt(jnp.mean(value * value, axis=1, keepdims=True) + EPSILON)
            normed[ring.ctx] = (value * rstat * gain[...].astype(F32)).astype(BF16)
            gather = ring_gather(ring, None, normed, *rows_sems, True)
            next(gather)
            mixed_shard = self.join(ring, weights, bias, bias_own, fetched, *joining[:2])
            yield from together(
                gather,
                shard_gather(ring, filled_from(mixed_shard), mixed_in, *mixed_sems),
            )
            early.ready(0, 1)
            self.project(normed, mixed_in, bias_own, qkv, gate, info)
            early.ready(2, 4)
            self.decay(info, across, seg)
            yield
            yield from self.attend(qkv, info, across, attended)
            early.ready(3)
            for i in range(count):
                rows = slice(i * tall, (i + 1) * tall)
                sent[i] = fold((attended[rows] * gate[rows]).astype(BF16))
            yield from swap(ring, *swapping)
            gated[...] = jnp.concatenate([unfold(received[i]) for i in range(count)], axis=1)

        turns = count // 2 * RING_PIECES
        yield from together(
            main(),
            later(turns - 1, ring_gather(ring, cotangent, grad_out, *cotangent_sems, False)),
            later(turns // 2, shard_gather(ring, filled_from(w_out), full_out, *out_sems)),
        )
        early.finish()

    def fetch(self, ring, weights, windows, joined, sem):
        start = pl.multiple_of(ring.ctx * self.hidden // 128 * 128, 128)
        copies = [
            pltpu.make_async_copy(
                weights[i].at[:, pl.ds(start, windows.shape[2])], windows.at[i], sem.at[i]
            )
            for i in range(4)
        ]
        for copy in copies:
            copy.start()
        return copies

    def join(self, ring, weights, bias, bias_own, fetched, windows, joined):
        heads, hidden = self.heads, self.hidden
        shape = (bias.shape[1], 128)
        head = lax.broadcasted_iota(jnp.int32, shape, 0)
        spot = lax.broadcasted_iota(jnp.int32, shape, 1)
        chosen = ((head == ring.ctx * heads + spot) & (spot < heads)).astype(F32)
        bias_own[...] = jnp.dot(
            jnp.broadcast_to(bias[...], (8, bias.shape[1])), chosen, **EXACT
        )
        if not self.whole:
            return weights[0]
        for copy in fetched:
            copy.wait()
        parts = []
        for i in range(4):
            part = windows[i, :, :hidden]
            if hidden % 128 != 0:
                shifted = windows[i, :, 64 : 64 + hidden]
                part = jnp.where(ring.ctx * hidden % 128 == 0, part, shifted)
            parts.append(part)
        parts.append(matmul(weights[4][...], chosen.astype(BF16)).astype(BF16))
        joined[...] = jnp.concatenate(parts, axis=1)
        return joined

    def project(self, normed, mixed_in, bias, qkv, gate, info):
        count, tall, width = normed.shape
        pair = 2 if count % 2 == 0 else 1
        hidden = self.hidden

        @pl.loop(0, count // pair)
        def _(index):
            block = normed[pl.ds(index * pair, pair)].reshape(pair * tall, width)
            rows = pl.ds(pl.multiple_of(index * pair * tall, pair * tall), pair * tall)
            mixed = matmul(block, mixed_in[...])
            qkv[rows] = mixed[:, : 3 * hidden].astype(BF16)
            gate[rows] = jax.nn.sigmoid(mixed[:, 3 * hidden : 4 * hidden])
            info[rows] = mixed[:, 4 * hidden : 4 * hidden + 128]
            info[rows, 8:16] = info[rows, 0:8] + bias[0:1, 0:8]

    def decay(self, info, across, seg):
        tall = 128
        here = lax.broadcasted_iota(jnp.int32, (tall, tall), 0)
        there = lax.broadcasted_iota(jnp.int32, (tall, tall), 1)
        wedge = (there <= here).astype(F32)
        before = jnp.zeros((1, 8), F32)
        pad = jnp.zeros((tall, 120), F32)
        across[8:9] = seg[...].astype(F32)
        for index in range(self.rows // tall):
            rows = slice(index * tall, (index + 1) * tall)
            info[rows, 24:25] = jnp.broadcast_to(across[8:9, rows], (tall, tall)).T[:, 0:1]
            logs = jax.nn.log_sigmoid(info[rows, 8:16])
            sums = jnp.dot(wedge, jnp.concatenate([logs, pad], axis=1), **EXACT)[:, :8] + before
            before = sums[tall - 1 :]
            info[rows, 0:8] = sums
            across[0:8, rows] = jnp.concatenate([sums, pad], axis=1).T[:8]

    def attend(self, qkv, info, across, attended):
        for index in range(self.rows // self.tall):
            rows, wide = self.block(index)
            allowed = self.allowed(rows, wide, info, across)
            mixed = []
            for head in range(self.heads):
                _, _, scores = self.scores(qkv, info, across, head, rows, wide, allowed)
                row_max = jnp.max(scores, axis=1, keepdims=True)
                raised = jnp.exp(scores - row_max)
                row_total = jnp.sum(raised, axis=1, keepdims=True)
                probabilities = (raised * (1.0 / row_total)).astype(BF16)
                mixed.append(matmul(probabilities, self.part(qkv, 2, head, slice(0, wide))))
                info[rows, 16 + head : 17 + head] = row_max + jnp.log(row_total)
                if head < self.heads - 1:
                    yield
            attended[rows] = jnp.concatenate(mixed, axis=1)
            yield


def slow(walk, turns):
    for _ in walk:
        yield from idle(turns)


class Backward(Attention):
    def __init__(self, own_heads, named):
        rows = named["qkv"].shape[0]
        super().__init__(rows, own_heads, named["qkv"].shape[1] // 3 // own_heads)
        self.names = list(named)
        hbm = ("gated", "grad_ffn_in")
        self.loaded = ("full_out", "qkv", "attended", "gate_value", "mixed_in", "normed")
        self.late = Late([named[name] for name in self.loaded])
        self.ins = [named[name] for name in self.names]
        self.in_specs = [
            ANYWHERE if name in hbm + self.loaded else VMEM for name in self.names
        ]
        count, shards = lax.axis_size("ctx"), lax.axis_size("fsdp")
        tall, width = named["gated"].shape
        hidden = own_heads * self.dim
        self.main = 4 * hidden
        both = -(-(5 * hidden + own_heads) // 128) * 128
        ffn = [named["grad_ffn_in"]]
        shard_rows = width // shards
        swapped = pltpu.VMEM((count, tall // 2, 2 * hidden), BF16)
        block = pltpu.VMEM((shards * tall, width), BF16)
        heads = pltpu.VMEM((self.rows, hidden), BF16)
        self.outs = (
            [jax.ShapeDtypeStruct((tall, width), F32)]
            + [jax.ShapeDtypeStruct((count,) + grad.shape, BF16) for grad in ffn]
            + [jax.ShapeDtypeStruct((count, shard_rows, both), BF16)]
            + [jax.ShapeDtypeStruct((8, width), F32)]
        )
        self.out_specs = [VMEM] + [ANYWHERE] * 2 + [VMEM]
        ring = [pltpu.SemaphoreType.DMA] + ring_sems(count)
        groups = [
            [pltpu.VMEM((3, own_heads, self.rows, self.dim), F32)],
            [pltpu.VMEM((self.rows, 128), F32), pltpu.VMEM((8, self.rows), F32)],
            [pltpu.VMEM((self.rows, self.main + 128), BF16)],
            [
                pltpu.VMEM((count, shard_rows, hidden), BF16),
                pltpu.VMEM((2, count // 2, shard_rows, hidden), BF16),
                pltpu.VMEM((shard_rows, hidden), F32),
            ]
            + ring_sems(count),
            [
                pltpu.VMEM((count, tall, width), BF16),
                pltpu.VMEM((2, count // 2, tall, width), BF16),
                pltpu.VMEM((tall, width), F32),
            ]
            + ring_sems(count),
            [
                pltpu.VMEM((shard_rows, both), BF16),
                pltpu.VMEM((width, self.main + 128), BF16),
                pltpu.VMEM((shard_rows, self.main + 128), BF16),
            ]
            + shard_sum_scratch(shard_rows, self.main + 128),
            ring,
            ring,
            ring,
            [pltpu.VMEM((8, width), F32)] + small_sum_scratch((8, width)),
            [pltpu.VMEM((tall, width), F32), pltpu.VMEM((tall, count * hidden), BF16)],
            [swapped, swapped] + swap_sems(count),
            [heads, heads],
            [block] + shard_gather_sems(1),
            [block] + shard_gather_sems(1),
            [pltpu.VMEM((tall, width), BF16), pltpu.VMEM((shards * tall, shard_rows), BF16)],
            self.late.scratch,
        ]
        self.sizes = [len(group) for group in groups]
        self.scratch = sum(groups, [])

    def run(self, ring, ins, outs, scratch):
        groups = split_refs(scratch, self.sizes)
        named = dict(zip(self.names, ins))
        late = self.late.start([named[name] for name in self.loaded], groups[16])
        named.update(zip(self.loaded, late.held))
        out_part, out_held, out_sum, *out_sems = groups[3]
        rows_part, rows_held, rows_sum, *rows_sems = groups[4]
        grad_mixed = groups[2][0]
        grads_all, grads_part, grads_sum, *grads_rest = groups[5]
        small, *small_rest = groups[9]
        named["grad_middle"], grad_gated = groups[10]
        named["grad_attn"], named["grad_gatelog"] = groups[12]
        gated_block, *gated_sems = groups[13]
        branch_block, *branch_sems = groups[14]
        branch, gated_columns = groups[15]
        count, tall, width = rows_part.shape

        def filled_from(source):
            def fill(shard, local_sem):
                return [pltpu.make_async_copy(source, shard, local_sem.at[0])], source

            return fill

        gather_gated = shard_gather(
            ring, filled_from(named["gated"]), gated_block, *gated_sems, turns=1
        )

        def main():
            next(gather_gated)
            next(gather_gated)
            late.need(0)
            self.branch_back(named, grad_gated, groups[11][0], branch, small)
            yield from together(
                swap(ring, *groups[11]),
                shard_gather(ring, filled_from(branch), branch_block, *branch_sems, turns=2),
                gather_gated,
            )
            late.need(1, 2, 3)
            self.gate_back(named, groups[11][1])
            self.out_grads(ring, gated_block, branch_block, gated_columns, out_part)
            yield from together(
                self.attention(named, *groups[0], *groups[1]),
                ring_sum(ring, out_part, out_held, out_sum, *out_sems, True),
            )
            self.join(ring, named, *groups[0], *groups[1], grad_mixed, small)
            block = 256 if width % 256 == 0 else width
            late.need(4)

            @pl.loop(0, width // block)
            def _(index):
                columns = pl.ds(pl.multiple_of(index * block, block), block)
                part = matmul_rows(grad_mixed[...], named["mixed_in"][columns])
                rows_part[:, :, columns] = part.astype(BF16).reshape(count, tall, block)

            yield from together(
                ring_sum(ring, rows_part, rows_held, rows_sum, *rows_sems, True),
                weights(),
            )

        def weights():
            yield from idle(RING_PIECES)
            late.need(5)
            self.weight_grads(named, grad_mixed, grads_part)
            yield from shard_sum(ring, grads_part, grads_sum, *grads_rest)
            tail = grads_all.shape[1] - self.main - out_sum.shape[1]
            grads_all[:, : self.main] = grads_sum[:, : self.main]
            grads_all[:, self.main :] = jnp.concatenate(
                [out_sum[...].astype(BF16), grads_sum[:, self.main : self.main + tail]], axis=1
            )

        yield from together(
            slow(ring_gather(ring, named["grad_ffn_in"], outs[1], *groups[6], True), 2),
            main(),
        )
        self.norm_back(named, rows_sum, outs[0], small)
        yield from together(
            ring_gather(ring, grads_all, outs[2], *groups[8], True),
            small_sum(ring, small, outs[3], *small_rest),
        )

    def branch_back(self, named, grad_gated, sent, branch, small):
        grad, normed = named["grad_normed_two"][...], named["normed_two"][...]
        small[...] = jnp.zeros_like(small)
        small[1:2] = jnp.sum(grad * normed, axis=0, keepdims=True)
        grad_normed = grad * named["gain_two"][...].astype(F32)
        inner = jnp.mean(grad_normed * normed, axis=1, keepdims=True)
        named["grad_middle"][...] = named["cotangent"][...].astype(F32) + named["rstat_two"][...] * (
            grad_normed - normed * inner
        )
        branch[...] = named["grad_middle"][...].astype(BF16)
        count, hidden = sent.shape[0], sent.shape[2] // 2
        width = grad.shape[1]
        block = 256 if width % 256 == 0 else width
        if grad_gated.shape[1] > width:
            grad_gated[...] = jnp.zeros_like(grad_gated)

        @pl.loop(0, width // block)
        def _(index):
            columns = pl.ds(pl.multiple_of(index * block, block), block)
            part = matmul_rows(branch[...], named["full_out"][columns])
            grad_gated[:, columns] = part.astype(BF16)

        for i in range(count):
            sent[i] = fold(grad_gated[:, i * hidden : (i + 1) * hidden])

    def gate_back(self, named, received):
        count, tall = received.shape[0], 2 * received.shape[1]
        for i in range(count):
            rows = slice(i * tall, (i + 1) * tall)
            grad = unfold(received[i]).astype(F32)
            gate = named["gate_value"][rows]
            named["grad_attn"][rows] = (grad * gate).astype(BF16)
            named["grad_gatelog"][rows] = (
                grad * named["attended"][rows] * (gate * (1.0 - gate))
            ).astype(BF16)

    def attention(self, named, grads, sums_rows, sums_columns):
        qkv, info, across, grad_attn = [
            named[name] for name in ("qkv", "info", "across", "grad_attn")
        ]
        grad_q, grad_k, grad_v = [grads.at[i] for i in range(3)]
        blocks = self.rows // self.tall
        sums_columns[...] = jnp.zeros_like(sums_columns)
        pad = jnp.zeros((self.tall, 128 - self.heads), F32)
        for index in reversed(range(blocks)):
            rows, wide = self.block(index)
            allowed = self.allowed(rows, wide, info, across)
            own = slice(0, wide)
            row_sums = []
            for head in range(self.heads):
                queries, keys, scores = self.scores(
                    qkv, info, across, head, rows, wide, allowed
                )
                probabilities = jnp.exp(scores - info[rows, 16 + head : 17 + head])
                grad_part = grad_attn[rows, head * self.dim : (head + 1) * self.dim]
                grad_probs = matmul_rows(grad_part, self.part(qkv, 2, head, own))
                row_inner = jnp.sum(probabilities * grad_probs, axis=1, keepdims=True)
                grad_scores = (probabilities * (grad_probs - row_inner)).astype(BF16)
                grad_q[head, rows] = matmul(grad_scores, keys) * self.scaling
                from_k = weight_grad(grad_scores, queries) * self.scaling
                from_v = weight_grad(probabilities.astype(BF16), grad_part)
                wide_sums = grad_scores.astype(F32)
                row_sums.append(jnp.sum(wide_sums, axis=1, keepdims=True))
                column_sums = jnp.sum(wide_sums, axis=0, keepdims=True)
                if index == blocks - 1:
                    grad_k[head], grad_v[head] = from_k, from_v
                    sums_columns[head : head + 1] = column_sums
                else:
                    grad_k[head, own] += from_k
                    grad_v[head, own] += from_v
                    sums_columns[head : head + 1, own] += column_sums
                if head < self.heads - 1:
                    yield
            sums_rows[rows] = jnp.concatenate(row_sums + [pad], axis=1)
            yield

    def join(self, ring, named, grads, sums_rows, sums_columns, grad_mixed, small):
        for index in range(self.rows // self.tall):
            rows, _ = self.block(index)
            grad_mixed[rows, : self.main] = jnp.concatenate(
                [grads[i, head, rows].astype(BF16) for i in range(3) for head in range(self.heads)]
                + [named["grad_gatelog"][rows]],
                axis=1,
            )
        tall = 128
        here = lax.broadcasted_iota(jnp.int32, (tall, tall), 0)
        there = lax.broadcasted_iota(jnp.int32, (tall, tall), 1)
        wedge = (here <= there).astype(F32)
        later, bias = jnp.zeros((1, 8), F32), jnp.zeros((1, 8), F32)
        pad = jnp.zeros((tall, 120), BF16)
        for index in reversed(range(self.rows // tall)):
            rows = slice(index * tall, (index + 1) * tall)
            inside = jnp.dot(wedge, sums_rows[rows], **EXACT)[:, :8] - lax.dot_general(
                wedge, sums_columns[:, rows], (((1,), (1,)), ((), ())), **EXACT
            )
            logits = named["info"][rows, 8:16]
            grad_logits = ((inside + later) * jax.nn.sigmoid(-logits)).astype(BF16)
            later = later + inside[:1]
            bias = bias + jnp.sum(grad_logits.astype(F32), axis=0, keepdims=True)
            grad_mixed[rows, self.main :] = jnp.concatenate([grad_logits, pad], axis=1)
        spot = lax.broadcasted_iota(jnp.int32, (1, small.shape[1]), 1)
        small[2:3] = sum(
            jnp.where(spot == ring.ctx * self.heads + head, bias[:, head : head + 1], 0.0)
            for head in range(self.heads)
        )

    def out_grads(self, ring, gated_block, branch_block, gated_columns, parts):
        count, rows, hidden = parts.shape
        for i in range(lax.axis_size("fsdp")):

            @pl.when(ring.fsdp == i)
            def _():
                gated_columns[...] = gated_block[:, i * rows : (i + 1) * rows]

        for i in range(count):
            stop = min((i + 1) * hidden, branch_block.shape[1])
            if stop > i * hidden:
                part = weight_grad(gated_columns[...], branch_block[:, i * hidden : stop])
                parts[i] = part.astype(BF16)
            else:
                parts[i] = jnp.zeros((rows, hidden), BF16)

    def weight_grads(self, named, grad_mixed, parts):
        count, tall, width = named["normed"].shape
        tile = 128

        @pl.loop(0, width // tile)
        def _(index):
            columns = pl.ds(pl.multiple_of(index * tile, tile), tile)
            normed = named["normed"][:, :, columns].reshape(count * tall, tile)
            parts[columns] = weight_grad(normed, grad_mixed[...]).astype(BF16)

    def norm_back(self, named, rows_sum, grad_tokens, small):
        grad, value = rows_sum[...], named["tokens"][...].astype(F32)
        rstat = lax.rsqrt(jnp.mean(value * value, axis=1, keepdims=True) + EPSILON)
        normed = value * rstat
        small[0:1] = jnp.sum(grad * normed, axis=0, keepdims=True)
        grad_normed = grad * named["gain_one"][...].astype(F32)
        inner = jnp.mean(grad_normed * normed, axis=1, keepdims=True)
        grad_tokens[...] = named["grad_middle"][...] + rstat * (
            grad_normed - normed * inner
        )


def exchange(ident, name, *tasks):
    count = lax.axis_size("ctx")

    def take(refs, sizes):
        groups, at = [], 0
        for size in sizes:
            groups.append(refs[at : at + size])
            at += size
        return groups

    ins = [len(task.ins) for task in tasks]
    outs = [len(task.outs) for task in tasks]
    scratch = [len(task.scratch) for task in tasks]

    def kernel(*refs):
        ring = Ring(count)
        kinds = sum([task.kinds for task in tasks], ())
        peers = []
        if "all" in kinds:
            peers = sum(all_peers(ring), [])
        else:
            if "ring" in kinds:
                peers += [ring.device(1), ring.device(-1)]
            if "shard" in kinds:
                pair, others = shard_pair(ring, lax.axis_size("fsdp"))
                peers += [(ring.ctx, to) for to in [pair] + others]
        greet(peers)
        groups = [
            take(refs[: sum(ins)], ins),
            take(refs[sum(ins) : sum(ins) + sum(outs)], outs),
            take(refs[sum(ins) + sum(outs) :], scratch),
        ]
        for _ in together(*[task.run(ring, *parts) for task, *parts in zip(tasks, *groups)]):
            pass

    results = pl.pallas_call(
        kernel,
        out_shape=sum([task.outs for task in tasks], []),
        in_specs=sum([task.in_specs for task in tasks], []),
        out_specs=sum([task.out_specs for task in tasks], []),
        scratch_shapes=sum([task.scratch for task in tasks], []),
        compiler_params=pltpu.CompilerParams(
            collective_id=ident, has_side_effects=True, vmem_limit_bytes=62 * 2**20
        ),
        cost_estimate=pl.CostEstimate(flops=0, bytes_accessed=100_000_000, transcendentals=0),
        name=name,
    )(*sum([task.ins for task in tasks], []))
    return take(list(results), outs)


def flat(blocks):
    return blocks.reshape(-1, blocks.shape[-1])


def permute_rows(value, beside):
    count, me = lax.axis_size("ctx"), lax.axis_index("ctx")
    order = [ring_index(place, count) for place in range(count)]
    rows, half = value.shape[0], value.shape[0] // 2
    ways = [[(order[i], order[(i + sign) % count]) for i in range(count)] for sign in (1, -1)]

    parts, offsets = [value], [0]
    blocks, results, beside = [value, value], [], list(beside)
    for hops in range(1, count // 2 + 1):
        work = None
        if hops > 1 and beside:
            work, operand = beside.pop(0)
            blocks[0], blocks[1], operand = lax.optimization_barrier((*blocks, operand))
        last = hops == count // 2
        sent = [blocks[0][:half], blocks[1][half:]] if last else blocks
        blocks = [lax.ppermute(block, "ctx", way) for block, way in zip(sent, ways)]
        if work is not None:
            result = work(operand)
            blocks[0], blocks[1], result = lax.optimization_barrier((*blocks, result))
            results.append(result)
        parts += blocks
        offsets += [-hops, hops]
    place = (ring_place(me, count) + jnp.asarray(offsets[:-1], jnp.int32) + count) % count
    return place_rows(parts, ring_index(place, count)), results


def place_rows(parts, sources):
    rows, width = parts[0].shape
    count = len(parts) - 1
    half = rows // 2

    def kernel(source_ref, *refs):
        ins, out = refs[:-1], refs[-1]
        step = pl.program_id(0)
        for j in range(count):

            @pl.when(step == j)
            def _():
                if j < count - 1:
                    out[...] = ins[j][...].astype(F32)
                else:
                    out[:half] = ins[j][...].astype(F32)
                    out[half:] = ins[j + 1][...].astype(F32)

    return pl.pallas_call(
        kernel,
        out_shape=jax.ShapeDtypeStruct((rows * count, width), F32),
        grid_spec=pltpu.PrefetchScalarGridSpec(
            num_scalar_prefetch=1,
            grid=(count,),
            in_specs=[pl.BlockSpec(part.shape, lambda i, _: (0, 0)) for part in parts],
            out_specs=pl.BlockSpec((rows, width), lambda i, source: (source[i], 0)),
        ),
        compiler_params=pltpu.CompilerParams(vmem_limit_bytes=60 * 2**20),
        cost_estimate=pl.CostEstimate(
            flops=0, bytes_accessed=rows * width * count * 6, transcendentals=0
        ),
        name="place_rows",
    )(sources, *parts)


def ffn_columns(blocks, n_fsdp):
    count, rows, both = blocks.shape
    width, piece = both // 2, both // 2 // n_fsdp
    steps = 4
    tall = rows // steps

    def kernel(block_ref, *outs):
        for j in range(count):
            for half in range(2):
                for group in range(n_fsdp):
                    start, to = half * width + group * piece, (group * count + j) * piece
                    outs[half][:, to : to + piece] = block_ref[j, :, start : start + piece].astype(F32)

    wide = jax.ShapeDtypeStruct((rows, width * count), F32)
    spec = pl.BlockSpec((tall, width * count), lambda i: (i, 0))
    return pl.pallas_call(
        kernel,
        out_shape=(wide, wide),
        grid=(steps,),
        in_specs=[pl.BlockSpec((count, tall, both), lambda i: (0, i, 0))],
        out_specs=(spec, spec),
        compiler_params=pltpu.CompilerParams(vmem_limit_bytes=40 * 2**20),
        cost_estimate=pl.CostEstimate(
            flops=0, bytes_accessed=rows * both * count * 6, transcendentals=0
        ),
        name="ffn_columns",
    )(blocks)


def head_columns(blocks, sizes, widths):
    count, rows, total = blocks.shape
    steps = 4
    tall = rows // steps
    starts = [sum(sizes[:i]) for i in range(len(sizes))]

    def kernel(block_ref, *outs):
        for start, size, out in zip(starts, sizes, outs):
            for i in range(0, count, 2):
                pair = jnp.concatenate(
                    [block_ref[i + k][:, start : start + size].astype(F32) for k in range(2)], axis=1
                )
                at = i * size
                keep = min(2 * size, out.shape[1] - at)
                if keep > 0:
                    out[:, at : at + keep] = pair[:, :keep]

    return pl.pallas_call(
        kernel,
        out_shape=tuple(jax.ShapeDtypeStruct((rows, w), F32) for w in widths),
        grid=(steps,),
        in_specs=[pl.BlockSpec((count, tall, total), lambda i: (0, i, 0))],
        out_specs=tuple(pl.BlockSpec((tall, w), lambda i: (i, 0)) for w in widths),
        compiler_params=pltpu.CompilerParams(vmem_limit_bytes=40 * 2**20),
        cost_estimate=pl.CostEstimate(
            flops=0, bytes_accessed=count * rows * total * 6, transcendentals=0
        ),
        name="head_columns",
    )(blocks)


def shards(
    tokens,
    segments,
    gain_attn,
    w_query,
    w_key,
    w_value,
    w_forget,
    forget_bias,
    w_outgate,
    w_out,
    gain_ffn,
    w_gate,
    w_up,
    w_down,
    cotangent,
):
    n_ctx, me = lax.axis_size("ctx"), lax.axis_index("ctx")
    n_fsdp = lax.axis_size("fsdp")
    tok_rows, width = tokens.shape[1:]
    seq_rows = tok_rows * n_ctx
    n_heads = forget_bias.shape[0]
    head_dim = width // n_heads
    own_heads = -(-n_heads // n_ctx)
    own_width = own_heads * head_dim
    padded = own_width * n_ctx
    ffn_rows = w_down.shape[0]
    ffn_piece = ffn_rows // n_ctx
    ffn_width = ffn_piece * n_fsdp
    shard_rows = w_query.shape[0]

    def widen(value, size):
        return jnp.pad(value, ((0, 0), (0, size - value.shape[1])))

    def own_columns(weight, size):
        return lax.dynamic_slice_in_dim(widen(weight, size * n_ctx), me * size, size, 1)

    def own_ffn(weight):
        return [
            lax.dynamic_slice_in_dim(weight, (group * n_ctx + me) * ffn_piece, ffn_piece, 1)
            for group in range(n_fsdp)
        ]

    weights = [w_query, w_key, w_value, w_outgate, w_forget]
    if padded != width or own_width % 64 != 0:
        columns = [own_columns(w, own_width) for w in weights[:4]]
        columns.append(widen(own_columns(w_forget, own_heads), 128))
        weights = [jnp.concatenate(columns, axis=1)]
    gain_one, gain_two = gain_attn[None], gain_ffn[None]
    (
        (
            normed,
            grad_out_low,
            mixed_in,
            full_out,
            qkv,
            attended,
            gate_value,
            info,
            across,
            gated,
        ),
    ) = exchange(
        0,
        "forward",
        Forward(
            tokens[0],
            gain_one,
            cotangent[0],
            weights,
            w_out,
            forget_bias[None],
            segments,
            own_heads,
            head_dim,
        ),
    )
    w_in = [w_gate, w_up]
    if ffn_piece % 128 != 0:
        w_in = [jnp.concatenate(own_ffn(w_gate) + own_ffn(w_up), axis=1)]
    ((output, grad_normed_two, normed_two, rstat_two, grad_ffn_in, grad_ffn_out),) = exchange(
        1,
        "ffn",
        Ffn(tokens[0], gated, full_out, gain_two, grad_out_low, w_in, w_down, ffn_piece),
    )
    ((grad_inputs, spread_ffn_in, spread_attn, small),) = exchange(
        2,
        "backward",
        Backward(
            own_heads,
            {
                "qkv": qkv,
                "info": info,
                "across": across,
                "attended": attended,
                "gate_value": gate_value,
                "grad_normed_two": grad_normed_two,
                "normed_two": normed_two,
                "rstat_two": rstat_two,
                "gain_two": gain_two,
                "cotangent": cotangent[0],
                "full_out": full_out,
                "gated": gated[:, :width],
                "grad_ffn_in": grad_ffn_in,
                "normed": normed,
                "mixed_in": mixed_in,
                "tokens": tokens[0],
                "gain_one": gain_one,
            },
        ),
    )
    sizes = [own_width] * 5 + [own_heads]

    def place_ffn(blocks):
        if ffn_piece % 128 == 0:
            return ffn_columns(blocks, n_fsdp)
        whole = blocks.reshape(n_ctx, shard_rows, 2, n_fsdp, ffn_piece)
        whole = jnp.transpose(whole, (2, 1, 3, 0, 4)).reshape(2, shard_rows, -1).astype(F32)
        return whole[0], whole[1]

    def place_heads(blocks):
        return head_columns(blocks, sizes, [width] * 5 + [n_heads])

    grad_down, ((grad_gate, grad_up), grad_weights) = permute_rows(
        grad_ffn_out, [(place_ffn, spread_ffn_in), (place_heads, spread_attn)]
    )
    return (
        output[None],
        grad_inputs[None],
        small[0],
        grad_weights[0],
        grad_weights[1],
        grad_weights[2],
        grad_weights[5],
        small[2, :n_heads],
        grad_weights[3],
        grad_weights[4],
        small[1],
        grad_gate,
        grad_up,
        grad_down,
    )


def solution(mesh):
    rows, blocks = P("fsdp", None), P("fsdp", "ctx", None)
    return jax.shard_map(
        shards,
        mesh=mesh,
        in_specs=(blocks, rows, P())
        + (rows,) * 4
        + (P(), rows, rows, P(), rows, rows, rows, blocks),
        out_specs=(blocks, blocks, P())
        + (rows,) * 4
        + (P(), rows, rows, P(), rows, rows, rows),
        check_vma=False,
    )
```

```python
import jax
import jax.numpy as jnp
from jax import lax
from jax.experimental import pallas as pl
from jax.experimental.pallas import tpu as pltpu
from jax.sharding import PartitionSpec as P

EPSILON = 1e-06
NEGATIVE = -1e30
BF16, F32 = jnp.bfloat16, jnp.float32


def matmul(left, right):
    return jnp.dot(left, right, preferred_element_type=F32)


def matmul_rows(left, right):
    return lax.dot_general(left, right, (((1,), (1,)), ((), ())), preferred_element_type=F32)


def weight_grad(left, right):
    return lax.dot_general(left, right, (((0,), (0,)), ((), ())), preferred_element_type=F32)


MESH = pl.DeviceIdType.MESH
RING_PIECES = 4


def ring_place(ctx, count):
    odd = ctx % 2
    return ctx // 2 + odd * (count - 1 - 2 * (ctx // 2))


def ring_index(place, count):
    back = place // (count // 2)
    return 2 * place + back * (2 * (count - 1 - place) + 1 - 2 * place)


class Ring:
    def __init__(self, count):
        self.count, self.half = count, count // 2
        self.ctx, self.fsdp = lax.axis_index("ctx"), lax.axis_index("fsdp")
        self.place = ring_place(self.ctx, count)

    def at(self, offset):
        return ring_index((self.place + offset + self.count) % self.count, self.count)

    def device(self, offset):
        return (self.at(offset), self.fsdp)


def greet(devices):
    barrier = pltpu.get_barrier_semaphore()
    for device in devices:
        pl.semaphore_signal(barrier, inc=1, device_id=device, device_id_type=MESH)
    pl.semaphore_wait(barrier, len(devices))


def remote(src, dst, send, recv, device):
    return pltpu.make_async_remote_copy(
        src_ref=src, dst_ref=dst, send_sem=send, recv_sem=recv, device_id=device, device_id_type=MESH
    )


def carried(step, half, pieces, way):
    if step < half - 1:
        return range(pieces)
    return range(pieces // 2) if way == 0 else range(pieces // 2, pieces)


def ring_slot(ring, offset, absolute):
    if absolute:
        return ring.at(offset)
    if abs(offset) == ring.half:
        return ring.count - 1
    return 2 * offset - 1 if offset > 0 else -2 * offset


def ring_gather(ring, own, full, local_sem, send_sem, recv_sem, absolute, pieces=RING_PIECES):
    rows = full.shape[1] // pieces

    def part(k):
        return pl.ds(k * rows, rows)

    def slot(offset):
        return ring_slot(ring, offset, absolute)

    keep = None
    if own is None:
        own = full.at[slot(0)]
    else:
        keep = pltpu.make_async_copy(own, full.at[slot(0)], local_sem)
        keep.start()
    copies = {}
    for step in range(ring.half):
        for k in range(pieces):
            for way, sign in ((0, 1), (1, -1)):
                if step > 0:
                    copies[step - 1, k, way].wait_recv()
                if k not in carried(step, ring.half, pieces, way):
                    continue
                src = own.at[part(k)] if step == 0 else full.at[slot(-sign * step), part(k)]
                to = slot(-sign * step if absolute else -sign * (step + 1))
                copy = remote(
                    src,
                    full.at[to, part(k)],
                    send_sem.at[step, k, way],
                    recv_sem.at[step, k, way],
                    ring.device(sign),
                )
                copy.start()
                copies[step, k, way] = copy
            yield
    for (step, _, _), copy in copies.items():
        if step == ring.half - 1:
            copy.wait_recv()
    for copy in copies.values():
        copy.wait_send()
    if keep is not None:
        keep.wait()


def ring_sum(
    ring, parts, held, total, send_sem, recv_sem, absolute, ahead=False, pieces=RING_PIECES
):
    rows = parts.shape[1] // pieces

    def place(offset):
        return ring_slot(ring, offset, absolute)

    def part(k):
        return pl.ds(k * rows, rows)

    copies = {}

    def send(step, k, way, sign):
        src = parts.at[place(sign * (ring.half - step)), part(k)]
        if (step - 1, k, way) in copies:
            copies[step - 1, k, way].wait_recv()
            slot = held.at[way, step - 1, part(k)]
            slot[...] = (slot[...].astype(F32) + src[...].astype(F32)).astype(BF16)
            src = slot
        copy = remote(
            src,
            held.at[way, step, part(k)],
            send_sem.at[step, k, way],
            recv_sem.at[step, k, way],
            ring.device(sign),
        )
        copy.start()
        copies[step, k, way] = copy

    def farthest(k, way):
        return k in carried(ring.half - 1, ring.half, pieces, way)

    for step in ([None] if ahead else []) + list(range(ring.half)):
        for k in range(pieces):
            for way, sign in ((0, 1), (1, -1)):
                if step is None and not farthest(k, way):
                    send(1, k, way, sign)
                elif step == 0 and farthest(k, way):
                    send(0, k, way, sign)
                elif step == 1 and (farthest(k, way) or not ahead):
                    send(1, k, way, sign)
                elif step is not None and step > 1:
                    send(step, k, way, sign)
            yield
    last = ring.half - 1
    for k in range(pieces):
        for way in range(2):
            copies[last, k, way].wait_recv()
        total[part(k)] = (
            parts[place(0), part(k)].astype(F32)
            + held[0, last, part(k)].astype(F32)
            + held[1, last, part(k)].astype(F32)
        )
    for copy in copies.values():
        copy.wait_send()


def ring_sems(count, pieces=RING_PIECES):
    shape = (count // 2, pieces, 2)
    return [pltpu.SemaphoreType.DMA(shape), pltpu.SemaphoreType.DMA(shape)]


def sems(*counts):
    return [pltpu.SemaphoreType.DMA((max(count, 1),)) for count in counts]


ANYWHERE, VMEM = pl.BlockSpec(memory_space=pl.ANY), pl.BlockSpec(memory_space=pltpu.VMEM)


def shard_pair(ring, shards):
    me = ring.fsdp
    pair = me + 1 - 2 * (me % 2)
    return pair, [(me + 2 * hop) % shards for hop in range(1, shards // 2)]


def all_peers(ring):
    count, shards = lax.axis_size("ctx"), lax.axis_size("fsdp")
    siblings = [(ring.ctx, (ring.fsdp + hop) % shards) for hop in range(1, shards)]
    return siblings, [((ring.ctx + hop) % count, ring.fsdp) for hop in range(1, count)]


def idle(turns):
    for _ in range(turns):
        yield


def together(*walks):
    walks = list(walks)
    while walks:
        walks = [walk for walk in walks if next(walk, walks) is None]
        yield


def shard_gather(ring, fill, whole, local_sem, send_sem, recv_sem, turns=3 * RING_PIECES):
    shards, me = lax.axis_size("fsdp"), ring.fsdp
    rows = whole.shape[0] // shards
    pair, others = shard_pair(ring, shards)

    def shard(index):
        return whole.at[pl.ds(pl.multiple_of(index * rows, rows), rows)]

    local, source = fill(shard(me), local_sem)
    for copy in local:
        copy.start()
    yield
    if source is None:
        for copy in local:
            copy.wait()
    sent = shard(me) if source is None else source
    copies = [
        remote(sent, shard(me), send_sem.at[i], recv_sem.at[i], (ring.ctx, to))
        for i, to in enumerate([pair] + others)
    ]
    for copy in copies:
        copy.start()
    yield from idle(turns)
    passed = []
    for i in range(1, len(copies)):
        copies[i].wait_recv()
        origin = (me - 2 * i + shards) % shards
        at = shards // 2 - 1 + i
        copy = remote(
            shard(origin), shard(origin), send_sem.at[at], recv_sem.at[at], (ring.ctx, pair)
        )
        copy.start()
        passed.append(copy)
    yield from idle(2)
    copies[0].wait_recv()
    for copy in passed:
        copy.wait_recv()
    for copy in copies + passed:
        copy.wait_send()
    if source is not None:
        for copy in local:
            copy.wait()


def shard_gather_sems(parts):
    shards = lax.axis_size("fsdp")
    return sems(parts, shards - 1, shards - 1)


def shard_sum(ring, parts, total, near, far, near_send, near_recv, far_send, far_recv):
    shards, me = lax.axis_size("fsdp"), ring.fsdp
    half, core, chip = shards // 2, me % 2, me // 2
    pair, others = shard_pair(ring, shards)
    rows = parts.shape[0] // shards

    def shard(index):
        return pl.ds(pl.multiple_of(index * rows, rows), rows)

    first = [
        remote(
            parts.at[shard(2 * i + 1 - core)],
            near.at[i],
            near_send.at[i],
            near_recv.at[i],
            (ring.ctx, pair),
        )
        for i in range(half)
    ]
    for copy in first:
        copy.start()
    yield from idle(2)
    for copy in first:
        copy.wait_recv()
    second = []
    for hop in range(1, half):
        to = (chip + hop) % half
        near[to] = (near[to].astype(F32) + parts[shard(2 * to + core)].astype(F32)).astype(BF16)
        copy = remote(
            near.at[to],
            far.at[hop - 1],
            far_send.at[hop - 1],
            far_recv.at[hop - 1],
            (ring.ctx, others[hop - 1]),
        )
        copy.start()
        second.append(copy)
    yield from idle(3 * RING_PIECES)
    sums = parts[shard(me)].astype(F32) + near[chip].astype(F32)
    for hop, copy in enumerate(second):
        copy.wait_recv()
        sums = sums + far[hop].astype(F32)
    total[...] = sums.astype(BF16)
    for copy in first + second:
        copy.wait_send()


def shard_sum_scratch(rows, width):
    half = lax.axis_size("fsdp") // 2
    return [
        pltpu.VMEM((half, rows, width), BF16),
        pltpu.VMEM((max(half - 1, 1), rows, width), BF16),
    ] + sems(half, half, half - 1, half - 1)


class Ffn:
    kinds = ("ring", "shard")

    def __init__(self, tokens, gated, full_out, gain, grad_out, w_in, w_out, piece):
        count, shards = lax.axis_size("ctx"), lax.axis_size("fsdp")
        rows, width = tokens.shape
        self.aligned = len(w_in) == 2
        self.piece, self.inner = piece, piece * shards
        inner, both = self.inner, 2 * self.inner
        shard_rows = width // shards
        self.ins = [grad_out, tokens, gated, full_out, gain, w_out] + list(w_in)
        self.in_specs = [ANYWHERE, VMEM, VMEM, ANYWHERE, VMEM] + [ANYWHERE] * (1 + len(w_in))
        self.late = Late([full_out, grad_out])
        self.outs = [
            jax.ShapeDtypeStruct((rows, width), BF16),
            jax.ShapeDtypeStruct((rows, width), F32),
            jax.ShapeDtypeStruct((rows, width), F32),
            jax.ShapeDtypeStruct((rows, 1), F32),
            jax.ShapeDtypeStruct((shard_rows, both), BF16),
            jax.ShapeDtypeStruct((piece, width), BF16),
        ]
        self.out_specs = [VMEM] * 6
        held = pltpu.VMEM((2, count // 2, rows, width), BF16)
        groups = [
            [pltpu.VMEM((count, rows, width), BF16), pltpu.SemaphoreType.DMA] + ring_sems(count),
            [pltpu.VMEM((width, both), BF16)] + shard_gather_sems(2 * shards),
            [pltpu.VMEM((inner, width), BF16)] + shard_gather_sems(1),
            [pltpu.VMEM((count, rows, inner), BF16), pltpu.VMEM((count, rows, both), BF16)],
            [pltpu.VMEM((count, rows, width), BF16), held] + ring_sems(count),
            [pltpu.VMEM((count, rows, width), BF16), held] + ring_sems(count),
            [pltpu.VMEM((width, both), BF16)] + shard_sum_scratch(shard_rows, both),
            [pltpu.VMEM((inner, width), BF16)] + shard_sum_scratch(piece, width),
            [
                pltpu.VMEM((rows, width), F32),
                pltpu.VMEM((rows, width), BF16),
                pltpu.VMEM((rows, width), F32),
            ],
            self.late.scratch,
        ]
        self.sizes = [len(group) for group in groups]
        self.scratch = sum(groups, [])

    def run(self, ring, ins, outs, scratch):
        _, tokens, gated, _, gain, w_out_rows = ins[:6]
        w_in_rows = ins[6:]
        inner, piece = self.inner, self.piece
        groups = split_refs(scratch, self.sizes)
        late = self.late.start([ins[3], ins[0]], groups[9])
        full_out, grad_out = late.held
        (rows_all, *rows_sems), (w_in, *w_in_sems), (w_out, *w_out_sems) = groups[:3]
        hidden, grad_mid = groups[3]
        (out_part, out_held, *out_sems), (in_part, in_held, *in_sems) = groups[4:6]
        (grad_w_in, *grad_in_rest), (grad_w_out, *grad_out_rest) = groups[6:8]
        middle, normed, out_sum = groups[8]
        count, tall = rows_all.shape[:2]
        width = rows_all.shape[2]

        def fill_in(shard, local_sem):
            if not self.aligned:
                return [pltpu.make_async_copy(w_in_rows[0], shard, local_sem.at[0])], w_in_rows[0]
            copies = []
            for i in range(2):
                for group in range(inner // piece):
                    at = i * (inner // piece) + group
                    start = pl.multiple_of((group * count + ring.ctx) * piece, piece)
                    copies.append(
                        pltpu.make_async_copy(
                            w_in_rows[i].at[:, pl.ds(start, piece)],
                            shard.at[:, pl.ds(at * piece, piece)],
                            local_sem.at[at],
                        )
                    )
            return copies, None

        def fill_out(shard, local_sem):
            start = pl.multiple_of(ring.ctx * piece, piece)
            own = w_out_rows.at[pl.ds(start, piece)]
            return [pltpu.make_async_copy(own, shard, local_sem.at[0])], own

        def compute(slots):
            size = (slots.stop - slots.start) * tall

            def load(ref):
                return ref[slots].reshape(size, ref.shape[2])

            def store(ref, columns, value):
                ref[slots, :, columns] = value.astype(BF16).reshape(-1, tall, value.shape[1])

            tile = min(256, inner)

            @pl.loop(0, inner // tile)
            def _(index):
                def columns(start):
                    return pl.ds(pl.multiple_of(start + index * tile, tile), tile)

                gate = matmul(load(rows_all), w_in[:, columns(0)])
                up = matmul(load(rows_all), w_in[:, columns(inner)])
                grad_hidden = matmul_rows(load(grad_out), w_out[columns(0)])
                sig = jax.nn.sigmoid(gate)
                silu = gate * sig
                store(hidden, columns(0), silu * up)
                store(
                    grad_mid, columns(0), grad_hidden * up * (sig * (1.0 + gate * (1.0 - sig)))
                )
                store(grad_mid, columns(inner), grad_hidden * silu)

            wide = 256 if width % 256 == 0 else width

            @pl.loop(0, width // wide)
            def _(index):
                columns = pl.ds(pl.multiple_of(index * wide, wide), wide)
                store(in_part, columns, matmul_rows(load(grad_mid), w_in[columns]))
                store(out_part, columns, matmul(load(hidden), w_out[:, columns]))

        def weight_grads(left, right, grads):
            tile = 128 if left.shape[2] % 128 == 0 else left.shape[2]

            @pl.loop(0, left.shape[2] // tile)
            def _(index):
                columns = pl.ds(pl.multiple_of(index * tile, tile), tile)
                grads[columns] = weight_grad(
                    left[:, :, columns].reshape(count * tall, tile),
                    right[...].reshape(count * tall, right.shape[2]),
                ).astype(BF16)

        def first():
            block = 256 if width % 256 == 0 else width
            late.need(0)

            @pl.loop(0, width // block)
            def _(index):
                columns = pl.ds(pl.multiple_of(index * block, block), block)
                middle[:, columns] = tokens[:, columns].astype(F32) + matmul(
                    gated[:, :width], full_out[:, columns]
                )

            value = middle[...]
            rstat = lax.rsqrt(jnp.mean(value * value, axis=1, keepdims=True) + EPSILON)
            outs[2][...] = value * rstat
            outs[3][...] = rstat
            normed[...] = (outs[2][...] * gain[...].astype(F32)).astype(BF16)

        weights = together(
            shard_gather(ring, fill_in, w_in, *w_in_sems),
            shard_gather(ring, fill_out, w_out, *w_out_sems),
        )
        next(weights)
        next(weights)
        first()
        yield from together(weights, ring_gather(ring, normed, rows_all, *rows_sems, False))
        sums = together(
            ring_sum(ring, in_part, in_held, outs[1], *in_sems, False, True),
            ring_sum(ring, out_part, out_held, out_sum, *out_sems, False, True),
        )

        def turn():
            for _ in range(RING_PIECES):
                next(sums)

        late.need(1)
        nearest = count // 2 - 1
        compute(slice(2 * nearest - 1, 2 * nearest + 1))
        turn()
        compute(slice(count - 1, count))
        turn()
        for pair in range(nearest - 1, 0, -1):
            compute(slice(2 * pair - 1, 2 * pair + 1))
        compute(slice(0, 1))
        turn()
        weight_grads(hidden, grad_out, grad_w_out)
        weight_grads(rows_all, grad_mid, grad_w_in)
        yield from together(
            sums,
            shard_sum(ring, grad_w_in, outs[4], *grad_in_rest),
            shard_sum(ring, grad_w_out, outs[5], *grad_out_rest),
        )
        outs[0][...] = (middle[...] + out_sum[...]).astype(BF16)


def fold(block):
    half = block.shape[0] // 2
    return jnp.concatenate([block[:half], block[half:]], axis=1)


def unfold(block):
    half = block.shape[1] // 2
    return jnp.concatenate([block[:, :half], block[:, half:]], axis=0)


def swap_sems(count):
    return sems(count - 1, count - 1)


def swap(ring, sent, received, send_sem, recv_sem):
    _, peers = all_peers(ring)
    copies = [
        remote(sent.at[to[0]], received.at[ring.ctx], send_sem.at[i], recv_sem.at[i], to)
        for i, to in enumerate(peers)
    ]
    for copy in copies:
        copy.start()
    received[ring.ctx] = sent[ring.ctx]
    yield from idle(RING_PIECES)
    for copy in copies:
        copy.wait()


def small_sum_scratch(shape):
    count, shards = lax.axis_size("ctx"), lax.axis_size("fsdp")
    return [
        pltpu.VMEM((shards,) + shape, F32),
        pltpu.VMEM((count,) + shape, F32),
    ] + sems(shards - 1, shards - 1, count - 1, count - 1)


def small_sum(ring, small, total, near, far, near_send, near_recv, far_send, far_recv):
    siblings, peers = all_peers(ring)
    me, row = ring.fsdp, ring.ctx
    near[me] = small[...]
    first = [
        remote(small, near.at[me], near_send.at[i], near_recv.at[i], to)
        for i, to in enumerate(siblings)
    ]
    for copy in first:
        copy.start()
    yield from idle(RING_PIECES)
    for copy in first:
        copy.wait()
    far[row] = sum([near[i] for i in range(len(siblings) + 1)])
    second = [
        remote(far.at[row], far.at[row], far_send.at[i], far_recv.at[i], to)
        for i, to in enumerate(peers)
    ]
    for copy in second:
        copy.start()
    yield from idle(2 * RING_PIECES)
    for copy in second:
        copy.wait()
    total[...] = sum([far[i] for i in range(len(peers) + 1)])


class Attention:
    kinds = ("all",)

    def __init__(self, rows, heads, dim):
        self.rows, self.heads, self.dim = rows, heads, dim
        self.scaling = dim ** (-0.5)
        self.tall = min(256 if rows <= 1024 else 128, rows)

    def block(self, index):
        rows = slice(index * self.tall, (index + 1) * self.tall)
        return rows, (index + 1) * self.tall

    def allowed(self, rows, wide, info, across):
        shape = (self.tall, wide)
        here = lax.broadcasted_iota(jnp.int32, shape, 0) + rows.start
        there = lax.broadcasted_iota(jnp.int32, shape, 1)
        return (there <= here) & (info[rows, 24:25] == across[8:9, :wide])

    def part(self, qkv, which, head, rows):
        start = (which * self.heads + head) * self.dim
        return qkv[rows, start : start + self.dim]

    def scores(self, qkv, info, across, head, rows, wide, allowed):
        queries = self.part(qkv, 0, head, rows)
        keys = self.part(qkv, 1, head, slice(0, wide))
        scores = matmul_rows(queries, keys) * self.scaling
        scores = scores + info[rows, head : head + 1] - across[head : head + 1, :wide]
        return queries, keys, jnp.where(allowed, scores, NEGATIVE)


class Late:
    def __init__(self, arrays):
        self.count = len(arrays)
        self.scratch = [pltpu.VMEM(a.shape, a.dtype) for a in arrays]
        self.scratch += [pltpu.SemaphoreType.DMA((self.count,))]

    def start(self, refs, scratch):
        self.held, self.waiting = list(scratch[: self.count]), {}
        for i, ref in enumerate(refs):
            copy = pltpu.make_async_copy(ref, self.held[i], scratch[self.count].at[i])
            copy.start()
            self.waiting[i] = copy
        return self

    def need(self, *which):
        for i in which:
            if i in self.waiting:
                self.waiting.pop(i).wait()


class Early:
    def __init__(self, shapes):
        self.count = len(shapes)
        self.scratch = [pltpu.VMEM(a.shape, a.dtype) for a in shapes]
        self.scratch += [pltpu.SemaphoreType.DMA((self.count,))]

    def begin(self, refs, scratch):
        self.refs, self.held, self.sem = refs, list(scratch[: self.count]), scratch[self.count]
        self.leaving = []
        return self

    def ready(self, *which):
        for i in which:
            copy = pltpu.make_async_copy(self.held[i], self.refs[i], self.sem.at[i])
            copy.start()
            self.leaving.append(copy)

    def finish(self):
        for copy in self.leaving:
            copy.wait()


def split_refs(refs, sizes):
    groups, at = [], 0
    for size in sizes:
        groups.append(list(refs[at : at + size]))
        at += size
    return groups


EXACT = dict(preferred_element_type=F32, precision=lax.Precision.HIGHEST)


class Forward(Attention):
    def __init__(self, tokens, gain, cotangent, weights, w_out, bias, seg, heads, dim):
        count, shards = lax.axis_size("ctx"), lax.axis_size("fsdp")
        tall, width = tokens.shape
        rows = tall * count
        super().__init__(rows, heads, dim)
        hidden = heads * dim
        self.hidden = hidden
        self.whole = len(weights) > 1
        self.ins = [tokens, gain, bias, seg, cotangent, w_out] + list(weights)
        self.in_specs = [VMEM] * 4 + [ANYWHERE] * 2
        self.in_specs += [ANYWHERE] * 4 + [VMEM] if self.whole else [ANYWHERE]
        shard_rows = width // shards
        joined = (shard_rows, 4 * hidden + 128)
        window = hidden if hidden % 128 == 0 else hidden + 64
        everyone = jax.ShapeDtypeStruct((count, tall, width), BF16)
        self.outs = [
            everyone,
            everyone,
            jax.ShapeDtypeStruct((width, joined[1]), BF16),
            jax.ShapeDtypeStruct((width, width), BF16),
            jax.ShapeDtypeStruct((rows, 3 * hidden), BF16),
            jax.ShapeDtypeStruct((rows, hidden), F32),
            jax.ShapeDtypeStruct((rows, hidden), F32),
            jax.ShapeDtypeStruct((rows, 128), F32),
            jax.ShapeDtypeStruct((16, rows), F32),
            jax.ShapeDtypeStruct((tall, count * hidden), BF16),
        ]
        self.out_specs = [ANYWHERE] * 7 + [VMEM] * 3
        self.early = Early([self.outs[i] for i in (0, 2, 4, 5, 6)])
        ring = [pltpu.SemaphoreType.DMA] + ring_sems(count)
        swapped = pltpu.VMEM((count, tall // 2, 2 * hidden), BF16)
        groups = [
            ring,
            ring,
            shard_gather_sems(1),
            shard_gather_sems(1),
            [swapped, swapped] + swap_sems(count),
            self.early.scratch,
            [pltpu.VMEM((4, shard_rows, window), BF16), pltpu.VMEM(joined, BF16)] + sems(4),
            [pltpu.VMEM((8, 128), F32)],
        ]
        self.sizes = [len(group) for group in groups]
        self.scratch = sum(groups, [])

    def run(self, ring, ins, outs, scratch):
        rows_sems, cotangent_sems, mixed_sems, out_sems, swapping, held, joining, own_bias = (
            split_refs(scratch, self.sizes)
        )
        tokens, gain, bias, seg, cotangent, w_out, *weights = ins
        (bias_own,) = own_bias
        _, grad_out, _, full_out, _, _, _, info, across, gated = outs
        early = self.early.begin([outs[i] for i in (0, 2, 4, 5, 6)], held)
        normed, mixed_in, qkv, attended, gate = early.held
        sent, received = swapping[:2]
        count, tall, _ = normed.shape

        def filled_from(source):
            def fill(shard, local_sem):
                return [pltpu.make_async_copy(source, shard, local_sem.at[0])], source

            return fill

        def later(turns, walk):
            yield from idle(turns)
            yield from walk

        def main():
            fetched = self.fetch(ring, weights, *joining) if self.whole else []
            value = tokens[...].astype(F32)
            rstat = lax.rsqrt(jnp.mean(value * value, axis=1, keepdims=True) + EPSILON)
            normed[ring.ctx] = (value * rstat * gain[...].astype(F32)).astype(BF16)
            gather = ring_gather(ring, None, normed, *rows_sems, True)
            next(gather)
            mixed_shard = self.join(ring, weights, bias, bias_own, fetched, *joining[:2])
            yield from together(
                gather,
                shard_gather(ring, filled_from(mixed_shard), mixed_in, *mixed_sems),
            )
            early.ready(0, 1)
            self.project(normed, mixed_in, bias_own, qkv, gate, info)
            early.ready(2, 4)
            self.decay(info, across, seg)
            yield
            yield from self.attend(qkv, info, across, attended)
            early.ready(3)
            for i in range(count):
                rows = slice(i * tall, (i + 1) * tall)
                sent[i] = fold((attended[rows] * gate[rows]).astype(BF16))
            yield from swap(ring, *swapping)
            gated[...] = jnp.concatenate([unfold(received[i]) for i in range(count)], axis=1)

        turns = count // 2 * RING_PIECES
        yield from together(
            main(),
            later(turns - 1, ring_gather(ring, cotangent, grad_out, *cotangent_sems, False)),
            later(turns // 2, shard_gather(ring, filled_from(w_out), full_out, *out_sems)),
        )
        early.finish()

    def fetch(self, ring, weights, windows, joined, sem):
        start = pl.multiple_of(ring.ctx * self.hidden // 128 * 128, 128)
        copies = [
            pltpu.make_async_copy(
                weights[i].at[:, pl.ds(start, windows.shape[2])], windows.at[i], sem.at[i]
            )
            for i in range(4)
        ]
        for copy in copies:
            copy.start()
        return copies

    def join(self, ring, weights, bias, bias_own, fetched, windows, joined):
        heads, hidden = self.heads, self.hidden
        shape = (bias.shape[1], 128)
        head = lax.broadcasted_iota(jnp.int32, shape, 0)
        spot = lax.broadcasted_iota(jnp.int32, shape, 1)
        chosen = ((head == ring.ctx * heads + spot) & (spot < heads)).astype(F32)
        bias_own[...] = jnp.dot(
            jnp.broadcast_to(bias[...], (8, bias.shape[1])), chosen, **EXACT
        )
        if not self.whole:
            return weights[0]
        for copy in fetched:
            copy.wait()
        parts = []
        for i in range(4):
            part = windows[i, :, :hidden]
            if hidden % 128 != 0:
                shifted = windows[i, :, 64 : 64 + hidden]
                part = jnp.where(ring.ctx * hidden % 128 == 0, part, shifted)
            parts.append(part)
        parts.append(matmul(weights[4][...], chosen.astype(BF16)).astype(BF16))
        joined[...] = jnp.concatenate(parts, axis=1)
        return joined

    def project(self, normed, mixed_in, bias, qkv, gate, info):
        count, tall, width = normed.shape
        pair = 2 if count % 2 == 0 else 1
        hidden = self.hidden

        @pl.loop(0, count // pair)
        def _(index):
            block = normed[pl.ds(index * pair, pair)].reshape(pair * tall, width)
            rows = pl.ds(pl.multiple_of(index * pair * tall, pair * tall), pair * tall)
            mixed = matmul(block, mixed_in[...])
            qkv[rows] = mixed[:, : 3 * hidden].astype(BF16)
            gate[rows] = jax.nn.sigmoid(mixed[:, 3 * hidden : 4 * hidden])
            info[rows] = mixed[:, 4 * hidden : 4 * hidden + 128]
            info[rows, 8:16] = info[rows, 0:8] + bias[0:1, 0:8]

    def decay(self, info, across, seg):
        tall = 128
        here = lax.broadcasted_iota(jnp.int32, (tall, tall), 0)
        there = lax.broadcasted_iota(jnp.int32, (tall, tall), 1)
        wedge = (there <= here).astype(F32)
        before = jnp.zeros((1, 8), F32)
        pad = jnp.zeros((tall, 120), F32)
        across[8:9] = seg[...].astype(F32)
        for index in range(self.rows // tall):
            rows = slice(index * tall, (index + 1) * tall)
            info[rows, 24:25] = jnp.broadcast_to(across[8:9, rows], (tall, tall)).T[:, 0:1]
            logs = jax.nn.log_sigmoid(info[rows, 8:16])
            sums = jnp.dot(wedge, jnp.concatenate([logs, pad], axis=1), **EXACT)[:, :8] + before
            before = sums[tall - 1 :]
            info[rows, 0:8] = sums
            across[0:8, rows] = jnp.concatenate([sums, pad], axis=1).T[:8]

    def attend(self, qkv, info, across, attended):
        for index in range(self.rows // self.tall):
            rows, wide = self.block(index)
            allowed = self.allowed(rows, wide, info, across)
            mixed = []
            for head in range(self.heads):
                _, _, scores = self.scores(qkv, info, across, head, rows, wide, allowed)
                row_max = jnp.max(scores, axis=1, keepdims=True)
                raised = jnp.exp(scores - row_max)
                row_total = jnp.sum(raised, axis=1, keepdims=True)
                probabilities = (raised * (1.0 / row_total)).astype(BF16)
                mixed.append(matmul(probabilities, self.part(qkv, 2, head, slice(0, wide))))
                info[rows, 16 + head : 17 + head] = row_max + jnp.log(row_total)
                if head < self.heads - 1:
                    yield
            attended[rows] = jnp.concatenate(mixed, axis=1)
            yield


def slow(walk, turns):
    for _ in walk:
        yield from idle(turns)


class Backward(Attention):
    def __init__(self, own_heads, named):
        rows = named["qkv"].shape[0]
        super().__init__(rows, own_heads, named["qkv"].shape[1] // 3 // own_heads)
        self.names = list(named)
        hbm = ("gated", "grad_ffn_in")
        self.loaded = ("full_out", "qkv", "attended", "gate_value", "mixed_in", "normed")
        self.late = Late([named[name] for name in self.loaded])
        self.ins = [named[name] for name in self.names]
        self.in_specs = [
            ANYWHERE if name in hbm + self.loaded else VMEM for name in self.names
        ]
        count, shards = lax.axis_size("ctx"), lax.axis_size("fsdp")
        tall, width = named["gated"].shape
        hidden = own_heads * self.dim
        self.main = 4 * hidden
        both = -(-(5 * hidden + own_heads) // 128) * 128
        ffn = [named["grad_ffn_in"]]
        shard_rows = width // shards
        swapped = pltpu.VMEM((count, tall // 2, 2 * hidden), BF16)
        block = pltpu.VMEM((shards * tall, width), BF16)
        heads = pltpu.VMEM((self.rows, hidden), BF16)
        self.outs = (
            [jax.ShapeDtypeStruct((tall, width), F32)]
            + [jax.ShapeDtypeStruct((count,) + grad.shape, BF16) for grad in ffn]
            + [jax.ShapeDtypeStruct((count, shard_rows, both), BF16)]
            + [jax.ShapeDtypeStruct((8, width), F32)]
        )
        self.out_specs = [VMEM] + [ANYWHERE] * 2 + [VMEM]
        ring = [pltpu.SemaphoreType.DMA] + ring_sems(count)
        groups = [
            [pltpu.VMEM((3, own_heads, self.rows, self.dim), F32)],
            [pltpu.VMEM((self.rows, 128), F32), pltpu.VMEM((8, self.rows), F32)],
            [pltpu.VMEM((self.rows, self.main + 128), BF16)],
            [
                pltpu.VMEM((count, shard_rows, hidden), BF16),
                pltpu.VMEM((2, count // 2, shard_rows, hidden), BF16),
                pltpu.VMEM((shard_rows, hidden), F32),
            ]
            + ring_sems(count),
            [
                pltpu.VMEM((count, tall, width), BF16),
                pltpu.VMEM((2, count // 2, tall, width), BF16),
                pltpu.VMEM((tall, width), F32),
            ]
            + ring_sems(count),
            [
                pltpu.VMEM((shard_rows, both), BF16),
                pltpu.VMEM((width, self.main + 128), BF16),
                pltpu.VMEM((shard_rows, self.main + 128), BF16),
            ]
            + shard_sum_scratch(shard_rows, self.main + 128),
            ring,
            ring,
            ring,
            [pltpu.VMEM((8, width), F32)] + small_sum_scratch((8, width)),
            [pltpu.VMEM((tall, width), F32), pltpu.VMEM((tall, count * hidden), BF16)],
            [swapped, swapped] + swap_sems(count),
            [heads, heads],
            [block] + shard_gather_sems(1),
            [block] + shard_gather_sems(1),
            [pltpu.VMEM((tall, width), BF16), pltpu.VMEM((shards * tall, shard_rows), BF16)],
            self.late.scratch,
        ]
        self.sizes = [len(group) for group in groups]
        self.scratch = sum(groups, [])

    def run(self, ring, ins, outs, scratch):
        groups = split_refs(scratch, self.sizes)
        named = dict(zip(self.names, ins))
        late = self.late.start([named[name] for name in self.loaded], groups[16])
        named.update(zip(self.loaded, late.held))
        out_part, out_held, out_sum, *out_sems = groups[3]
        rows_part, rows_held, rows_sum, *rows_sems = groups[4]
        grad_mixed = groups[2][0]
        grads_all, grads_part, grads_sum, *grads_rest = groups[5]
        small, *small_rest = groups[9]
        named["grad_middle"], grad_gated = groups[10]
        named["grad_attn"], named["grad_gatelog"] = groups[12]
        gated_block, *gated_sems = groups[13]
        branch_block, *branch_sems = groups[14]
        branch, gated_columns = groups[15]
        count, tall, width = rows_part.shape

        def filled_from(source):
            def fill(shard, local_sem):
                return [pltpu.make_async_copy(source, shard, local_sem.at[0])], source

            return fill

        gather_gated = shard_gather(
            ring, filled_from(named["gated"]), gated_block, *gated_sems, turns=1
        )

        def main():
            next(gather_gated)
            next(gather_gated)
            late.need(0)
            self.branch_back(named, grad_gated, groups[11][0], branch, small)
            yield from together(
                swap(ring, *groups[11]),
                shard_gather(ring, filled_from(branch), branch_block, *branch_sems, turns=2),
                gather_gated,
            )
            late.need(1, 2, 3)
            self.gate_back(named, groups[11][1])
            self.out_grads(ring, gated_block, branch_block, gated_columns, out_part)
            yield from together(
                self.attention(named, *groups[0], *groups[1]),
                ring_sum(ring, out_part, out_held, out_sum, *out_sems, True),
            )
            self.join(ring, named, *groups[0], *groups[1], grad_mixed, small)
            block = 256 if width % 256 == 0 else width
            late.need(4)

            @pl.loop(0, width // block)
            def _(index):
                columns = pl.ds(pl.multiple_of(index * block, block), block)
                part = matmul_rows(grad_mixed[...], named["mixed_in"][columns])
                rows_part[:, :, columns] = part.astype(BF16).reshape(count, tall, block)

            yield from together(
                ring_sum(ring, rows_part, rows_held, rows_sum, *rows_sems, True),
                weights(),
            )

        def weights():
            yield from idle(RING_PIECES)
            late.need(5)
            self.weight_grads(named, grad_mixed, grads_part)
            yield from shard_sum(ring, grads_part, grads_sum, *grads_rest)
            tail = grads_all.shape[1] - self.main - out_sum.shape[1]
            grads_all[:, : self.main] = grads_sum[:, : self.main]
            grads_all[:, self.main :] = jnp.concatenate(
                [out_sum[...].astype(BF16), grads_sum[:, self.main : self.main + tail]], axis=1
            )

        yield from together(
            slow(ring_gather(ring, named["grad_ffn_in"], outs[1], *groups[6], True), 2),
            main(),
        )
        self.norm_back(named, rows_sum, outs[0], small)
        yield from together(
            ring_gather(ring, grads_all, outs[2], *groups[8], True),
            small_sum(ring, small, outs[3], *small_rest),
        )

    def branch_back(self, named, grad_gated, sent, branch, small):
        grad, normed = named["grad_normed_two"][...], named["normed_two"][...]
        small[...] = jnp.zeros_like(small)
        small[1:2] = jnp.sum(grad * normed, axis=0, keepdims=True)
        grad_normed = grad * named["gain_two"][...].astype(F32)
        inner = jnp.mean(grad_normed * normed, axis=1, keepdims=True)
        named["grad_middle"][...] = named["cotangent"][...].astype(F32) + named["rstat_two"][...] * (
            grad_normed - normed * inner
        )
        branch[...] = named["grad_middle"][...].astype(BF16)
        count, hidden = sent.shape[0], sent.shape[2] // 2
        width = grad.shape[1]
        block = 256 if width % 256 == 0 else width
        if grad_gated.shape[1] > width:
            grad_gated[...] = jnp.zeros_like(grad_gated)

        @pl.loop(0, width // block)
        def _(index):
            columns = pl.ds(pl.multiple_of(index * block, block), block)
            part = matmul_rows(branch[...], named["full_out"][columns])
            grad_gated[:, columns] = part.astype(BF16)

        for i in range(count):
            sent[i] = fold(grad_gated[:, i * hidden : (i + 1) * hidden])

    def gate_back(self, named, received):
        count, tall = received.shape[0], 2 * received.shape[1]
        for i in range(count):
            rows = slice(i * tall, (i + 1) * tall)
            grad = unfold(received[i]).astype(F32)
            gate = named["gate_value"][rows]
            named["grad_attn"][rows] = (grad * gate).astype(BF16)
            named["grad_gatelog"][rows] = (
                grad * named["attended"][rows] * (gate * (1.0 - gate))
            ).astype(BF16)

    def attention(self, named, grads, sums_rows, sums_columns):
        qkv, info, across, grad_attn = [
            named[name] for name in ("qkv", "info", "across", "grad_attn")
        ]
        grad_q, grad_k, grad_v = [grads.at[i] for i in range(3)]
        blocks = self.rows // self.tall
        sums_columns[...] = jnp.zeros_like(sums_columns)
        pad = jnp.zeros((self.tall, 128 - self.heads), F32)
        for index in reversed(range(blocks)):
            rows, wide = self.block(index)
            allowed = self.allowed(rows, wide, info, across)
            own = slice(0, wide)
            row_sums = []
            for head in range(self.heads):
                queries, keys, scores = self.scores(
                    qkv, info, across, head, rows, wide, allowed
                )
                probabilities = jnp.exp(scores - info[rows, 16 + head : 17 + head])
                grad_part = grad_attn[rows, head * self.dim : (head + 1) * self.dim]
                grad_probs = matmul_rows(grad_part, self.part(qkv, 2, head, own))
                row_inner = jnp.sum(probabilities * grad_probs, axis=1, keepdims=True)
                grad_scores = (probabilities * (grad_probs - row_inner)).astype(BF16)
                grad_q[head, rows] = matmul(grad_scores, keys) * self.scaling
                from_k = weight_grad(grad_scores, queries) * self.scaling
                from_v = weight_grad(probabilities.astype(BF16), grad_part)
                wide_sums = grad_scores.astype(F32)
                row_sums.append(jnp.sum(wide_sums, axis=1, keepdims=True))
                column_sums = jnp.sum(wide_sums, axis=0, keepdims=True)
                if index == blocks - 1:
                    grad_k[head], grad_v[head] = from_k, from_v
                    sums_columns[head : head + 1] = column_sums
                else:
                    grad_k[head, own] += from_k
                    grad_v[head, own] += from_v
                    sums_columns[head : head + 1, own] += column_sums
                if head < self.heads - 1:
                    yield
            sums_rows[rows] = jnp.concatenate(row_sums + [pad], axis=1)
            yield

    def join(self, ring, named, grads, sums_rows, sums_columns, grad_mixed, small):
        for index in range(self.rows // self.tall):
            rows, _ = self.block(index)
            grad_mixed[rows, : self.main] = jnp.concatenate(
                [grads[i, head, rows].astype(BF16) for i in range(3) for head in range(self.heads)]
                + [named["grad_gatelog"][rows]],
                axis=1,
            )
        tall = 128
        here = lax.broadcasted_iota(jnp.int32, (tall, tall), 0)
        there = lax.broadcasted_iota(jnp.int32, (tall, tall), 1)
        wedge = (here <= there).astype(F32)
        later, bias = jnp.zeros((1, 8), F32), jnp.zeros((1, 8), F32)
        pad = jnp.zeros((tall, 120), BF16)
        for index in reversed(range(self.rows // tall)):
            rows = slice(index * tall, (index + 1) * tall)
            inside = jnp.dot(wedge, sums_rows[rows], **EXACT)[:, :8] - lax.dot_general(
                wedge, sums_columns[:, rows], (((1,), (1,)), ((), ())), **EXACT
            )
            logits = named["info"][rows, 8:16]
            grad_logits = ((inside + later) * jax.nn.sigmoid(-logits)).astype(BF16)
            later = later + inside[:1]
            bias = bias + jnp.sum(grad_logits.astype(F32), axis=0, keepdims=True)
            grad_mixed[rows, self.main :] = jnp.concatenate([grad_logits, pad], axis=1)
        spot = lax.broadcasted_iota(jnp.int32, (1, small.shape[1]), 1)
        small[2:3] = sum(
            jnp.where(spot == ring.ctx * self.heads + head, bias[:, head : head + 1], 0.0)
            for head in range(self.heads)
        )

    def out_grads(self, ring, gated_block, branch_block, gated_columns, parts):
        count, rows, hidden = parts.shape
        for i in range(lax.axis_size("fsdp")):

            @pl.when(ring.fsdp == i)
            def _():
                gated_columns[...] = gated_block[:, i * rows : (i + 1) * rows]

        for i in range(count):
            stop = min((i + 1) * hidden, branch_block.shape[1])
            if stop > i * hidden:
                part = weight_grad(gated_columns[...], branch_block[:, i * hidden : stop])
                parts[i] = part.astype(BF16)
            else:
                parts[i] = jnp.zeros((rows, hidden), BF16)

    def weight_grads(self, named, grad_mixed, parts):
        count, tall, width = named["normed"].shape
        tile = 128

        @pl.loop(0, width // tile)
        def _(index):
            columns = pl.ds(pl.multiple_of(index * tile, tile), tile)
            normed = named["normed"][:, :, columns].reshape(count * tall, tile)
            parts[columns] = weight_grad(normed, grad_mixed[...]).astype(BF16)

    def norm_back(self, named, rows_sum, grad_tokens, small):
        grad, value = rows_sum[...], named["tokens"][...].astype(F32)
        rstat = lax.rsqrt(jnp.mean(value * value, axis=1, keepdims=True) + EPSILON)
        normed = value * rstat
        small[0:1] = jnp.sum(grad * normed, axis=0, keepdims=True)
        grad_normed = grad * named["gain_one"][...].astype(F32)
        inner = jnp.mean(grad_normed * normed, axis=1, keepdims=True)
        grad_tokens[...] = named["grad_middle"][...] + rstat * (
            grad_normed - normed * inner
        )


def exchange(ident, name, *tasks):
    count = lax.axis_size("ctx")

    def take(refs, sizes):
        groups, at = [], 0
        for size in sizes:
            groups.append(refs[at : at + size])
            at += size
        return groups

    ins = [len(task.ins) for task in tasks]
    outs = [len(task.outs) for task in tasks]
    scratch = [len(task.scratch) for task in tasks]

    def kernel(*refs):
        ring = Ring(count)
        kinds = sum([task.kinds for task in tasks], ())
        peers = []
        if "all" in kinds:
            peers = sum(all_peers(ring), [])
        else:
            if "ring" in kinds:
                peers += [ring.device(1), ring.device(-1)]
            if "shard" in kinds:
                pair, others = shard_pair(ring, lax.axis_size("fsdp"))
                peers += [(ring.ctx, to) for to in [pair] + others]
        greet(peers)
        groups = [
            take(refs[: sum(ins)], ins),
            take(refs[sum(ins) : sum(ins) + sum(outs)], outs),
            take(refs[sum(ins) + sum(outs) :], scratch),
        ]
        for _ in together(*[task.run(ring, *parts) for task, *parts in zip(tasks, *groups)]):
            pass

    results = pl.pallas_call(
        kernel,
        out_shape=sum([task.outs for task in tasks], []),
        in_specs=sum([task.in_specs for task in tasks], []),
        out_specs=sum([task.out_specs for task in tasks], []),
        scratch_shapes=sum([task.scratch for task in tasks], []),
        compiler_params=pltpu.CompilerParams(
            collective_id=ident, has_side_effects=True, vmem_limit_bytes=62 * 2**20
        ),
        cost_estimate=pl.CostEstimate(flops=0, bytes_accessed=100_000_000, transcendentals=0),
        name=name,
    )(*sum([task.ins for task in tasks], []))
    return take(list(results), outs)


def flat(blocks):
    return blocks.reshape(-1, blocks.shape[-1])


def permute_rows(value, beside):
    count, me = lax.axis_size("ctx"), lax.axis_index("ctx")
    order = [ring_index(place, count) for place in range(count)]
    rows, half = value.shape[0], value.shape[0] // 2
    ways = [[(order[i], order[(i + sign) % count]) for i in range(count)] for sign in (1, -1)]

    parts, offsets = [value], [0]
    blocks, results, beside = [value, value], [], list(beside)
    for hops in range(1, count // 2 + 1):
        work = None
        if hops > 1 and beside:
            work, operand = beside.pop(0)
            blocks[0], blocks[1], operand = lax.optimization_barrier((*blocks, operand))
        last = hops == count // 2
        sent = [blocks[0][:half], blocks[1][half:]] if last else blocks
        blocks = [lax.ppermute(block, "ctx", way) for block, way in zip(sent, ways)]
        if work is not None:
            result = work(operand)
            blocks[0], blocks[1], result = lax.optimization_barrier((*blocks, result))
            results.append(result)
        parts += blocks
        offsets += [-hops, hops]
    place = (ring_place(me, count) + jnp.asarray(offsets[:-1], jnp.int32) + count) % count
    return place_rows(parts, ring_index(place, count)), results


def place_rows(parts, sources):
    rows, width = parts[0].shape
    count = len(parts) - 1
    half = rows // 2

    def kernel(source_ref, *refs):
        ins, out = refs[:-1], refs[-1]
        for j in range(count):
            at = source_ref[j] * rows
            if j < count - 1:
                out[pl.ds(pl.multiple_of(at, rows), rows)] = ins[j][...].astype(F32)
            else:
                for k in range(2):
                    start = pl.multiple_of(at + k * half, half)
                    out[pl.ds(start, half)] = ins[j + k][...].astype(F32)

    return pl.pallas_call(
        kernel,
        out_shape=jax.ShapeDtypeStruct((rows * count, width), F32),
        in_specs=[pl.BlockSpec(memory_space=pltpu.SMEM)] + [VMEM] * len(parts),
        out_specs=VMEM,
        compiler_params=pltpu.CompilerParams(vmem_limit_bytes=40 * 2**20),
        cost_estimate=pl.CostEstimate(
            flops=0, bytes_accessed=rows * width * count * 6, transcendentals=0
        ),
        name="place_rows",
    )(sources, *parts)


def ffn_columns(blocks, n_fsdp):
    count, rows, both = blocks.shape
    width, piece = both // 2, both // 2 // n_fsdp
    steps = 4
    tall = rows // steps

    def kernel(block_ref, *outs):
        for j in range(count):
            for half in range(2):
                for group in range(n_fsdp):
                    start, to = half * width + group * piece, (group * count + j) * piece
                    outs[half][:, to : to + piece] = block_ref[j, :, start : start + piece].astype(F32)

    wide = jax.ShapeDtypeStruct((rows, width * count), F32)
    spec = pl.BlockSpec((tall, width * count), lambda i: (i, 0))
    return pl.pallas_call(
        kernel,
        out_shape=(wide, wide),
        grid=(steps,),
        in_specs=[pl.BlockSpec((count, tall, both), lambda i: (0, i, 0))],
        out_specs=(spec, spec),
        compiler_params=pltpu.CompilerParams(vmem_limit_bytes=40 * 2**20),
        cost_estimate=pl.CostEstimate(
            flops=0, bytes_accessed=rows * both * count * 6, transcendentals=0
        ),
        name="ffn_columns",
    )(blocks)


def head_columns(blocks, sizes, widths):
    count, rows, total = blocks.shape
    steps = 4
    tall = rows // steps
    starts = [sum(sizes[:i]) for i in range(len(sizes))]

    def kernel(block_ref, *outs):
        for start, size, out in zip(starts, sizes, outs):
            for i in range(0, count, 2):
                pair = jnp.concatenate(
                    [block_ref[i + k][:, start : start + size].astype(F32) for k in range(2)], axis=1
                )
                at = i * size
                keep = min(2 * size, out.shape[1] - at)
                if keep > 0:
                    out[:, at : at + keep] = pair[:, :keep]

    return pl.pallas_call(
        kernel,
        out_shape=tuple(jax.ShapeDtypeStruct((rows, w), F32) for w in widths),
        grid=(steps,),
        in_specs=[pl.BlockSpec((count, tall, total), lambda i: (0, i, 0))],
        out_specs=tuple(pl.BlockSpec((tall, w), lambda i: (i, 0)) for w in widths),
        compiler_params=pltpu.CompilerParams(vmem_limit_bytes=40 * 2**20),
        cost_estimate=pl.CostEstimate(
            flops=0, bytes_accessed=count * rows * total * 6, transcendentals=0
        ),
        name="head_columns",
    )(blocks)


def shards(
    tokens,
    segments,
    gain_attn,
    w_query,
    w_key,
    w_value,
    w_forget,
    forget_bias,
    w_outgate,
    w_out,
    gain_ffn,
    w_gate,
    w_up,
    w_down,
    cotangent,
):
    n_ctx, me = lax.axis_size("ctx"), lax.axis_index("ctx")
    n_fsdp = lax.axis_size("fsdp")
    tok_rows, width = tokens.shape[1:]
    seq_rows = tok_rows * n_ctx
    n_heads = forget_bias.shape[0]
    head_dim = width // n_heads
    own_heads = -(-n_heads // n_ctx)
    own_width = own_heads * head_dim
    padded = own_width * n_ctx
    ffn_rows = w_down.shape[0]
    ffn_piece = ffn_rows // n_ctx
    ffn_width = ffn_piece * n_fsdp
    shard_rows = w_query.shape[0]

    def widen(value, size):
        return jnp.pad(value, ((0, 0), (0, size - value.shape[1])))

    def own_columns(weight, size):
        return lax.dynamic_slice_in_dim(widen(weight, size * n_ctx), me * size, size, 1)

    def own_ffn(weight):
        return [
            lax.dynamic_slice_in_dim(weight, (group * n_ctx + me) * ffn_piece, ffn_piece, 1)
            for group in range(n_fsdp)
        ]

    weights = [w_query, w_key, w_value, w_outgate, w_forget]
    if padded != width or own_width % 64 != 0:
        columns = [own_columns(w, own_width) for w in weights[:4]]
        columns.append(widen(own_columns(w_forget, own_heads), 128))
        weights = [jnp.concatenate(columns, axis=1)]
    gain_one, gain_two = gain_attn, gain_ffn
    (
        (
            normed,
            grad_out_low,
            mixed_in,
            full_out,
            qkv,
            attended,
            gate_value,
            info,
            across,
            gated,
        ),
    ) = exchange(
        0,
        "forward",
        Forward(
            tokens[0],
            gain_one,
            cotangent[0],
            weights,
            w_out,
            forget_bias[None],
            segments,
            own_heads,
            head_dim,
        ),
    )
    w_in = [w_gate, w_up]
    if ffn_piece % 128 != 0:
        w_in = [jnp.concatenate(own_ffn(w_gate) + own_ffn(w_up), axis=1)]
    ((output, grad_normed_two, normed_two, rstat_two, grad_ffn_in, grad_ffn_out),) = exchange(
        1,
        "ffn",
        Ffn(tokens[0], gated, full_out, gain_two, grad_out_low, w_in, w_down, ffn_piece),
    )
    ((grad_inputs, spread_ffn_in, spread_attn, small),) = exchange(
        2,
        "backward",
        Backward(
            own_heads,
            {
                "qkv": qkv,
                "info": info,
                "across": across,
                "attended": attended,
                "gate_value": gate_value,
                "grad_normed_two": grad_normed_two,
                "normed_two": normed_two,
                "rstat_two": rstat_two,
                "gain_two": gain_two,
                "cotangent": cotangent[0],
                "full_out": full_out,
                "gated": gated[:, :width],
                "grad_ffn_in": grad_ffn_in,
                "normed": normed,
                "mixed_in": mixed_in,
                "tokens": tokens[0],
                "gain_one": gain_one,
            },
        ),
    )
    sizes = [own_width] * 5 + [own_heads]

    def place_ffn(blocks):
        if ffn_piece % 128 == 0:
            return ffn_columns(blocks, n_fsdp)
        whole = blocks.reshape(n_ctx, shard_rows, 2, n_fsdp, ffn_piece)
        whole = jnp.transpose(whole, (2, 1, 3, 0, 4)).reshape(2, shard_rows, -1).astype(F32)
        return whole[0], whole[1]

    def place_heads(blocks):
        return head_columns(blocks, sizes, [width] * 5 + [n_heads])

    grad_down, ((grad_gate, grad_up), grad_weights) = permute_rows(
        grad_ffn_out, [(place_ffn, spread_ffn_in), (place_heads, spread_attn)]
    )
    return (
        output[None],
        grad_inputs[None],
        small[0],
        grad_weights[0],
        grad_weights[1],
        grad_weights[2],
        grad_weights[5],
        small[2, :n_heads],
        grad_weights[3],
        grad_weights[4],
        small[1],
        grad_gate,
        grad_up,
        grad_down,
    )


def solution(mesh):
    rows, blocks = P("fsdp", None), P("fsdp", "ctx", None)
    return jax.shard_map(
        shards,
        mesh=mesh,
        in_specs=(blocks, rows, P())
        + (rows,) * 4
        + (P(), rows, rows, P(), rows, rows, rows, blocks),
        out_specs=(blocks, blocks, P())
        + (rows,) * 4
        + (P(), rows, rows, P(), rows, rows, rows),
        check_vma=False,
    )
```

```python
import jax
import jax.numpy as jnp
from jax import lax
from jax.experimental import pallas as pl
from jax.experimental.pallas import tpu as pltpu
from jax.sharding import PartitionSpec as P

EPSILON = 1e-06
NEGATIVE = -1e30
BF16, F32 = jnp.bfloat16, jnp.float32


def matmul(left, right):
    return jnp.dot(left, right, preferred_element_type=F32)


def matmul_rows(left, right):
    return lax.dot_general(left, right, (((1,), (1,)), ((), ())), preferred_element_type=F32)


def weight_grad(left, right):
    return lax.dot_general(left, right, (((0,), (0,)), ((), ())), preferred_element_type=F32)


MESH = pl.DeviceIdType.MESH
RING_PIECES = 4
FFN_PIECES = 2


def ring_place(ctx, count):
    odd = ctx % 2
    return ctx // 2 + odd * (count - 1 - 2 * (ctx // 2))


def ring_index(place, count):
    back = place // (count // 2)
    return 2 * place + back * (2 * (count - 1 - place) + 1 - 2 * place)


class Ring:
    def __init__(self, count):
        self.count, self.half = count, count // 2
        self.ctx, self.fsdp = lax.axis_index("ctx"), lax.axis_index("fsdp")
        self.place = ring_place(self.ctx, count)

    def at(self, offset):
        return ring_index((self.place + offset + self.count) % self.count, self.count)

    def device(self, offset):
        return (self.at(offset), self.fsdp)


def greet(devices):
    barrier = pltpu.get_barrier_semaphore()
    for device in devices:
        pl.semaphore_signal(barrier, inc=1, device_id=device, device_id_type=MESH)
    pl.semaphore_wait(barrier, len(devices))


def remote(src, dst, send, recv, device):
    return pltpu.make_async_remote_copy(
        src_ref=src, dst_ref=dst, send_sem=send, recv_sem=recv, device_id=device, device_id_type=MESH
    )


def carried(step, half, pieces, way):
    if step < half - 1:
        return range(pieces)
    return range(pieces // 2) if way == 0 else range(pieces // 2, pieces)


def ring_slot(ring, offset, absolute):
    if absolute:
        return ring.at(offset)
    if abs(offset) == ring.half:
        return ring.count - 1
    return 2 * offset - 1 if offset > 0 else -2 * offset


def ring_gather(ring, own, full, local_sem, send_sem, recv_sem, absolute, pieces=RING_PIECES):
    rows = full.shape[1] // pieces

    def part(k):
        return pl.ds(k * rows, rows)

    def slot(offset):
        return ring_slot(ring, offset, absolute)

    keep = None
    if own is None:
        own = full.at[slot(0)]
    else:
        keep = pltpu.make_async_copy(own, full.at[slot(0)], local_sem)
        keep.start()
    copies = {}
    for step in range(ring.half):
        for k in range(pieces):
            for way, sign in ((0, 1), (1, -1)):
                if step > 0:
                    copies[step - 1, k, way].wait_recv()
                if k not in carried(step, ring.half, pieces, way):
                    continue
                src = own.at[part(k)] if step == 0 else full.at[slot(-sign * step), part(k)]
                to = slot(-sign * step if absolute else -sign * (step + 1))
                copy = remote(
                    src,
                    full.at[to, part(k)],
                    send_sem.at[step, k, way],
                    recv_sem.at[step, k, way],
                    ring.device(sign),
                )
                copy.start()
                copies[step, k, way] = copy
            yield
    for (step, _, _), copy in copies.items():
        if step == ring.half - 1:
            copy.wait_recv()
    for copy in copies.values():
        copy.wait_send()
    if keep is not None:
        keep.wait()


def ring_sum(
    ring, parts, held, total, send_sem, recv_sem, absolute, ahead=False, pieces=RING_PIECES
):
    rows = parts.shape[1] // pieces

    def place(offset):
        return ring_slot(ring, offset, absolute)

    def part(k):
        return pl.ds(k * rows, rows)

    copies = {}

    def send(step, k, way, sign):
        src = parts.at[place(sign * (ring.half - step)), part(k)]
        if (step - 1, k, way) in copies:
            copies[step - 1, k, way].wait_recv()
            slot = held.at[way, step - 1, part(k)]
            slot[...] = (slot[...].astype(F32) + src[...].astype(F32)).astype(BF16)
            src = slot
        copy = remote(
            src,
            held.at[way, step, part(k)],
            send_sem.at[step, k, way],
            recv_sem.at[step, k, way],
            ring.device(sign),
        )
        copy.start()
        copies[step, k, way] = copy

    def farthest(k, way):
        return k in carried(ring.half - 1, ring.half, pieces, way)

    for step in ([None] if ahead else []) + list(range(ring.half)):
        for k in range(pieces):
            for way, sign in ((0, 1), (1, -1)):
                if step is None and not farthest(k, way):
                    send(1, k, way, sign)
                elif step == 0 and farthest(k, way):
                    send(0, k, way, sign)
                elif step == 1 and (farthest(k, way) or not ahead):
                    send(1, k, way, sign)
                elif step is not None and step > 1:
                    send(step, k, way, sign)
            yield
    last = ring.half - 1
    for k in range(pieces):
        for way in range(2):
            copies[last, k, way].wait_recv()
        total[part(k)] = (
            parts[place(0), part(k)].astype(F32)
            + held[0, last, part(k)].astype(F32)
            + held[1, last, part(k)].astype(F32)
        )
    for copy in copies.values():
        copy.wait_send()


def ring_sems(count, pieces=RING_PIECES):
    shape = (count // 2, pieces, 2)
    return [pltpu.SemaphoreType.DMA(shape), pltpu.SemaphoreType.DMA(shape)]


def sems(*counts):
    return [pltpu.SemaphoreType.DMA((max(count, 1),)) for count in counts]


ANYWHERE, VMEM = pl.BlockSpec(memory_space=pl.ANY), pl.BlockSpec(memory_space=pltpu.VMEM)


def shard_pair(ring, shards):
    me = ring.fsdp
    pair = me + 1 - 2 * (me % 2)
    return pair, [(me + 2 * hop) % shards for hop in range(1, shards // 2)]


def all_peers(ring):
    count, shards = lax.axis_size("ctx"), lax.axis_size("fsdp")
    siblings = [(ring.ctx, (ring.fsdp + hop) % shards) for hop in range(1, shards)]
    return siblings, [((ring.ctx + hop) % count, ring.fsdp) for hop in range(1, count)]


def idle(turns):
    for _ in range(turns):
        yield


def together(*walks):
    walks = list(walks)
    while walks:
        walks = [walk for walk in walks if next(walk, walks) is None]
        yield


def shard_gather(ring, fill, whole, local_sem, send_sem, recv_sem, turns=3 * RING_PIECES):
    shards, me = lax.axis_size("fsdp"), ring.fsdp
    rows = whole.shape[0] // shards
    pair, others = shard_pair(ring, shards)

    def shard(index):
        return whole.at[pl.ds(pl.multiple_of(index * rows, rows), rows)]

    local, source = fill(shard(me), local_sem)
    for copy in local:
        copy.start()
    yield
    if source is None:
        for copy in local:
            copy.wait()
    sent = shard(me) if source is None else source
    copies = [
        remote(sent, shard(me), send_sem.at[i], recv_sem.at[i], (ring.ctx, to))
        for i, to in enumerate([pair] + others)
    ]
    for copy in copies:
        copy.start()
    yield from idle(turns)
    passed = []
    for i in range(1, len(copies)):
        copies[i].wait_recv()
        origin = (me - 2 * i + shards) % shards
        at = shards // 2 - 1 + i
        copy = remote(
            shard(origin), shard(origin), send_sem.at[at], recv_sem.at[at], (ring.ctx, pair)
        )
        copy.start()
        passed.append(copy)
    yield from idle(2)
    copies[0].wait_recv()
    for copy in passed:
        copy.wait_recv()
    for copy in copies + passed:
        copy.wait_send()
    if source is not None:
        for copy in local:
            copy.wait()


def shard_gather_sems(parts):
    shards = lax.axis_size("fsdp")
    return sems(parts, shards - 1, shards - 1)


def shard_sum(ring, parts, total, near, far, near_send, near_recv, far_send, far_recv):
    shards, me = lax.axis_size("fsdp"), ring.fsdp
    half, core, chip = shards // 2, me % 2, me // 2
    pair, others = shard_pair(ring, shards)
    rows = parts.shape[0] // shards

    def shard(index):
        return pl.ds(pl.multiple_of(index * rows, rows), rows)

    first = [
        remote(
            parts.at[shard(2 * i + 1 - core)],
            near.at[i],
            near_send.at[i],
            near_recv.at[i],
            (ring.ctx, pair),
        )
        for i in range(half)
    ]
    for copy in first:
        copy.start()
    yield from idle(2)
    for copy in first:
        copy.wait_recv()
    second = []
    for hop in range(1, half):
        to = (chip + hop) % half
        near[to] = (near[to].astype(F32) + parts[shard(2 * to + core)].astype(F32)).astype(BF16)
        copy = remote(
            near.at[to],
            far.at[hop - 1],
            far_send.at[hop - 1],
            far_recv.at[hop - 1],
            (ring.ctx, others[hop - 1]),
        )
        copy.start()
        second.append(copy)
    yield from idle(3 * RING_PIECES)
    sums = parts[shard(me)].astype(F32) + near[chip].astype(F32)
    for hop, copy in enumerate(second):
        copy.wait_recv()
        sums = sums + far[hop].astype(F32)
    total[...] = sums.astype(BF16)
    for copy in first + second:
        copy.wait_send()


def shard_sum_scratch(rows, width):
    half = lax.axis_size("fsdp") // 2
    return [
        pltpu.VMEM((half, rows, width), BF16),
        pltpu.VMEM((max(half - 1, 1), rows, width), BF16),
    ] + sems(half, half, half - 1, half - 1)


class Ffn:
    kinds = ("ring", "shard")

    def __init__(self, tokens, gated, full_out, gain, grad_out, w_in, w_out, piece):
        count, shards = lax.axis_size("ctx"), lax.axis_size("fsdp")
        rows, width = tokens.shape
        self.aligned = len(w_in) == 2
        self.piece, self.inner = piece, piece * shards
        inner, both = self.inner, 2 * self.inner
        shard_rows = width // shards
        self.ins = [grad_out, tokens, gated, full_out, gain, w_out] + list(w_in)
        self.in_specs = [ANYWHERE, VMEM, VMEM, ANYWHERE, VMEM] + [ANYWHERE] * (1 + len(w_in))
        self.late = Late([full_out, grad_out])
        self.outs = [
            jax.ShapeDtypeStruct((rows, width), BF16),
            jax.ShapeDtypeStruct((rows, width), F32),
            jax.ShapeDtypeStruct((rows, width), F32),
            jax.ShapeDtypeStruct((rows, 1), F32),
            jax.ShapeDtypeStruct((shard_rows, both), BF16),
            jax.ShapeDtypeStruct((piece, width), BF16),
        ]
        self.out_specs = [VMEM] * 6
        held = pltpu.VMEM((2, count // 2, rows, width), BF16)
        groups = [
            [pltpu.VMEM((count, rows, width), BF16), pltpu.SemaphoreType.DMA] + ring_sems(count, FFN_PIECES),
            [pltpu.VMEM((width, both), BF16)] + shard_gather_sems(2 * shards),
            [pltpu.VMEM((inner, width), BF16)] + shard_gather_sems(1),
            [pltpu.VMEM((count, rows, inner), BF16), pltpu.VMEM((count, rows, both), BF16)],
            [pltpu.VMEM((count, rows, width), BF16), held] + ring_sems(count, FFN_PIECES),
            [pltpu.VMEM((count, rows, width), BF16), held] + ring_sems(count, FFN_PIECES),
            [pltpu.VMEM((width, both), BF16)] + shard_sum_scratch(shard_rows, both),
            [pltpu.VMEM((inner, width), BF16)] + shard_sum_scratch(piece, width),
            [
                pltpu.VMEM((rows, width), F32),
                pltpu.VMEM((rows, width), BF16),
                pltpu.VMEM((rows, width), F32),
            ],
            self.late.scratch,
        ]
        self.sizes = [len(group) for group in groups]
        self.scratch = sum(groups, [])

    def run(self, ring, ins, outs, scratch):
        _, tokens, gated, _, gain, w_out_rows = ins[:6]
        w_in_rows = ins[6:]
        inner, piece = self.inner, self.piece
        groups = split_refs(scratch, self.sizes)
        late = self.late.start([ins[3], ins[0]], groups[9])
        full_out, grad_out = late.held
        (rows_all, *rows_sems), (w_in, *w_in_sems), (w_out, *w_out_sems) = groups[:3]
        hidden, grad_mid = groups[3]
        (out_part, out_held, *out_sems), (in_part, in_held, *in_sems) = groups[4:6]
        (grad_w_in, *grad_in_rest), (grad_w_out, *grad_out_rest) = groups[6:8]
        middle, normed, out_sum = groups[8]
        count, tall = rows_all.shape[:2]
        width = rows_all.shape[2]

        def fill_in(shard, local_sem):
            if not self.aligned:
                return [pltpu.make_async_copy(w_in_rows[0], shard, local_sem.at[0])], w_in_rows[0]
            copies = []
            for i in range(2):
                for group in range(inner // piece):
                    at = i * (inner // piece) + group
                    start = pl.multiple_of((group * count + ring.ctx) * piece, piece)
                    copies.append(
                        pltpu.make_async_copy(
                            w_in_rows[i].at[:, pl.ds(start, piece)],
                            shard.at[:, pl.ds(at * piece, piece)],
                            local_sem.at[at],
                        )
                    )
            return copies, None

        def fill_out(shard, local_sem):
            start = pl.multiple_of(ring.ctx * piece, piece)
            own = w_out_rows.at[pl.ds(start, piece)]
            return [pltpu.make_async_copy(own, shard, local_sem.at[0])], own

        def compute(slots):
            size = (slots.stop - slots.start) * tall

            def load(ref):
                return ref[slots].reshape(size, ref.shape[2])

            def store(ref, columns, value):
                ref[slots, :, columns] = value.astype(BF16).reshape(-1, tall, value.shape[1])

            tile = min(256, inner)

            @pl.loop(0, inner // tile)
            def _(index):
                def columns(start):
                    return pl.ds(pl.multiple_of(start + index * tile, tile), tile)

                gate = matmul(load(rows_all), w_in[:, columns(0)])
                up = matmul(load(rows_all), w_in[:, columns(inner)])
                grad_hidden = matmul_rows(load(grad_out), w_out[columns(0)])
                sig = jax.nn.sigmoid(gate)
                silu = gate * sig
                store(hidden, columns(0), silu * up)
                store(
                    grad_mid, columns(0), grad_hidden * up * (sig * (1.0 + gate * (1.0 - sig)))
                )
                store(grad_mid, columns(inner), grad_hidden * silu)

            wide = 256 if width % 256 == 0 else width

            @pl.loop(0, width // wide)
            def _(index):
                columns = pl.ds(pl.multiple_of(index * wide, wide), wide)
                store(in_part, columns, matmul_rows(load(grad_mid), w_in[columns]))
                store(out_part, columns, matmul(load(hidden), w_out[:, columns]))

        def weight_grads(left, right, grads):
            tile = 128 if left.shape[2] % 128 == 0 else left.shape[2]

            @pl.loop(0, left.shape[2] // tile)
            def _(index):
                columns = pl.ds(pl.multiple_of(index * tile, tile), tile)
                grads[columns] = weight_grad(
                    left[:, :, columns].reshape(count * tall, tile),
                    right[...].reshape(count * tall, right.shape[2]),
                ).astype(BF16)

        def first():
            block = 256 if width % 256 == 0 else width
            late.need(0)

            @pl.loop(0, width // block)
            def _(index):
                columns = pl.ds(pl.multiple_of(index * block, block), block)
                middle[:, columns] = tokens[:, columns].astype(F32) + matmul(
                    gated[:, :width], full_out[:, columns]
                )

            value = middle[...]
            rstat = lax.rsqrt(jnp.mean(value * value, axis=1, keepdims=True) + EPSILON)
            outs[2][...] = value * rstat
            outs[3][...] = rstat
            normed[...] = (outs[2][...] * gain[...].astype(F32)).astype(BF16)

        weights = together(
            shard_gather(ring, fill_in, w_in, *w_in_sems),
            shard_gather(ring, fill_out, w_out, *w_out_sems),
        )
        next(weights)
        next(weights)
        first()
        yield from together(weights, ring_gather(ring, normed, rows_all, *rows_sems, False, FFN_PIECES))
        sums = together(
            ring_sum(ring, in_part, in_held, outs[1], *in_sems, False, True, FFN_PIECES),
            ring_sum(ring, out_part, out_held, out_sum, *out_sems, False, True, FFN_PIECES),
        )

        def turn():
            for _ in range(FFN_PIECES):
                next(sums)

        late.need(1)
        nearest = count // 2 - 1
        compute(slice(2 * nearest - 1, 2 * nearest + 1))
        turn()
        compute(slice(count - 1, count))
        turn()
        for pair in range(nearest - 1, 0, -1):
            compute(slice(2 * pair - 1, 2 * pair + 1))
        compute(slice(0, 1))
        turn()
        weight_grads(hidden, grad_out, grad_w_out)
        weight_grads(rows_all, grad_mid, grad_w_in)
        yield from together(
            sums,
            shard_sum(ring, grad_w_in, outs[4], *grad_in_rest),
            shard_sum(ring, grad_w_out, outs[5], *grad_out_rest),
        )
        outs[0][...] = (middle[...] + out_sum[...]).astype(BF16)


def fold(block):
    half = block.shape[0] // 2
    return jnp.concatenate([block[:half], block[half:]], axis=1)


def unfold(block):
    half = block.shape[1] // 2
    return jnp.concatenate([block[:, :half], block[:, half:]], axis=0)


def swap_sems(count):
    return sems(count - 1, count - 1)


def swap(ring, sent, received, send_sem, recv_sem):
    _, peers = all_peers(ring)
    copies = [
        remote(sent.at[to[0]], received.at[ring.ctx], send_sem.at[i], recv_sem.at[i], to)
        for i, to in enumerate(peers)
    ]
    for copy in copies:
        copy.start()
    received[ring.ctx] = sent[ring.ctx]
    yield from idle(RING_PIECES)
    for copy in copies:
        copy.wait()


def small_sum_scratch(shape):
    count, shards = lax.axis_size("ctx"), lax.axis_size("fsdp")
    return [
        pltpu.VMEM((shards,) + shape, F32),
        pltpu.VMEM((count,) + shape, F32),
    ] + sems(shards - 1, shards - 1, count - 1, count - 1)


def small_sum(ring, small, total, near, far, near_send, near_recv, far_send, far_recv):
    siblings, peers = all_peers(ring)
    me, row = ring.fsdp, ring.ctx
    near[me] = small[...]
    first = [
        remote(small, near.at[me], near_send.at[i], near_recv.at[i], to)
        for i, to in enumerate(siblings)
    ]
    for copy in first:
        copy.start()
    yield from idle(RING_PIECES)
    for copy in first:
        copy.wait()
    far[row] = sum([near[i] for i in range(len(siblings) + 1)])
    second = [
        remote(far.at[row], far.at[row], far_send.at[i], far_recv.at[i], to)
        for i, to in enumerate(peers)
    ]
    for copy in second:
        copy.start()
    yield from idle(2 * RING_PIECES)
    for copy in second:
        copy.wait()
    total[...] = sum([far[i] for i in range(len(peers) + 1)])


class Attention:
    kinds = ("all",)

    def __init__(self, rows, heads, dim):
        self.rows, self.heads, self.dim = rows, heads, dim
        self.scaling = dim ** (-0.5)
        self.tall = min(256 if rows <= 1024 else 128, rows)

    def block(self, index):
        rows = slice(index * self.tall, (index + 1) * self.tall)
        return rows, (index + 1) * self.tall

    def allowed(self, rows, wide, info, across):
        shape = (self.tall, wide)
        here = lax.broadcasted_iota(jnp.int32, shape, 0) + rows.start
        there = lax.broadcasted_iota(jnp.int32, shape, 1)
        return (there <= here) & (info[rows, 24:25] == across[8:9, :wide])

    def part(self, qkv, which, head, rows):
        start = (which * self.heads + head) * self.dim
        return qkv[rows, start : start + self.dim]

    def scores(self, qkv, info, across, head, rows, wide, allowed):
        queries = self.part(qkv, 0, head, rows)
        keys = self.part(qkv, 1, head, slice(0, wide))
        scores = matmul_rows(queries, keys) * self.scaling
        scores = scores + info[rows, head : head + 1] - across[head : head + 1, :wide]
        return queries, keys, jnp.where(allowed, scores, NEGATIVE)


class Late:
    def __init__(self, arrays):
        self.count = len(arrays)
        self.scratch = [pltpu.VMEM(a.shape, a.dtype) for a in arrays]
        self.scratch += [pltpu.SemaphoreType.DMA((self.count,))]

    def start(self, refs, scratch):
        self.held, self.waiting = list(scratch[: self.count]), {}
        for i, ref in enumerate(refs):
            copy = pltpu.make_async_copy(ref, self.held[i], scratch[self.count].at[i])
            copy.start()
            self.waiting[i] = copy
        return self

    def need(self, *which):
        for i in which:
            if i in self.waiting:
                self.waiting.pop(i).wait()


class Early:
    def __init__(self, shapes):
        self.count = len(shapes)
        self.scratch = [pltpu.VMEM(a.shape, a.dtype) for a in shapes]
        self.scratch += [pltpu.SemaphoreType.DMA((self.count,))]

    def begin(self, refs, scratch):
        self.refs, self.held, self.sem = refs, list(scratch[: self.count]), scratch[self.count]
        self.leaving = []
        return self

    def ready(self, *which):
        for i in which:
            copy = pltpu.make_async_copy(self.held[i], self.refs[i], self.sem.at[i])
            copy.start()
            self.leaving.append(copy)

    def finish(self):
        for copy in self.leaving:
            copy.wait()


def split_refs(refs, sizes):
    groups, at = [], 0
    for size in sizes:
        groups.append(list(refs[at : at + size]))
        at += size
    return groups


EXACT = dict(preferred_element_type=F32, precision=lax.Precision.HIGHEST)


class Forward(Attention):
    def __init__(self, tokens, gain, cotangent, weights, w_out, bias, seg, heads, dim):
        count, shards = lax.axis_size("ctx"), lax.axis_size("fsdp")
        tall, width = tokens.shape
        rows = tall * count
        super().__init__(rows, heads, dim)
        hidden = heads * dim
        self.hidden = hidden
        self.whole = len(weights) > 1
        self.ins = [tokens, gain, bias, seg, cotangent, w_out] + list(weights)
        self.in_specs = [VMEM] * 4 + [ANYWHERE] * 2
        self.in_specs += [ANYWHERE] * 4 + [VMEM] if self.whole else [ANYWHERE]
        shard_rows = width // shards
        joined = (shard_rows, 4 * hidden + 128)
        window = hidden if hidden % 128 == 0 else hidden + 64
        everyone = jax.ShapeDtypeStruct((count, tall, width), BF16)
        self.outs = [
            everyone,
            everyone,
            jax.ShapeDtypeStruct((width, joined[1]), BF16),
            jax.ShapeDtypeStruct((width, width), BF16),
            jax.ShapeDtypeStruct((rows, 3 * hidden), BF16),
            jax.ShapeDtypeStruct((rows, hidden), F32),
            jax.ShapeDtypeStruct((rows, hidden), F32),
            jax.ShapeDtypeStruct((rows, 128), F32),
            jax.ShapeDtypeStruct((16, rows), F32),
            jax.ShapeDtypeStruct((tall, count * hidden), BF16),
        ]
        self.out_specs = [ANYWHERE] * 7 + [VMEM] * 3
        self.early = Early([self.outs[i] for i in (0, 2, 4, 5, 6)])
        ring = [pltpu.SemaphoreType.DMA] + ring_sems(count)
        swapped = pltpu.VMEM((count, tall // 2, 2 * hidden), BF16)
        groups = [
            ring,
            ring,
            shard_gather_sems(1),
            shard_gather_sems(1),
            [swapped, swapped] + swap_sems(count),
            self.early.scratch,
            [pltpu.VMEM((4, shard_rows, window), BF16), pltpu.VMEM(joined, BF16)] + sems(4),
            [pltpu.VMEM((8, 128), F32)],
        ]
        self.sizes = [len(group) for group in groups]
        self.scratch = sum(groups, [])

    def run(self, ring, ins, outs, scratch):
        rows_sems, cotangent_sems, mixed_sems, out_sems, swapping, held, joining, own_bias = (
            split_refs(scratch, self.sizes)
        )
        tokens, gain, bias, seg, cotangent, w_out, *weights = ins
        (bias_own,) = own_bias
        _, grad_out, _, full_out, _, _, _, info, across, gated = outs
        early = self.early.begin([outs[i] for i in (0, 2, 4, 5, 6)], held)
        normed, mixed_in, qkv, attended, gate = early.held
        sent, received = swapping[:2]
        count, tall, _ = normed.shape

        def filled_from(source):
            def fill(shard, local_sem):
                return [pltpu.make_async_copy(source, shard, local_sem.at[0])], source

            return fill

        def later(turns, walk):
            yield from idle(turns)
            yield from walk

        def main():
            fetched = self.fetch(ring, weights, *joining) if self.whole else []
            value = tokens[...].astype(F32)
            rstat = lax.rsqrt(jnp.mean(value * value, axis=1, keepdims=True) + EPSILON)
            normed[ring.ctx] = (value * rstat * gain[...].astype(F32)).astype(BF16)
            gather = ring_gather(ring, None, normed, *rows_sems, True)
            next(gather)
            mixed_shard = self.join(ring, weights, bias, bias_own, fetched, *joining[:2])
            yield from together(
                gather,
                shard_gather(ring, filled_from(mixed_shard), mixed_in, *mixed_sems),
            )
            early.ready(0, 1)
            self.project(normed, mixed_in, bias_own, qkv, gate, info)
            early.ready(2, 4)
            self.decay(info, across, seg)
            yield
            yield from self.attend(qkv, info, across, attended)
            early.ready(3)
            for i in range(count):
                rows = slice(i * tall, (i + 1) * tall)
                sent[i] = fold((attended[rows] * gate[rows]).astype(BF16))
            yield from swap(ring, *swapping)
            gated[...] = jnp.concatenate([unfold(received[i]) for i in range(count)], axis=1)

        turns = count // 2 * RING_PIECES
        yield from together(
            main(),
            later(turns - 1, ring_gather(ring, cotangent, grad_out, *cotangent_sems, False)),
            later(turns // 2, shard_gather(ring, filled_from(w_out), full_out, *out_sems)),
        )
        early.finish()

    def fetch(self, ring, weights, windows, joined, sem):
        start = pl.multiple_of(ring.ctx * self.hidden // 128 * 128, 128)
        copies = [
            pltpu.make_async_copy(
                weights[i].at[:, pl.ds(start, windows.shape[2])], windows.at[i], sem.at[i]
            )
            for i in range(4)
        ]
        for copy in copies:
            copy.start()
        return copies

    def join(self, ring, weights, bias, bias_own, fetched, windows, joined):
        heads, hidden = self.heads, self.hidden
        shape = (bias.shape[1], 128)
        head = lax.broadcasted_iota(jnp.int32, shape, 0)
        spot = lax.broadcasted_iota(jnp.int32, shape, 1)
        chosen = ((head == ring.ctx * heads + spot) & (spot < heads)).astype(F32)
        bias_own[...] = jnp.dot(
            jnp.broadcast_to(bias[...], (8, bias.shape[1])), chosen, **EXACT
        )
        if not self.whole:
            return weights[0]
        for copy in fetched:
            copy.wait()
        parts = []
        for i in range(4):
            part = windows[i, :, :hidden]
            if hidden % 128 != 0:
                shifted = windows[i, :, 64 : 64 + hidden]
                part = jnp.where(ring.ctx * hidden % 128 == 0, part, shifted)
            parts.append(part)
        parts.append(matmul(weights[4][...], chosen.astype(BF16)).astype(BF16))
        joined[...] = jnp.concatenate(parts, axis=1)
        return joined

    def project(self, normed, mixed_in, bias, qkv, gate, info):
        count, tall, width = normed.shape
        pair = 2 if count % 2 == 0 else 1
        hidden = self.hidden

        @pl.loop(0, count // pair)
        def _(index):
            block = normed[pl.ds(index * pair, pair)].reshape(pair * tall, width)
            rows = pl.ds(pl.multiple_of(index * pair * tall, pair * tall), pair * tall)
            mixed = matmul(block, mixed_in[...])
            qkv[rows] = mixed[:, : 3 * hidden].astype(BF16)
            gate[rows] = jax.nn.sigmoid(mixed[:, 3 * hidden : 4 * hidden])
            info[rows] = mixed[:, 4 * hidden : 4 * hidden + 128]
            info[rows, 8:16] = info[rows, 0:8] + bias[0:1, 0:8]

    def decay(self, info, across, seg):
        tall = 128
        here = lax.broadcasted_iota(jnp.int32, (tall, tall), 0)
        there = lax.broadcasted_iota(jnp.int32, (tall, tall), 1)
        wedge = (there <= here).astype(F32)
        before = jnp.zeros((1, 8), F32)
        pad = jnp.zeros((tall, 120), F32)
        across[8:9] = seg[...].astype(F32)
        for index in range(self.rows // tall):
            rows = slice(index * tall, (index + 1) * tall)
            info[rows, 24:25] = jnp.broadcast_to(across[8:9, rows], (tall, tall)).T[:, 0:1]
            logs = jax.nn.log_sigmoid(info[rows, 8:16])
            sums = jnp.dot(wedge, jnp.concatenate([logs, pad], axis=1), **EXACT)[:, :8] + before
            before = sums[tall - 1 :]
            info[rows, 0:8] = sums
            across[0:8, rows] = jnp.concatenate([sums, pad], axis=1).T[:8]

    def attend(self, qkv, info, across, attended):
        for index in range(self.rows // self.tall):
            rows, wide = self.block(index)
            allowed = self.allowed(rows, wide, info, across)
            mixed = []
            for head in range(self.heads):
                _, _, scores = self.scores(qkv, info, across, head, rows, wide, allowed)
                row_max = jnp.max(scores, axis=1, keepdims=True)
                raised = jnp.exp(scores - row_max)
                row_total = jnp.sum(raised, axis=1, keepdims=True)
                probabilities = (raised * (1.0 / row_total)).astype(BF16)
                mixed.append(matmul(probabilities, self.part(qkv, 2, head, slice(0, wide))))
                info[rows, 16 + head : 17 + head] = row_max + jnp.log(row_total)
                if head < self.heads - 1:
                    yield
            attended[rows] = jnp.concatenate(mixed, axis=1)
            yield


def slow(walk, turns):
    for _ in walk:
        yield from idle(turns)


class Backward(Attention):
    def __init__(self, own_heads, named):
        rows = named["qkv"].shape[0]
        super().__init__(rows, own_heads, named["qkv"].shape[1] // 3 // own_heads)
        self.names = list(named)
        hbm = ("gated", "grad_ffn_in")
        self.loaded = ("full_out", "qkv", "attended", "gate_value", "mixed_in", "normed")
        self.late = Late([named[name] for name in self.loaded])
        self.ins = [named[name] for name in self.names]
        self.in_specs = [
            ANYWHERE if name in hbm + self.loaded else VMEM for name in self.names
        ]
        count, shards = lax.axis_size("ctx"), lax.axis_size("fsdp")
        tall, width = named["gated"].shape
        hidden = own_heads * self.dim
        self.main = 4 * hidden
        both = -(-(5 * hidden + own_heads) // 128) * 128
        ffn = [named["grad_ffn_in"]]
        shard_rows = width // shards
        swapped = pltpu.VMEM((count, tall // 2, 2 * hidden), BF16)
        block = pltpu.VMEM((shards * tall, width), BF16)
        heads = pltpu.VMEM((self.rows, hidden), BF16)
        self.outs = (
            [jax.ShapeDtypeStruct((tall, width), F32)]
            + [jax.ShapeDtypeStruct((count,) + grad.shape, BF16) for grad in ffn]
            + [jax.ShapeDtypeStruct((count, shard_rows, both), BF16)]
            + [jax.ShapeDtypeStruct((8, width), F32)]
        )
        self.out_specs = [VMEM] + [ANYWHERE] * 2 + [VMEM]
        ring = [pltpu.SemaphoreType.DMA] + ring_sems(count)
        groups = [
            [pltpu.VMEM((3, own_heads, self.rows, self.dim), F32)],
            [pltpu.VMEM((self.rows, 128), F32), pltpu.VMEM((8, self.rows), F32)],
            [pltpu.VMEM((self.rows, self.main + 128), BF16)],
            [
                pltpu.VMEM((count, shard_rows, hidden), BF16),
                pltpu.VMEM((2, count // 2, shard_rows, hidden), BF16),
                pltpu.VMEM((shard_rows, hidden), F32),
            ]
            + ring_sems(count),
            [
                pltpu.VMEM((count, tall, width), BF16),
                pltpu.VMEM((2, count // 2, tall, width), BF16),
                pltpu.VMEM((tall, width), F32),
            ]
            + ring_sems(count),
            [
                pltpu.VMEM((shard_rows, both), BF16),
                pltpu.VMEM((width, self.main + 128), BF16),
                pltpu.VMEM((shard_rows, self.main + 128), BF16),
            ]
            + shard_sum_scratch(shard_rows, self.main + 128),
            ring,
            ring,
            ring,
            [pltpu.VMEM((8, width), F32)] + small_sum_scratch((8, width)),
            [pltpu.VMEM((tall, width), F32), pltpu.VMEM((tall, count * hidden), BF16)],
            [swapped, swapped] + swap_sems(count),
            [heads, heads],
            [block] + shard_gather_sems(1),
            [block] + shard_gather_sems(1),
            [pltpu.VMEM((tall, width), BF16), pltpu.VMEM((shards * tall, shard_rows), BF16)],
            self.late.scratch,
        ]
        self.sizes = [len(group) for group in groups]
        self.scratch = sum(groups, [])

    def run(self, ring, ins, outs, scratch):
        groups = split_refs(scratch, self.sizes)
        named = dict(zip(self.names, ins))
        late = self.late.start([named[name] for name in self.loaded], groups[16])
        named.update(zip(self.loaded, late.held))
        out_part, out_held, out_sum, *out_sems = groups[3]
        rows_part, rows_held, rows_sum, *rows_sems = groups[4]
        grad_mixed = groups[2][0]
        grads_all, grads_part, grads_sum, *grads_rest = groups[5]
        small, *small_rest = groups[9]
        named["grad_middle"], grad_gated = groups[10]
        named["grad_attn"], named["grad_gatelog"] = groups[12]
        gated_block, *gated_sems = groups[13]
        branch_block, *branch_sems = groups[14]
        branch, gated_columns = groups[15]
        count, tall, width = rows_part.shape

        def filled_from(source):
            def fill(shard, local_sem):
                return [pltpu.make_async_copy(source, shard, local_sem.at[0])], source

            return fill

        gather_gated = shard_gather(
            ring, filled_from(named["gated"]), gated_block, *gated_sems, turns=1
        )

        def main():
            next(gather_gated)
            next(gather_gated)
            late.need(0)
            self.branch_back(named, grad_gated, groups[11][0], branch, small)
            yield from together(
                swap(ring, *groups[11]),
                shard_gather(ring, filled_from(branch), branch_block, *branch_sems, turns=2),
                gather_gated,
            )
            late.need(1, 2, 3)
            self.gate_back(named, groups[11][1])
            self.out_grads(ring, gated_block, branch_block, gated_columns, out_part)
            yield from together(
                self.attention(named, *groups[0], *groups[1]),
                ring_sum(ring, out_part, out_held, out_sum, *out_sems, True),
            )
            self.join(ring, named, *groups[0], *groups[1], grad_mixed, small)
            block = 256 if width % 256 == 0 else width
            late.need(4)

            @pl.loop(0, width // block)
            def _(index):
                columns = pl.ds(pl.multiple_of(index * block, block), block)
                part = matmul_rows(grad_mixed[...], named["mixed_in"][columns])
                rows_part[:, :, columns] = part.astype(BF16).reshape(count, tall, block)

            yield from together(
                ring_sum(ring, rows_part, rows_held, rows_sum, *rows_sems, True),
                weights(),
            )

        def weights():
            yield from idle(RING_PIECES)
            late.need(5)
            self.weight_grads(named, grad_mixed, grads_part)
            yield from shard_sum(ring, grads_part, grads_sum, *grads_rest)
            tail = grads_all.shape[1] - self.main - out_sum.shape[1]
            grads_all[:, : self.main] = grads_sum[:, : self.main]
            grads_all[:, self.main :] = jnp.concatenate(
                [out_sum[...].astype(BF16), grads_sum[:, self.main : self.main + tail]], axis=1
            )

        yield from together(
            slow(ring_gather(ring, named["grad_ffn_in"], outs[1], *groups[6], True), 2),
            main(),
        )
        self.norm_back(named, rows_sum, outs[0], small)
        yield from together(
            ring_gather(ring, grads_all, outs[2], *groups[8], True),
            small_sum(ring, small, outs[3], *small_rest),
        )

    def branch_back(self, named, grad_gated, sent, branch, small):
        grad, normed = named["grad_normed_two"][...], named["normed_two"][...]
        small[...] = jnp.zeros_like(small)
        small[1:2] = jnp.sum(grad * normed, axis=0, keepdims=True)
        grad_normed = grad * named["gain_two"][...].astype(F32)
        inner = jnp.mean(grad_normed * normed, axis=1, keepdims=True)
        named["grad_middle"][...] = named["cotangent"][...].astype(F32) + named["rstat_two"][...] * (
            grad_normed - normed * inner
        )
        branch[...] = named["grad_middle"][...].astype(BF16)
        count, hidden = sent.shape[0], sent.shape[2] // 2
        width = grad.shape[1]
        block = 256 if width % 256 == 0 else width
        if grad_gated.shape[1] > width:
            grad_gated[...] = jnp.zeros_like(grad_gated)

        @pl.loop(0, width // block)
        def _(index):
            columns = pl.ds(pl.multiple_of(index * block, block), block)
            part = matmul_rows(branch[...], named["full_out"][columns])
            grad_gated[:, columns] = part.astype(BF16)

        for i in range(count):
            sent[i] = fold(grad_gated[:, i * hidden : (i + 1) * hidden])

    def gate_back(self, named, received):
        count, tall = received.shape[0], 2 * received.shape[1]
        for i in range(count):
            rows = slice(i * tall, (i + 1) * tall)
            grad = unfold(received[i]).astype(F32)
            gate = named["gate_value"][rows]
            named["grad_attn"][rows] = (grad * gate).astype(BF16)
            named["grad_gatelog"][rows] = (
                grad * named["attended"][rows] * (gate * (1.0 - gate))
            ).astype(BF16)

    def attention(self, named, grads, sums_rows, sums_columns):
        qkv, info, across, grad_attn = [
            named[name] for name in ("qkv", "info", "across", "grad_attn")
        ]
        grad_q, grad_k, grad_v = [grads.at[i] for i in range(3)]
        blocks = self.rows // self.tall
        sums_columns[...] = jnp.zeros_like(sums_columns)
        pad = jnp.zeros((self.tall, 128 - self.heads), F32)
        for index in reversed(range(blocks)):
            rows, wide = self.block(index)
            allowed = self.allowed(rows, wide, info, across)
            own = slice(0, wide)
            row_sums = []
            for head in range(self.heads):
                queries, keys, scores = self.scores(
                    qkv, info, across, head, rows, wide, allowed
                )
                probabilities = jnp.exp(scores - info[rows, 16 + head : 17 + head])
                grad_part = grad_attn[rows, head * self.dim : (head + 1) * self.dim]
                grad_probs = matmul_rows(grad_part, self.part(qkv, 2, head, own))
                row_inner = jnp.sum(probabilities * grad_probs, axis=1, keepdims=True)
                grad_scores = (probabilities * (grad_probs - row_inner)).astype(BF16)
                grad_q[head, rows] = matmul(grad_scores, keys) * self.scaling
                from_k = weight_grad(grad_scores, queries) * self.scaling
                from_v = weight_grad(probabilities.astype(BF16), grad_part)
                wide_sums = grad_scores.astype(F32)
                row_sums.append(jnp.sum(wide_sums, axis=1, keepdims=True))
                column_sums = jnp.sum(wide_sums, axis=0, keepdims=True)
                if index == blocks - 1:
                    grad_k[head], grad_v[head] = from_k, from_v
                    sums_columns[head : head + 1] = column_sums
                else:
                    grad_k[head, own] += from_k
                    grad_v[head, own] += from_v
                    sums_columns[head : head + 1, own] += column_sums
                if head < self.heads - 1:
                    yield
            sums_rows[rows] = jnp.concatenate(row_sums + [pad], axis=1)
            yield

    def join(self, ring, named, grads, sums_rows, sums_columns, grad_mixed, small):
        for index in range(self.rows // self.tall):
            rows, _ = self.block(index)
            grad_mixed[rows, : self.main] = jnp.concatenate(
                [grads[i, head, rows].astype(BF16) for i in range(3) for head in range(self.heads)]
                + [named["grad_gatelog"][rows]],
                axis=1,
            )
        tall = 128
        here = lax.broadcasted_iota(jnp.int32, (tall, tall), 0)
        there = lax.broadcasted_iota(jnp.int32, (tall, tall), 1)
        wedge = (here <= there).astype(F32)
        later, bias = jnp.zeros((1, 8), F32), jnp.zeros((1, 8), F32)
        pad = jnp.zeros((tall, 120), BF16)
        for index in reversed(range(self.rows // tall)):
            rows = slice(index * tall, (index + 1) * tall)
            inside = jnp.dot(wedge, sums_rows[rows], **EXACT)[:, :8] - lax.dot_general(
                wedge, sums_columns[:, rows], (((1,), (1,)), ((), ())), **EXACT
            )
            logits = named["info"][rows, 8:16]
            grad_logits = ((inside + later) * jax.nn.sigmoid(-logits)).astype(BF16)
            later = later + inside[:1]
            bias = bias + jnp.sum(grad_logits.astype(F32), axis=0, keepdims=True)
            grad_mixed[rows, self.main :] = jnp.concatenate([grad_logits, pad], axis=1)
        spot = lax.broadcasted_iota(jnp.int32, (1, small.shape[1]), 1)
        small[2:3] = sum(
            jnp.where(spot == ring.ctx * self.heads + head, bias[:, head : head + 1], 0.0)
            for head in range(self.heads)
        )

    def out_grads(self, ring, gated_block, branch_block, gated_columns, parts):
        count, rows, hidden = parts.shape
        for i in range(lax.axis_size("fsdp")):

            @pl.when(ring.fsdp == i)
            def _():
                gated_columns[...] = gated_block[:, i * rows : (i + 1) * rows]

        for i in range(count):
            stop = min((i + 1) * hidden, branch_block.shape[1])
            if stop > i * hidden:
                part = weight_grad(gated_columns[...], branch_block[:, i * hidden : stop])
                parts[i] = part.astype(BF16)
            else:
                parts[i] = jnp.zeros((rows, hidden), BF16)

    def weight_grads(self, named, grad_mixed, parts):
        count, tall, width = named["normed"].shape
        tile = 128

        @pl.loop(0, width // tile)
        def _(index):
            columns = pl.ds(pl.multiple_of(index * tile, tile), tile)
            normed = named["normed"][:, :, columns].reshape(count * tall, tile)
            parts[columns] = weight_grad(normed, grad_mixed[...]).astype(BF16)

    def norm_back(self, named, rows_sum, grad_tokens, small):
        grad, value = rows_sum[...], named["tokens"][...].astype(F32)
        rstat = lax.rsqrt(jnp.mean(value * value, axis=1, keepdims=True) + EPSILON)
        normed = value * rstat
        small[0:1] = jnp.sum(grad * normed, axis=0, keepdims=True)
        grad_normed = grad * named["gain_one"][...].astype(F32)
        inner = jnp.mean(grad_normed * normed, axis=1, keepdims=True)
        grad_tokens[...] = named["grad_middle"][...] + rstat * (
            grad_normed - normed * inner
        )


def exchange(ident, name, *tasks):
    count = lax.axis_size("ctx")

    def take(refs, sizes):
        groups, at = [], 0
        for size in sizes:
            groups.append(refs[at : at + size])
            at += size
        return groups

    ins = [len(task.ins) for task in tasks]
    outs = [len(task.outs) for task in tasks]
    scratch = [len(task.scratch) for task in tasks]

    def kernel(*refs):
        ring = Ring(count)
        kinds = sum([task.kinds for task in tasks], ())
        peers = []
        if "all" in kinds:
            peers = sum(all_peers(ring), [])
        else:
            if "ring" in kinds:
                peers += [ring.device(1), ring.device(-1)]
            if "shard" in kinds:
                pair, others = shard_pair(ring, lax.axis_size("fsdp"))
                peers += [(ring.ctx, to) for to in [pair] + others]
        greet(peers)
        groups = [
            take(refs[: sum(ins)], ins),
            take(refs[sum(ins) : sum(ins) + sum(outs)], outs),
            take(refs[sum(ins) + sum(outs) :], scratch),
        ]
        for _ in together(*[task.run(ring, *parts) for task, *parts in zip(tasks, *groups)]):
            pass

    results = pl.pallas_call(
        kernel,
        out_shape=sum([task.outs for task in tasks], []),
        in_specs=sum([task.in_specs for task in tasks], []),
        out_specs=sum([task.out_specs for task in tasks], []),
        scratch_shapes=sum([task.scratch for task in tasks], []),
        compiler_params=pltpu.CompilerParams(
            collective_id=ident, has_side_effects=True, vmem_limit_bytes=62 * 2**20
        ),
        cost_estimate=pl.CostEstimate(flops=0, bytes_accessed=100_000_000, transcendentals=0),
        name=name,
    )(*sum([task.ins for task in tasks], []))
    return take(list(results), outs)


def flat(blocks):
    return blocks.reshape(-1, blocks.shape[-1])


def permute_rows(value, beside):
    count, me = lax.axis_size("ctx"), lax.axis_index("ctx")
    order = [ring_index(place, count) for place in range(count)]
    rows, half = value.shape[0], value.shape[0] // 2
    ways = [[(order[i], order[(i + sign) % count]) for i in range(count)] for sign in (1, -1)]

    parts, offsets = [value], [0]
    blocks, results, beside = [value, value], [], list(beside)
    for hops in range(1, count // 2 + 1):
        work = None
        if hops > 1 and beside:
            work, operand = beside.pop(0)
            blocks[0], blocks[1], operand = lax.optimization_barrier((*blocks, operand))
        last = hops == count // 2
        sent = [blocks[0][:half], blocks[1][half:]] if last else blocks
        blocks = [lax.ppermute(block, "ctx", way) for block, way in zip(sent, ways)]
        if work is not None:
            result = work(operand)
            blocks[0], blocks[1], result = lax.optimization_barrier((*blocks, result))
            results.append(result)
        parts += blocks
        offsets += [-hops, hops]
    place = (ring_place(me, count) + jnp.asarray(offsets[:-1], jnp.int32) + count) % count
    return place_rows(parts, ring_index(place, count)), results


def place_rows(parts, sources):
    rows, width = parts[0].shape
    count = len(parts) - 1
    half = rows // 2

    def kernel(source_ref, *refs):
        ins, out = refs[:-1], refs[-1]
        for j in range(count):
            at = source_ref[j] * rows
            if j < count - 1:
                out[pl.ds(pl.multiple_of(at, rows), rows)] = ins[j][...].astype(F32)
            else:
                for k in range(2):
                    start = pl.multiple_of(at + k * half, half)
                    out[pl.ds(start, half)] = ins[j + k][...].astype(F32)

    return pl.pallas_call(
        kernel,
        out_shape=jax.ShapeDtypeStruct((rows * count, width), F32),
        in_specs=[pl.BlockSpec(memory_space=pltpu.SMEM)] + [VMEM] * len(parts),
        out_specs=VMEM,
        compiler_params=pltpu.CompilerParams(vmem_limit_bytes=40 * 2**20),
        cost_estimate=pl.CostEstimate(
            flops=0, bytes_accessed=rows * width * count * 6, transcendentals=0
        ),
        name="place_rows",
    )(sources, *parts)


def ffn_columns(blocks, n_fsdp):
    count, rows, both = blocks.shape
    width, piece = both // 2, both // 2 // n_fsdp
    steps = 4
    tall = rows // steps

    def kernel(block_ref, *outs):
        for j in range(count):
            for half in range(2):
                for group in range(n_fsdp):
                    start, to = half * width + group * piece, (group * count + j) * piece
                    outs[half][:, to : to + piece] = block_ref[j, :, start : start + piece].astype(F32)

    wide = jax.ShapeDtypeStruct((rows, width * count), F32)
    spec = pl.BlockSpec((tall, width * count), lambda i: (i, 0))
    return pl.pallas_call(
        kernel,
        out_shape=(wide, wide),
        grid=(steps,),
        in_specs=[pl.BlockSpec((count, tall, both), lambda i: (0, i, 0))],
        out_specs=(spec, spec),
        compiler_params=pltpu.CompilerParams(vmem_limit_bytes=40 * 2**20),
        cost_estimate=pl.CostEstimate(
            flops=0, bytes_accessed=rows * both * count * 6, transcendentals=0
        ),
        name="ffn_columns",
    )(blocks)


def head_columns(blocks, sizes, widths):
    count, rows, total = blocks.shape
    steps = 4
    tall = rows // steps
    starts = [sum(sizes[:i]) for i in range(len(sizes))]

    def kernel(block_ref, *outs):
        for start, size, out in zip(starts, sizes, outs):
            for i in range(0, count, 2):
                pair = jnp.concatenate(
                    [block_ref[i + k][:, start : start + size].astype(F32) for k in range(2)], axis=1
                )
                at = i * size
                keep = min(2 * size, out.shape[1] - at)
                if keep > 0:
                    out[:, at : at + keep] = pair[:, :keep]

    return pl.pallas_call(
        kernel,
        out_shape=tuple(jax.ShapeDtypeStruct((rows, w), F32) for w in widths),
        grid=(steps,),
        in_specs=[pl.BlockSpec((count, tall, total), lambda i: (0, i, 0))],
        out_specs=tuple(pl.BlockSpec((tall, w), lambda i: (i, 0)) for w in widths),
        compiler_params=pltpu.CompilerParams(vmem_limit_bytes=40 * 2**20),
        cost_estimate=pl.CostEstimate(
            flops=0, bytes_accessed=count * rows * total * 6, transcendentals=0
        ),
        name="head_columns",
    )(blocks)


def shards(
    tokens,
    segments,
    gain_attn,
    w_query,
    w_key,
    w_value,
    w_forget,
    forget_bias,
    w_outgate,
    w_out,
    gain_ffn,
    w_gate,
    w_up,
    w_down,
    cotangent,
):
    n_ctx, me = lax.axis_size("ctx"), lax.axis_index("ctx")
    n_fsdp = lax.axis_size("fsdp")
    tok_rows, width = tokens.shape[1:]
    seq_rows = tok_rows * n_ctx
    n_heads = forget_bias.shape[0]
    head_dim = width // n_heads
    own_heads = -(-n_heads // n_ctx)
    own_width = own_heads * head_dim
    padded = own_width * n_ctx
    ffn_rows = w_down.shape[0]
    ffn_piece = ffn_rows // n_ctx
    ffn_width = ffn_piece * n_fsdp
    shard_rows = w_query.shape[0]

    def widen(value, size):
        return jnp.pad(value, ((0, 0), (0, size - value.shape[1])))

    def own_columns(weight, size):
        return lax.dynamic_slice_in_dim(widen(weight, size * n_ctx), me * size, size, 1)

    def own_ffn(weight):
        return [
            lax.dynamic_slice_in_dim(weight, (group * n_ctx + me) * ffn_piece, ffn_piece, 1)
            for group in range(n_fsdp)
        ]

    weights = [w_query, w_key, w_value, w_outgate, w_forget]
    if padded != width or own_width % 64 != 0:
        columns = [own_columns(w, own_width) for w in weights[:4]]
        columns.append(widen(own_columns(w_forget, own_heads), 128))
        weights = [jnp.concatenate(columns, axis=1)]
    gain_one, gain_two = gain_attn, gain_ffn
    (
        (
            normed,
            grad_out_low,
            mixed_in,
            full_out,
            qkv,
            attended,
            gate_value,
            info,
            across,
            gated,
        ),
    ) = exchange(
        0,
        "forward",
        Forward(
            tokens[0],
            gain_one,
            cotangent[0],
            weights,
            w_out,
            forget_bias[None],
            segments,
            own_heads,
            head_dim,
        ),
    )
    w_in = [w_gate, w_up]
    if ffn_piece % 128 != 0:
        w_in = [jnp.concatenate(own_ffn(w_gate) + own_ffn(w_up), axis=1)]
    ((output, grad_normed_two, normed_two, rstat_two, grad_ffn_in, grad_ffn_out),) = exchange(
        1,
        "ffn",
        Ffn(tokens[0], gated, full_out, gain_two, grad_out_low, w_in, w_down, ffn_piece),
    )
    ((grad_inputs, spread_ffn_in, spread_attn, small),) = exchange(
        2,
        "backward",
        Backward(
            own_heads,
            {
                "qkv": qkv,
                "info": info,
                "across": across,
                "attended": attended,
                "gate_value": gate_value,
                "grad_normed_two": grad_normed_two,
                "normed_two": normed_two,
                "rstat_two": rstat_two,
                "gain_two": gain_two,
                "cotangent": cotangent[0],
                "full_out": full_out,
                "gated": gated[:, :width],
                "grad_ffn_in": grad_ffn_in,
                "normed": normed,
                "mixed_in": mixed_in,
                "tokens": tokens[0],
                "gain_one": gain_one,
            },
        ),
    )
    sizes = [own_width] * 5 + [own_heads]

    def place_ffn(blocks):
        if ffn_piece % 128 == 0:
            return ffn_columns(blocks, n_fsdp)
        whole = blocks.reshape(n_ctx, shard_rows, 2, n_fsdp, ffn_piece)
        whole = jnp.transpose(whole, (2, 1, 3, 0, 4)).reshape(2, shard_rows, -1).astype(F32)
        return whole[0], whole[1]

    def place_heads(blocks):
        return head_columns(blocks, sizes, [width] * 5 + [n_heads])

    grad_down, ((grad_gate, grad_up), grad_weights) = permute_rows(
        grad_ffn_out, [(place_ffn, spread_ffn_in), (place_heads, spread_attn)]
    )
    return (
        output[None],
        grad_inputs[None],
        small[0],
        grad_weights[0],
        grad_weights[1],
        grad_weights[2],
        grad_weights[5],
        small[2, :n_heads],
        grad_weights[3],
        grad_weights[4],
        small[1],
        grad_gate,
        grad_up,
        grad_down,
    )


def solution(mesh):
    rows, blocks = P("fsdp", None), P("fsdp", "ctx", None)
    return jax.shard_map(
        shards,
        mesh=mesh,
        in_specs=(blocks, rows, P())
        + (rows,) * 4
        + (P(), rows, rows, P(), rows, rows, rows, blocks),
        out_specs=(blocks, blocks, P())
        + (rows,) * 4
        + (P(), rows, rows, P(), rows, rows, rows),
        check_vma=False,
    )
```
